32 devices in a mesh: dp: 4 (over y, x), fsdp: 8 (over z, core).
Axes of the slice: x: 2, y: 2, z: 4, core: 2. Of those that a mesh axis runs over, the one named last changes fastest.
Arguments:
- tokens: bfloat16 [32768, 1024], P(('dp', 'fsdp')), may hold values from -6 to 6
- segment_ids: int32 [32, 1024], P(('dp', 'fsdp')), may hold values from 0 to 19, never falling along the last dimension, each value on 1 to 512 neighbouring positions
- expert_ids: int32 [32768, 1], P(('dp', 'fsdp')), may hold values from 0 to 1; in each aligned block of 1024 rows (0 to 1023, 1024 to 2047, ...) at most 640 rows name the same one
- ln1_gain: bfloat16 [1024], P(('dp', 'fsdp')), may hold values from 0.5 to 1.5
- ln1_bias: bfloat16 [1024], P(('dp', 'fsdp')), may hold values from -0.59765625 to 0.59765625
- qkv_weight: bfloat16 [1024, 3072], P(('dp', 'fsdp')), may hold values from -0.1875 to 0.1875
- query_bias: bfloat16 [1024], P(('dp', 'fsdp')), may hold values from -0.59765625 to 0.59765625
- value_bias: bfloat16 [1024], P(('dp', 'fsdp')), may hold values from -0.59765625 to 0.59765625
- out_weight: bfloat16 [1024, 1024], P(('dp', 'fsdp')), may hold values from -0.375 to 0.375
- out_bias: bfloat16 [1024], P(('dp', 'fsdp')), may hold values from -0.59765625 to 0.59765625
- ln2_gain: bfloat16 [1024], P(('dp', 'fsdp')), may hold values from 0.5 to 1.5
- ln2_bias: bfloat16 [1024], P(('dp', 'fsdp')), may hold values from -0.59765625 to 0.59765625
- up_weight: bfloat16 [1024, 2, 4096], P(('dp', 'fsdp')), may hold values from -0.1875 to 0.1875
- up_bias: bfloat16 [2, 4096], P(None, ('dp', 'fsdp')), may hold values from -0.59765625 to 0.59765625
- down_weight: bfloat16 [4096, 2, 1024], P(('dp', 'fsdp')), may hold values from -0.125 to 0.125
- down_bias: bfloat16 [2, 1024], P(None, ('dp', 'fsdp')), may hold values from -0.59765625 to 0.59765625
- cotangent: bfloat16 [32768, 1024], P(('dp', 'fsdp')), may hold values from -6 to 6
Outputs:
- block_out: bfloat16 [32768, 1024], P(('dp', 'fsdp'))
- input_grad: float32 [32768, 1024], P(('dp', 'fsdp'))
- ln1_gain_grad: float32 [1024], P(('dp', 'fsdp'))
- ln1_bias_grad: float32 [1024], P(('dp', 'fsdp'))
- qkv_weight_grad: float32 [1024, 3072], P(('dp', 'fsdp'))
- query_bias_grad: float32 [1024], P(('dp', 'fsdp'))
- value_bias_grad: float32 [1024], P(('dp', 'fsdp'))
- out_weight_grad: float32 [1024, 1024], P(('dp', 'fsdp'))
- out_bias_grad: float32 [1024], P(('dp', 'fsdp'))
- ln2_gain_grad: float32 [1024], P(('dp', 'fsdp'))
- ln2_bias_grad: float32 [1024], P(('dp', 'fsdp'))
- up_weight_grad: float32 [1024, 2, 4096], P(('dp', 'fsdp'))
- up_bias_grad: float32 [2, 4096], P(None, ('dp', 'fsdp'))
- down_weight_grad: float32 [4096, 2, 1024], P(('dp', 'fsdp'))
- down_bias_grad: float32 [2, 1024], P(None, ('dp', 'fsdp'))
The draws below stay inside these ranges and needn't reach their ends.
Inputs may be any that keep to these rules, and one draw needn't show every extreme that they name: `segment_ids`: each device's 1024 tokens are one packed sequence; its segment numbers never fall. `expert_ids`: at most 640 of the tokens of one device name one expert, and some device's tokens name one expert exactly that often.
All inputs are finite; a program needn't handle non-finite values.
Results may differ from the reference program's by a relative error of at most 0.012.
Values may be sent and summed in bfloat16 or wider, within the bound.
No kernel may reach another device: no remote copies, remote signals or barrier semaphores. Data moves between devices by JAX's collectives and lax.ppermute only.
A program may use at most 512 MiB of HBM per device.

```python
import math
from functools import partial
import jax
import jax.numpy as jnp
import numpy as np
from jax import lax

D = 1024
HEADS = 16
HEAD_DIM = 64
FF = 4096
EXPERTS = 2
TOK_DEV = 1024
CAPACITY = 640
TOKENS = 32768
N_DP = 4
N_FSDP = 8


def block_scale(rng, extent, split, smallest, top_value):
    factor_of = 1.0
    for axis_at, parts in split:
        draws = jax.random.uniform(jax.random.fold_in(jax.random.fold_in(rng, 6), axis_at), (parts,), jnp.float32, smallest / len(split), top_value / len(split))
        factor_of = factor_of * jnp.repeat(jnp.exp(draws), extent[axis_at] // parts).reshape((-1,) + (1,) * (len(extent) - 1 - axis_at))
    return factor_of


def length_profile(amount, total, limit, lean):
    portions = [(1 << 20) // math.isqrt(standing ** lean) + 1 for standing in range(2, amount + 1)]
    surplus, given = total - limit - (amount - 1), [1] * (amount - 1)
    while surplus > 0:
        free = [i for i in range(amount - 1) if given[i] < limit]
        pool, remaining = sum([portions[i] for i in free]), surplus
        for i in free:
            more = min(limit - given[i], max(1, remaining * portions[i] // pool), surplus)
            given[i] = given[i] + more
            surplus = surplus - more
    return np.array([limit] + given)


def uneven(key, count, total, reach, lean):
    if count == 2:
        one = jax.random.randint(key, (), max(1, total - reach), min(reach, total - 1) + 1)
        return jnp.stack([one, total - one])
    sizes = jnp.asarray(length_profile(count, total, reach, lean), jnp.int32)
    twos = (count - 1) // 2
    giver, receiver = sizes[1:1 + 2 * twos:2], sizes[2:2 + 2 * twos:2]
    slack = jnp.minimum(giver - 1, reach - receiver)
    passed = jax.random.randint(jax.random.fold_in(key, 1), (twos,), 0, 1 << 20) % (slack + 1)
    sizes = sizes.at[1:1 + 2 * twos:2].set(giver - passed).at[2:2 + 2 * twos:2].set(receiver + passed)
    return sizes[jax.random.permutation(jax.random.fold_in(key, 2), count)]


def shared_out(own_key, own, number, rows, amount, top, reach, lean):
    ranking = jax.random.permutation(own_key, amount)
    packed, ordinary = load_shares(amount, rows * top, reach, lean, True), load_shares(amount, rows * top, reach, lean, False)
    places = jnp.arange(amount)

    def named(lengths, rotation):
        used = int((lengths > 0).sum())
        fixed = max(1, used // 4)
        moved = fixed + (places - fixed + rotation * (used - fixed)) % max(1, amount - fixed)
        return jnp.zeros((amount,), jnp.int32).at[ranking[jnp.where(places < fixed, places, moved)]].set(jnp.asarray(lengths, jnp.int32))

    lengths = jnp.where(number % 4 == 0, named(packed, number // 4), named(ordinary, number - number // 4 - 1))
    mixed = jax.random.permutation(jax.random.fold_in(own, 3), amount)
    giver, sink = mixed[0:amount // 2 * 2:2], mixed[1:amount // 2 * 2:2]
    slack = jnp.minimum(lengths[giver] - 1, reach - lengths[sink]) // 2
    slack = jnp.where((giver == ranking[0]) | (sink == ranking[0]) | (lengths[sink] == 0), 0, jnp.maximum(slack, 0))
    moved = jax.random.randint(jax.random.fold_in(own, 4), (amount // 2,), 0, 1 << 20) % (slack + 1)
    lengths = lengths.at[giver].add(-moved).at[sink].add(moved)
    labels = jnp.searchsorted(jnp.cumsum(lengths), jnp.arange(rows * top), side="right").astype(jnp.int32)
    table = labels.reshape(top, rows).T
    table = table[jax.random.permutation(jax.random.fold_in(own, 1), rows)]
    rotation = jax.random.randint(jax.random.fold_in(own, 2), (rows, 1), 0, top)
    return jnp.take_along_axis(table, (jnp.arange(top)[None, :] + rotation) % top, axis=1)


def load_shares(number_of, total, reach, skew, full):
    weights = [(1 << 20) // math.isqrt(grade ** skew) + 1 for grade in range(1, number_of + 1)]
    largest = reach if full else min(reach, max(-(-total // number_of), total * weights[0] // sum(weights)))
    least = 1 if total - largest >= number_of - 1 else 0
    counts, surplus = [largest] + [least] * (number_of - 1), total - largest - least * (number_of - 1)
    while surplus > 0:
        movable = [i for i in range(1, number_of) if counts[i] < largest] or [i for i in range(1, number_of) if counts[i] < reach]
        pool, budget = sum([weights[i] for i in movable]), surplus
        for i in movable:
            more = min(reach - counts[i], max(1, budget * weights[i] // pool), surplus)
            counts[i] = counts[i] + more
            surplus = surplus - more
    return np.array(counts)


def scatter_about(stream_key, dims, scale, bound, split=(), kind=jnp.bfloat16):
    entries = jax.random.normal(stream_key, dims, jnp.float32) * scale
    if len(split) > 0:
        entries = block_scale(stream_key, dims, split, -0.22, 0.18) * entries
    return jnp.clip(entries, min=-bound, max=bound).astype(kind)


def setup_inputs(seed: int = 0) -> dict:
    arg_keys = jax.random.split(jax.random.key(seed), 18)
    tokens = scatter_about(arg_keys[0], (TOKENS, D), 1.0, 6.0, ((0, 32),))
    segment_ids = jax.vmap(lambda own: jnp.searchsorted(jnp.cumsum(uneven(own, TOK_DEV // 64 + 4, TOK_DEV, TOK_DEV // 2, 1)), jnp.arange(TOK_DEV), side="right"))(jax.random.split(arg_keys[1], (N_DP * N_FSDP))).reshape((N_DP * N_FSDP, TOK_DEV)).astype(jnp.int32)
    expert_ids_keys = jax.random.split(jax.random.fold_in(arg_keys[2], 1), TOKENS // TOK_DEV)
    expert_ids_turns = jax.random.permutation(jax.random.fold_in(arg_keys[2], 3), TOKENS // TOK_DEV)
    expert_ids = jax.vmap(lambda own, number: shared_out(jax.random.fold_in(arg_keys[2], 2), own, number, TOK_DEV, EXPERTS, 1, CAPACITY, 0))(expert_ids_keys, expert_ids_turns).reshape((TOKENS, 1))
    ln1_gain = jnp.clip(1.0 + 0.1 * jax.random.normal(arg_keys[3], (D,), jnp.float32), 0.5, 1.5).astype(jnp.bfloat16)
    ln1_bias = scatter_about(arg_keys[4], (D,), 0.1, 0.59765625, ((0, 32),))
    qkv_weight = scatter_about(arg_keys[5], (D, 3 * D), D ** -0.5, 0.1875, ((0, 32),))
    query_bias = scatter_about(arg_keys[6], (D,), 0.1, 0.59765625, ((0, 32),))
    value_bias = scatter_about(arg_keys[7], (D,), 0.1, 0.59765625, ((0, 32),))
    out_weight = scatter_about(arg_keys[8], (D, D), (D // 4) ** -0.5, 0.375, ((0, 32),))
    out_bias = scatter_about(arg_keys[9], (D,), 0.1, 0.59765625, ((0, 32),))
    ln2_gain = jnp.clip(1.0 + 0.1 * jax.random.normal(arg_keys[10], (D,), jnp.float32), 0.5, 1.5).astype(jnp.bfloat16)
    ln2_bias = scatter_about(arg_keys[11], (D,), 0.1, 0.59765625, ((0, 32),))
    up_weight = scatter_about(arg_keys[12], (D, EXPERTS, FF), D ** -0.5, 0.1875, ((0, 32),))
    up_bias = scatter_about(arg_keys[13], (EXPERTS, FF), 0.1, 0.59765625, ((1, 32),))
    down_weight = scatter_about(arg_keys[14], (FF, EXPERTS, D), (FF // 2) ** -0.5, 0.125, ((0, 32),))
    down_bias = scatter_about(arg_keys[15], (EXPERTS, D), 0.1, 0.59765625, ((1, 32),))
    cotangent = scatter_about(arg_keys[16], (TOKENS, D), 1.0, 6.0, ((0, 32),))
    return dict(tokens=tokens, segment_ids=segment_ids, expert_ids=expert_ids, ln1_gain=ln1_gain, ln1_bias=ln1_bias, qkv_weight=qkv_weight, query_bias=query_bias, value_bias=value_bias, out_weight=out_weight, out_bias=out_bias, ln2_gain=ln2_gain, ln2_bias=ln2_bias, up_weight=up_weight, up_bias=up_bias, down_weight=down_weight, down_bias=down_bias, cotangent=cotangent)


@jax.custom_vjp
def low(v):
    return lax.optimization_barrier(v.astype(jnp.bfloat16)).astype(jnp.float32)

@jax.custom_vjp
def low_back(v):
    return v

def low_keep(v):
    return (low(v), None)

def low_pass(kept, grad):
    return (grad,)

def back_keep(v):
    return (v, None)

def back_low(kept, grad):
    return (low(grad),)
low.defvjp(low_keep, low_pass)
low_back.defvjp(back_keep, back_low)
highest = lax.Precision.HIGHEST

def layer_norm(values, gain, shift):
    centre = values - lax.optimization_barrier(jnp.mean(values, -1, keepdims=True))
    spread = lax.optimization_barrier(jnp.mean(centre * centre, -1, keepdims=True))
    return centre * lax.rsqrt(spread + 1e-05) * gain + shift

def head_attention(allowed, items):
    queries, keys_all, values_all = items
    raw = low_back(jnp.dot(queries, keys_all.T, precision=highest)) * HEAD_DIM ** (-0.5)
    scores = jnp.where(allowed, raw, -1e+30)
    probs = low(jax.nn.softmax(scores, axis=-1))
    return jnp.dot(probs, values_all, precision=highest)

def block(weights, pieces):
    gain_one, shift_one, w_qkv, bias_query, bias_value, w_out, bias_out, gain_two, shift_two, w_up, bias_up, w_down, bias_down = weights
    flat, segments, routes = pieces
    length, width = flat.shape
    normed = low(layer_norm(flat, gain_one, shift_one))
    qkv_bias = jnp.concatenate([bias_query, jnp.zeros_like(bias_query), bias_value])
    qkv = jnp.dot(normed, w_qkv, precision=highest) + qkv_bias
    qkv = low(low_back(qkv)).reshape(length, 3, HEADS, HEAD_DIM)
    queries = jnp.transpose(qkv[:, 0], (1, 0, 2))
    keys_all = jnp.transpose(qkv[:, 1], (1, 0, 2))
    values_all = jnp.transpose(qkv[:, 2], (1, 0, 2))
    positions = jnp.arange(length)
    causal = positions[None, :] <= positions[:, None]
    allowed = causal & (segments[:, None] == segments[None, :])
    heads_out = lax.map(jax.checkpoint(partial(head_attention, allowed)), (queries, keys_all, values_all))
    attended = jnp.transpose(heads_out, (1, 0, 2)).reshape(length, width)
    attended = low(low_back(attended))
    projected = low_back(jnp.dot(attended, w_out, precision=highest) + bias_out)
    middle = flat + projected
    normed_two = low(layer_norm(middle, gain_two, shift_two))
    result = middle
    for expert in range(EXPERTS):
        inner = low_back(jnp.dot(normed_two, w_up[:, expert, :], precision=highest) + bias_up[expert])
        hidden = low(jax.nn.gelu(inner))
        branch = low_back(jnp.dot(hidden, w_down[:, expert, :], precision=highest) + bias_down[expert])
        chosen = (routes == expert).astype(jnp.float32)[:, None]
        result = result + chosen * branch
    return result

def reference(tokens, segment_ids, expert_ids, ln1_gain, ln1_bias, qkv_weight, query_bias, value_bias, out_weight, out_bias, ln2_gain, ln2_bias, up_weight, up_bias, down_weight, down_bias, cotangent):
    device_count = N_DP * N_FSDP
    params = tuple((item.astype(jnp.float32) for item in (ln1_gain, ln1_bias, qkv_weight, query_bias, value_bias, out_weight, out_bias, ln2_gain, ln2_bias, up_weight, up_bias, down_weight, down_bias)))
    inputs = tokens.astype(jnp.float32)
    segments = segment_ids.reshape(device_count, TOK_DEV)
    routes = expert_ids[:, 0].reshape(device_count, TOK_DEV)

    def forward(weights, values):
        stacked = values.reshape(device_count, TOK_DEV, D)
        outputs = lax.map(jax.checkpoint(partial(block, weights)), (stacked, segments, routes))
        return outputs.reshape(TOKENS, D)
    result, pull = jax.vjp(forward, params, inputs)
    weight_grads, input_grad = pull(cotangent.astype(jnp.float32))
    return (result.astype(jnp.bfloat16), input_grad, weight_grads[0], weight_grads[1], weight_grads[2], weight_grads[3], weight_grads[4], weight_grads[5], weight_grads[6], weight_grads[7], weight_grads[8], weight_grads[9], weight_grads[10], weight_grads[11], weight_grads[12])
```

```python
import functools

import jax
import jax.numpy as jnp
from jax import lax
from jax.experimental import pallas as pl
from jax.experimental.pallas import tpu as pltpu
from jax.sharding import Mesh, PartitionSpec as P

HEAD_DIM = 64
CAPACITY = 640
LONGEST = 512
PAIR = 2 * HEAD_DIM
TILE_Q = 256
MASKED = -1e30
epsilon = 1e-05
bf16 = jnp.bfloat16
f32 = jnp.float32
ALL = ("dp", "z", "c")
NN = (((1,), (0,)), ((), ()))
NT = (((1,), (1,)), ((), ()))
TN = (((0,), (0,)), ((), ()))


def dot(a, b, dims=NN):
    return lax.dot_general(a, b, dims, preferred_element_type=f32)


def spans(rows):
    out = []
    for start in range(0, rows, TILE_Q):
        low = max(0, (start - LONGEST + 1) // TILE_Q * TILE_Q)
        out.append((start, low, start + TILE_Q))
    return out


def fill_bias(bias_refs, seg_col, seg_row, blocks):
    for bias, (start, low, high) in zip(bias_refs, blocks):
        shape = (high - low, TILE_Q)
        key = low + lax.broadcasted_iota(jnp.int32, shape, 0)
        query = start + lax.broadcasted_iota(jnp.int32, shape, 1)
        same = seg_col[low:high, :] == seg_row[:, start : start + TILE_Q]
        bias[...] = jnp.where((key <= query) & same, 0.0, MASKED)


def forward_kernel(blocks, seg_col, seg_row, q_ref, k_ref, v_ref, o_ref, lse_ref, *bias):
    @pl.when(pl.program_id(0) == 0)
    def _():
        fill_bias(bias, seg_col, seg_row, blocks)

    lane = lax.broadcasted_iota(jnp.int32, (TILE_Q, PAIR), 1)
    for masked, (start, low, high) in zip(bias, blocks):
        rows = slice(start, start + TILE_Q)
        q = q_ref[rows, :] * jnp.asarray(HEAD_DIM**-0.5, bf16)
        k = k_ref[low:high, :]
        v = v_ref[low:high, :]
        heads = []
        for head in range(2):
            mine = (lane < HEAD_DIM) == (head == 0)
            scores = dot(k, jnp.where(mine, q, jnp.zeros_like(q)), NT) + masked[...]
            top = jnp.max(scores, 0, keepdims=True)
            probs = jnp.exp(scores - top)
            total = jnp.sum(probs, 0, keepdims=True)
            out = dot(v, probs.astype(bf16), TN)
            heads.append(out[head * HEAD_DIM : (head + 1) * HEAD_DIM] * (1.0 / total))
            lse_ref[0, head : head + 1, rows] = top + jnp.log(total)
        o_ref[rows, :] = jnp.concatenate(heads, 0).T.astype(bf16)


def attention(qkv, seg_col, seg_row):
    rows, width = qkv.shape[0], qkv.shape[1] // 3
    pairs = width // PAIR
    blocks = spans(rows)
    return pl.pallas_call(
        functools.partial(forward_kernel, blocks),
        out_shape=(
            jax.ShapeDtypeStruct((rows, width), bf16),
            jax.ShapeDtypeStruct((pairs, 2, rows), f32),
        ),
        grid=(pairs,),
        in_specs=[
            pl.BlockSpec((rows, 1), lambda p: (0, 0)),
            pl.BlockSpec((1, rows), lambda p: (0, 0)),
            pl.BlockSpec((rows, PAIR), lambda p: (0, p)),
            pl.BlockSpec((rows, PAIR), lambda p: (0, pairs + p)),
            pl.BlockSpec((rows, PAIR), lambda p: (0, 2 * pairs + p)),
        ],
        out_specs=(
            pl.BlockSpec((rows, PAIR), lambda p: (0, p)),
            pl.BlockSpec((1, 2, rows), lambda p: (p, 0, 0)),
        ),
        scratch_shapes=[pltpu.VMEM((high - low, TILE_Q), f32) for _, low, high in blocks],
        compiler_params=pltpu.CompilerParams(vmem_limit_bytes=48 << 20),
        name="attention_forward",
    )(seg_col, seg_row, qkv, qkv, qkv)


def backward_kernel(
    blocks, first, seg_col, seg_row, q_ref, k_ref, v_ref, do_ref, lse_ref, d_ref, dk_sum, dv_sum, *bias
):
    @pl.when(pl.program_id(0) == 0)
    def _():
        fill_bias(bias, seg_col, seg_row, blocks)

    dk_sum[...] = jnp.zeros_like(dk_sum)
    dv_sum[...] = jnp.zeros_like(dv_sum)
    lane = lax.broadcasted_iota(jnp.int32, (TILE_Q, PAIR), 1)
    scale = HEAD_DIM**-0.5
    for masked, (start, low, high) in zip(bias, blocks):
        rows = slice(start, start + TILE_Q)
        q = q_ref[rows, :]
        do = do_ref[rows, :]
        k = k_ref[low:high, :]
        v = v_ref[low:high, :]
        scaled = q * jnp.asarray(scale, bf16)
        zero = jnp.zeros_like(q)
        dq, dk, dv = [], 0.0, 0.0
        for head in range(2):
            mine = (lane < HEAD_DIM) == (head == 0)
            do_head = jnp.where(mine, do, zero)
            scores = dot(k, jnp.where(mine, scaled, zero), NT) + masked[...]
            probs = jnp.exp(scores - lse_ref[0, head : head + 1, rows])
            weighted = probs * dot(v, do_head, NT)
            total = jnp.sum(weighted, 0, keepdims=True)
            ds = ((weighted - probs * total) * scale).astype(bf16)
            dv = dv + dot(probs.astype(bf16), do_head)
            dk = dk + dot(ds, jnp.where(mine, q, zero))
            dq.append(dot(k, ds, TN)[head * HEAD_DIM : (head + 1) * HEAD_DIM])
        d_ref[0, rows, :] = jnp.concatenate(dq, 0).T.astype(bf16)
        dk_sum[low:high, :] += dk
        dv_sum[low:high, :] += dv
    d_ref[1, ...] = dk_sum[...].astype(bf16)
    d_ref[2, ...] = dv_sum[...].astype(bf16)


def attention_grad(qkv, do, lse, seg_col, seg_row, half):
    rows, width = qkv.shape[0], qkv.shape[1] // 3
    pairs = width // PAIR
    count = pairs // 2
    blocks = spans(rows)
    first = jnp.reshape(half * count, (1,)).astype(jnp.int32)
    return pl.pallas_call(
        functools.partial(backward_kernel, blocks),
        out_shape=jax.ShapeDtypeStruct((3, rows, count * PAIR), bf16),
        grid_spec=pltpu.PrefetchScalarGridSpec(
            num_scalar_prefetch=1,
            grid=(count,),
            in_specs=[
                pl.BlockSpec((rows, 1), lambda p, b: (0, 0)),
                pl.BlockSpec((1, rows), lambda p, b: (0, 0)),
                pl.BlockSpec((rows, PAIR), lambda p, b: (0, b[0] + p)),
                pl.BlockSpec((rows, PAIR), lambda p, b: (0, pairs + b[0] + p)),
                pl.BlockSpec((rows, PAIR), lambda p, b: (0, 2 * pairs + b[0] + p)),
                pl.BlockSpec((rows, PAIR), lambda p, b: (0, b[0] + p)),
                pl.BlockSpec((1, 2, rows), lambda p, b: (b[0] + p, 0, 0)),
            ],
            out_specs=pl.BlockSpec((3, rows, PAIR), lambda p, b: (0, 0, p)),
            scratch_shapes=[pltpu.VMEM((rows, PAIR), f32)] * 2
            + [pltpu.VMEM((high - low, TILE_Q), f32) for _, low, high in blocks],
        ),
        compiler_params=pltpu.CompilerParams(vmem_limit_bytes=48 << 20),
        name="attention_backward",
    )(first, seg_col, seg_row, qkv, qkv, qkv, do, lse)


def layer_norm(values, gain, shift):
    centre = values - jnp.mean(values, -1, keepdims=True)
    spread = jnp.mean(centre * centre, -1, keepdims=True)
    return centre * lax.rsqrt(spread + epsilon) * gain + shift


def pick(array, index, axis=0):
    return lax.dynamic_index_in_dim(array, index, axis, keepdims=False)


def swap(value, axis, size, mask):
    return lax.ppermute(value, axis, [(i, i ^ mask) for i in range(size)])


def swap_core(value):
    return swap(value, "c", 2, 1)


def by_core(core, mine, other, axis=0):
    return jnp.where(core == 0, jnp.stack([mine, other], axis), jnp.stack([other, mine], axis))


def scatter_dp(partial, n_dp):
    me = lax.axis_index("dp")
    if n_dp != 4:
        total = pick(partial, me).astype(f32)
        for mask in range(1, n_dp):
            total = total + swap(pick(partial, me ^ mask), "dp", n_dp, mask).astype(f32)
        return total.astype(bf16)
    half = partial.shape[-1] // 2
    far = pick(partial, me ^ 3)
    by_x = swap(far[..., :half], "dp", 4, 1)
    by_y = swap(far[..., half:], "dp", 4, 2)
    next_x, next_y = pick(partial, me ^ 1), pick(partial, me ^ 2)
    add = lambda a, b: (a.astype(f32) + b.astype(f32)).astype(bf16)
    next_x = jnp.concatenate([next_x[..., :half], add(next_x[..., half:], by_y)], -1)
    next_y = jnp.concatenate([add(next_y[..., :half], by_x), next_y[..., half:]], -1)
    got_x = swap(next_x, "dp", 4, 1)
    got_y = swap(next_y, "dp", 4, 2)
    return (pick(partial, me).astype(f32) + got_x.astype(f32) + got_y.astype(f32)).astype(bf16)


def scatter(partial, n_dp, n_z):
    rows, columns = partial.shape
    mine = scatter_dp(partial.reshape(n_dp, rows // n_dp, columns), n_dp)
    blocks = mine.reshape(n_z, rows // n_dp // n_z, columns)
    at = lax.axis_index("z")
    total = pick(blocks, at).astype(f32)
    for mask in range(1, n_z):
        total = total + swap(pick(blocks, at ^ mask), "z", n_z, mask).astype(f32)
    core = lax.axis_index("c")
    halves = total.reshape(2, rows // n_dp // n_z // 2, columns)
    return pick(halves, core), swap_core(pick(halves, 1 - core))


def shards(
    n_dp,
    n_z,
    tokens,
    segment_ids,
    expert_ids,
    ln1_gain,
    ln1_bias,
    qkv_weight,
    query_bias,
    value_bias,
    out_weight,
    out_bias,
    ln2_gain,
    ln2_bias,
    up_weight,
    up_bias,
    down_weight,
    down_bias,
    cotangent,
):
    rows, width = tokens.shape
    devices = n_dp * n_z * 2
    share = qkv_weight.shape[0]
    up_share = up_bias.shape[1]
    hidden = up_share * devices
    core = lax.axis_index("c")

    small = jnp.concatenate(
        [ln1_gain, ln1_bias, query_bias, value_bias, out_bias, ln2_gain, ln2_bias, up_bias.reshape(-1), down_bias.reshape(-1)]
    )
    used = small.shape[0]
    small = jnp.pad(small, (0, share * 128 - used)).reshape(share, 128)
    packed = lax.all_gather(jnp.concatenate([qkv_weight, out_weight, small], 1), ALL, axis=0, tiled=True)
    w_qkv = packed[:, : 3 * width]
    w_out = packed[:, 3 * width : 4 * width]
    small = packed[:, 4 * width :].reshape(devices, share * 128)[:, :used].astype(f32)
    gain_one, shift_one, bias_query, bias_value, bias_out, gain_two, shift_two = (
        small[:, i * share : (i + 1) * share].reshape(-1) for i in range(7)
    )
    bias_up = small[:, 7 * share : 7 * share + 2 * up_share].reshape(devices, 2, up_share)
    bias_up = pick(bias_up, core, 1).reshape(-1)
    bias_down = small[:, 7 * share + 2 * up_share :].reshape(devices, 2, share)
    bias_down = jnp.swapaxes(bias_down, 0, 1).reshape(2, width)

    def expert_shard(weight):
        mine, other = pick(weight, core, 1), swap_core(pick(weight, 1 - core, 1))
        both = by_core(core, mine, other)
        return both.reshape(2 * weight.shape[0], weight.shape[2])

    w_up = lax.all_gather(expert_shard(up_weight), ("dp", "z"), axis=0, tiled=True)
    w_down = lax.all_gather(expert_shard(down_weight), ("dp", "z"), axis=0, tiled=True)

    route = expert_ids[:, 0]
    place = lax.iota(jnp.int32, rows)
    before = (route[:, None] == route[None, :]) & (place[None, :] < place[:, None])
    slot = jnp.sum(before.astype(jnp.int32), 1) + jnp.where(route == core, 0, CAPACITY)
    chosen = (lax.iota(jnp.int32, 2 * CAPACITY)[:, None] == slot[None, :]).astype(bf16)

    def dispatch(values):
        slots = dot(chosen, values).astype(bf16)
        return jnp.concatenate([slots[:CAPACITY], swap_core(slots[CAPACITY:])], 0)

    def combine(slots):
        both = jnp.concatenate([slots[:CAPACITY], swap_core(slots[CAPACITY:])], 0)
        return dot(chosen, both, TN)

    expert_grad = dispatch(cotangent)

    inputs = tokens.astype(f32)
    normed_one = layer_norm(inputs, gain_one, shift_one).astype(bf16)
    other_normed_one = swap_core(normed_one)
    qkv_bias = jnp.concatenate([bias_query, jnp.zeros_like(bias_query), bias_value])
    qkv = (dot(normed_one, w_qkv) + qkv_bias).astype(bf16)
    seg_row, seg_col = segment_ids, segment_ids.reshape(rows, 1)
    attended, lse = attention(qkv, seg_col, seg_row)
    other_attended = swap_core(attended)
    middle = inputs + dot(attended, w_out) + bias_out
    normed_two = layer_norm(middle, gain_two, shift_two).astype(bf16)

    expert_input = dispatch(normed_two)
    inner = dot(expert_input, w_up) + bias_up
    root = 0.7978845608028654
    inner_sq = inner * inner
    bent = jnp.tanh(root * inner * (1.0 + 0.044715 * inner_sq))
    act = (0.5 * inner * (1.0 + bent)).astype(bf16)
    slope = 0.5 * (1.0 + bent) + 0.5 * inner * (1.0 - bent * bent) * (root * (1.0 + 3 * 0.044715 * inner_sq))
    act, slope = lax.optimization_barrier((act, slope.astype(bf16)))
    down_partial = dot(act, expert_grad, TN).astype(bf16)
    branch = combine(dot(act, w_down).astype(bf16))
    token_bias = jnp.where(route[:, None] == 0, bias_down[:1], bias_down[1:])
    block_out = (middle + branch + token_bias).astype(bf16)

    inner_grad = (dot(expert_grad, w_down, NT) * slope.astype(f32)).astype(bf16)
    up_partial = dot(expert_input, inner_grad, TN).astype(bf16)
    up_bias_grad = jnp.sum(inner_grad.astype(f32), 0)
    down_bias_grad = jnp.sum(expert_grad.astype(f32), 0)
    normed_two_grad = combine(dot(inner_grad, w_up, NT).astype(bf16))
    down_mine, down_other = scatter(down_partial, n_dp, n_z)
    up_mine, up_other = scatter(up_partial, n_dp, n_z)
    down_weight_grad = by_core(core, down_mine, down_other, 1)
    up_weight_grad = by_core(core, up_mine, up_other, 1)

    _, pull_two = jax.vjp(layer_norm, middle, gain_two, shift_two)
    middle_part, gain_two_grad, shift_two_grad = pull_two(normed_two_grad)
    middle_grad = cotangent.astype(f32) + middle_part

    projected_grad = middle_grad.astype(bf16)
    halves = projected_grad.reshape(rows, 2, width // 2)
    mine_projected = pick(halves, core, 1)
    other_projected = swap_core(pick(halves, 1 - core, 1))
    out_partial = (dot(attended, mine_projected, TN) + dot(other_attended, other_projected, TN)).astype(bf16)
    out_bias_grad = jnp.sum(projected_grad.astype(f32), 0)
    attended_grad = dot(projected_grad, w_out, NT).astype(bf16)
    out_mine, out_other = scatter(out_partial, n_dp, n_z)
    out_weight_grad = by_core(core, out_mine, out_other, 1).reshape(share, width)

    grad_away = attention_grad(qkv, attended_grad, lse, seg_col, seg_row, 1 - core)
    grad_other = swap_core(grad_away)
    grad_mine = attention_grad(qkv, attended_grad, lse, seg_col, seg_row, core)
    qkv_partial = jnp.concatenate(
        [(dot(normed_one, grad_mine[j], TN) + dot(other_normed_one, grad_other[j], TN)).astype(bf16) for j in range(3)], 1
    )
    qkv_mine, qkv_other = scatter(qkv_partial, n_dp, n_z)
    qkv_weight_grad = by_core(
        core, qkv_mine.reshape(share, 3, width // 2), qkv_other.reshape(share, 3, width // 2), 2
    ).reshape(share, 3 * width)

    qkv_grad = by_core(core, grad_mine, grad_away, 2).reshape(3, rows, width)
    qkv_grad = jnp.concatenate([qkv_grad[0], qkv_grad[1], qkv_grad[2]], 1)
    query_bias_grad = jnp.sum(qkv_grad[:, :width].astype(f32), 0)
    value_bias_grad = jnp.sum(qkv_grad[:, 2 * width :].astype(f32), 0)
    normed_one_grad = dot(qkv_grad, w_qkv, NT)
    _, pull_one = jax.vjp(layer_norm, inputs, gain_one, shift_one)
    input_part, gain_one_grad, shift_one_grad = pull_one(normed_one_grad)
    input_grad = middle_grad + input_part

    vectors = [
        gain_one_grad,
        shift_one_grad,
        query_bias_grad,
        value_bias_grad,
        out_bias_grad,
        gain_two_grad,
        shift_two_grad,
        up_bias_grad,
        down_bias_grad,
    ]
    sent = jnp.concatenate([v.reshape(devices, -1) for v in vectors], 1)
    got = lax.all_to_all(sent, ALL, 0, 0, tiled=True).reshape(devices // 2, 2, -1)
    both = jnp.sum(got, 0)
    total = both[0] + both[1]
    sums = [total[i * share : (i + 1) * share] for i in range(7)]
    at = 7 * share
    up_bias_sum = both[:, at : at + up_share]
    down_bias_sum = both[:, at + up_share :]
    return (
        block_out,
        input_grad,
        sums[0],
        sums[1],
        qkv_weight_grad,
        sums[2],
        sums[3],
        out_weight_grad,
        sums[4],
        sums[5],
        sums[6],
        up_weight_grad,
        up_bias_sum,
        down_weight_grad,
        down_bias_sum,
    )


def solution(mesh):
    n_dp, n_z = mesh.shape["dp"], mesh.shape["fsdp"] // 2
    split = Mesh(mesh.devices.reshape(n_dp, n_z, 2), ALL)
    row, flat, wide, cube = P(ALL, None), P(ALL), P(None, ALL), P(ALL, None, None)
    in_specs = (row, row, row, flat, flat, row, flat, flat, row, flat, flat, flat, cube, wide, cube, wide, row)
    out_specs = (row, row, flat, flat, row, flat, flat, row, flat, flat, flat, cube, wide, cube, wide)
    return jax.shard_map(
        functools.partial(shards, n_dp, n_z), mesh=split, in_specs=in_specs, out_specs=out_specs, check_vma=False
    )
```

```python
import functools

import jax
import jax.numpy as jnp
from jax import lax
from jax.experimental import pallas as pl
from jax.experimental.pallas import tpu as pltpu
from jax.sharding import Mesh, PartitionSpec as P

HEAD_DIM = 64
CAPACITY = 640
LONGEST = 512
PAIR = 2 * HEAD_DIM
TILE_Q = 256
MASKED = -1e30
epsilon = 1e-05
bf16 = jnp.bfloat16
f32 = jnp.float32
ALL = ("dp", "z", "c")
BLOCK = 256
FBLOCK = 512
NN = (((1,), (0,)), ((), ()))
NT = (((1,), (1,)), ((), ()))
TN = (((0,), (0,)), ((), ()))


def dot(a, b, dims=NN):
    return lax.dot_general(a, b, dims, preferred_element_type=f32)


def params(flops, moved, special=0):
    return dict(
        compiler_params=pltpu.CompilerParams(vmem_limit_bytes=58 << 20),
        cost_estimate=pl.CostEstimate(flops=2 * int(flops), bytes_accessed=int(moved), transcendentals=int(special)),
    )


def launch(kernel, name, grid, args, in_specs, out_specs, out_shape, scratch=(), scalars=(), after=(), work=(0, 0)):
    first, last = len(scalars) + len(args), len(scalars) + len(args) + len(after)

    def body(*refs):
        kernel(*refs[:first], *refs[last:])

    return pl.pallas_call(
        body,
        grid_spec=pltpu.PrefetchScalarGridSpec(
            num_scalar_prefetch=len(scalars),
            grid=grid,
            in_specs=[*in_specs, *[pl.BlockSpec(memory_space=pl.ANY)] * len(after)],
            out_specs=out_specs,
            scratch_shapes=list(scratch),
        ),
        out_shape=out_shape,
        **params(*work),
        name=name,
    )(*scalars, *args, *after)


def whole(*shape):
    return pl.BlockSpec(shape, lambda *_: (0,) * len(shape))


def shape_of(shape, dtype):
    return jax.ShapeDtypeStruct(shape, dtype)


def spans(rows):
    out = []
    for start in range(0, rows, TILE_Q):
        low = max(0, (start - LONGEST + 1) // TILE_Q * TILE_Q)
        out.append((start, low, start + TILE_Q))
    return out


def fill_bias(bias_refs, seg_col, seg_row, blocks):
    for bias, (start, low, high) in zip(bias_refs, blocks):
        shape = (high - low, TILE_Q)
        key = low + lax.broadcasted_iota(jnp.int32, shape, 0)
        query = start + lax.broadcasted_iota(jnp.int32, shape, 1)
        same = seg_col[low:high, :] == seg_row[:, start : start + TILE_Q]
        bias[...] = jnp.where((key <= query) & same, 0.0, MASKED)


def forward_kernel(blocks, seg_col, seg_row, q_ref, k_ref, v_ref, o_ref, lse_ref, *bias):
    @pl.when(pl.program_id(0) == 0)
    def _():
        fill_bias(bias, seg_col, seg_row, blocks)

    lane = lax.broadcasted_iota(jnp.int32, (TILE_Q, PAIR), 1)
    for masked, (start, low, high) in zip(bias, blocks):
        rows = slice(start, start + TILE_Q)
        q = q_ref[rows, :] * jnp.asarray(HEAD_DIM**-0.5, bf16)
        k = k_ref[low:high, :]
        v = v_ref[low:high, :]
        heads = []
        for head in range(2):
            mine = (lane < HEAD_DIM) == (head == 0)
            scores = dot(k, jnp.where(mine, q, jnp.zeros_like(q)), NT) + masked[...]
            top = jnp.max(scores, 0, keepdims=True)
            probs = jnp.exp(scores - top)
            total = jnp.sum(probs, 0, keepdims=True)
            out = dot(v, probs.astype(bf16), TN)
            heads.append(out[head * HEAD_DIM : (head + 1) * HEAD_DIM] * (1.0 / total))
            lse_ref[0, head : head + 1, rows] = top + jnp.log(total)
        o_ref[rows, :] = jnp.concatenate(heads, 0).T.astype(bf16)


def attention(qkv, seg_col, seg_row, after=()):
    rows, width = qkv.shape[0], qkv.shape[1] // 3
    pairs = width // PAIR
    blocks = spans(rows)
    return launch(
        functools.partial(forward_kernel, blocks),
        "attention_forward",
        (pairs,),
        (seg_col, seg_row, qkv, qkv, qkv),
        [
            whole(rows, 1),
            whole(1, rows),
            pl.BlockSpec((rows, PAIR), lambda p: (0, p)),
            pl.BlockSpec((rows, PAIR), lambda p: (0, pairs + p)),
            pl.BlockSpec((rows, PAIR), lambda p: (0, 2 * pairs + p)),
        ],
        (pl.BlockSpec((rows, PAIR), lambda p: (0, p)), pl.BlockSpec((1, 2, rows), lambda p: (p, 0, 0))),
        (shape_of((rows, width), bf16), shape_of((pairs, 2, rows), f32)),
        [pltpu.VMEM((high - low, TILE_Q), f32) for _, low, high in blocks],
        after=after,
        work=(16 * rows * rows * width, 8 * rows * width),
    )


def backward_kernel(
    blocks, first, seg_col, seg_row, q_ref, k_ref, v_ref, do_ref, lse_ref, d_ref, dk_sum, dv_sum, *bias
):
    @pl.when(pl.program_id(0) == 0)
    def _():
        fill_bias(bias, seg_col, seg_row, blocks)

    dk_sum[...] = jnp.zeros_like(dk_sum)
    dv_sum[...] = jnp.zeros_like(dv_sum)
    lane = lax.broadcasted_iota(jnp.int32, (TILE_Q, PAIR), 1)
    scale = HEAD_DIM**-0.5
    for masked, (start, low, high) in zip(bias, blocks):
        rows = slice(start, start + TILE_Q)
        q = q_ref[rows, :]
        do = do_ref[rows, :]
        k = k_ref[low:high, :]
        v = v_ref[low:high, :]
        scaled = q * jnp.asarray(scale, bf16)
        zero = jnp.zeros_like(q)
        dq, dk, dv = [], 0.0, 0.0
        for head in range(2):
            mine = (lane < HEAD_DIM) == (head == 0)
            do_head = jnp.where(mine, do, zero)
            scores = dot(k, jnp.where(mine, scaled, zero), NT) + masked[...]
            probs = jnp.exp(scores - lse_ref[0, head : head + 1, rows])
            weighted = probs * dot(v, do_head, NT)
            total = jnp.sum(weighted, 0, keepdims=True)
            ds = ((weighted - probs * total) * scale).astype(bf16)
            dv = dv + dot(probs.astype(bf16), do_head)
            dk = dk + dot(ds, jnp.where(mine, q, zero))
            dq.append(dot(k, ds, TN)[head * HEAD_DIM : (head + 1) * HEAD_DIM])
        d_ref[0, rows, :] = jnp.concatenate(dq, 0).T.astype(bf16)
        dk_sum[low:high, :] += dk
        dv_sum[low:high, :] += dv
    d_ref[1, ...] = dk_sum[...].astype(bf16)
    d_ref[2, ...] = dv_sum[...].astype(bf16)


def attention_grad(qkv, do, lse, seg_col, seg_row, half, after=()):
    rows, width = qkv.shape[0], qkv.shape[1] // 3
    pairs = width // PAIR
    count = pairs // 2
    blocks = spans(rows)
    first = jnp.reshape(half * count, (1,)).astype(jnp.int32)
    return launch(
        functools.partial(backward_kernel, blocks),
        "attention_backward",
        (count,),
        (seg_col, seg_row, qkv, qkv, qkv, do, lse),
        [
            whole(rows, 1),
            whole(1, rows),
            pl.BlockSpec((rows, PAIR), lambda p, b: (0, b[0] + p)),
            pl.BlockSpec((rows, PAIR), lambda p, b: (0, pairs + b[0] + p)),
            pl.BlockSpec((rows, PAIR), lambda p, b: (0, 2 * pairs + b[0] + p)),
            pl.BlockSpec((rows, PAIR), lambda p, b: (0, b[0] + p)),
            pl.BlockSpec((1, 2, rows), lambda p, b: (b[0] + p, 0, 0)),
        ],
        pl.BlockSpec((3, rows, PAIR), lambda p, b: (0, 0, p)),
        shape_of((3, rows, count * PAIR), bf16),
        [pltpu.VMEM((rows, PAIR), f32)] * 2 + [pltpu.VMEM((high - low, TILE_Q), f32) for _, low, high in blocks],
        scalars=(first,),
        after=after,
        work=(12 * rows * rows * width, 8 * rows * width),
    )


def norm_parts(values):
    centre = values - jnp.mean(values, -1, keepdims=True)
    inverse = lax.rsqrt(jnp.mean(centre * centre, -1, keepdims=True) + epsilon)
    return centre * inverse, inverse


def norm_grad(normed, inverse, gain, grad):
    scaled = grad * gain
    return inverse * (
        scaled - jnp.mean(scaled, -1, keepdims=True) - normed * jnp.mean(scaled * normed, -1, keepdims=True)
    )


def add_rows(ref, value):
    @pl.when(pl.program_id(0) == 0)
    def _():
        ref[...] = value

    @pl.when(pl.program_id(0) > 0)
    def _():
        ref[...] += value


def sides(core, mine, other):
    return (mine, core[0]), (other, 1 - core[0])


def project_kernel(core, x_ref, gain, shift, bias, mine_w, other_w, a_ref, qkv_ref):
    half = x_ref.shape[1] // 2
    normed, _ = norm_parts(x_ref[...].astype(f32))
    a = (normed * gain[...] + shift[...]).astype(bf16)
    a_ref[...] = a
    for w, side in sides(core, mine_w, other_w):
        out = dot(a, w[...])
        for j in range(3):
            at = pl.ds(pl.multiple_of(2 * half * j + half * side, half), half)
            qkv_ref[:, at] = (out[:, half * j : half * (j + 1)] + bias[:, at]).astype(bf16)


def project(core, x, gain, shift, bias, mine_w, other_w, after=()):
    rows, width = x.shape
    weight = whole(width, 3 * width // 2)
    return launch(
        project_kernel,
        "project",
        (rows // BLOCK,),
        (x, gain, shift, bias, mine_w, other_w),
        [
            pl.BlockSpec((BLOCK, width), lambda i, c: (i, 0)),
            whole(1, width),
            whole(1, width),
            whole(1, 3 * width),
            weight,
            weight,
        ],
        (
            pl.BlockSpec((BLOCK, width), lambda i, c: (i, 0)),
            pl.BlockSpec((BLOCK, 3 * width), lambda i, c: (i, 0)),
        ),
        (shape_of((rows, width), bf16), shape_of((rows, 3 * width), bf16)),
        scalars=(core,),
        after=after,
        work=(6 * rows * width * width, 6 * width * width + 10 * rows * width),
    )


def send_slots(acc, slot, values, keep_ref, away_ref):
    step = pl.program_id(0)
    chosen = lax.broadcasted_iota(jnp.int32, (2 * CAPACITY, BLOCK), 0) == slot[...]
    part = dot(chosen.astype(bf16), values)

    @pl.when(step == 0)
    def _():
        acc[...] = part

    @pl.when(step > 0)
    def _():
        acc[...] += part

    @pl.when(step == pl.num_programs(0) - 1)
    def _():
        keep_ref[...] = acc[:CAPACITY, :].astype(bf16)
        away_ref[...] = acc[CAPACITY:, :].astype(bf16)


def dispatch_kernel(slot, g_ref, keep_ref, away_ref, acc):
    send_slots(acc, slot, g_ref[...], keep_ref, away_ref)


def dispatch(slot_row, values, after=()):
    rows, width = values.shape
    return launch(
        dispatch_kernel,
        "dispatch",
        (rows // BLOCK,),
        (slot_row, values),
        [pl.BlockSpec((1, BLOCK), lambda i: (0, i)), pl.BlockSpec((BLOCK, width), lambda i: (i, 0))],
        (whole(CAPACITY, width),) * 2,
        (shape_of((CAPACITY, width), bf16),) * 2,
        [pltpu.VMEM((2 * CAPACITY, width), f32)],
        after=after,
        work=(4 * CAPACITY * rows * width, 2 * rows * width + 4 * CAPACITY * width),
    )


def middle_kernel(
    core, slot, x_ref, o_ref, mine_w, other_w, bias, gain, shift, mid_ref, keep_ref, away_ref, acc
):
    half = x_ref.shape[1] // 2
    for w, side in sides(core, mine_w, other_w):
        at = pl.ds(pl.multiple_of(half * side, half), half)
        mid_ref[:, at] = x_ref[:, at].astype(f32) + dot(o_ref[...], w[...]) + bias[:, at]
    normed, _ = norm_parts(mid_ref[...])
    send_slots(acc, slot, (normed * gain[...] + shift[...]).astype(bf16), keep_ref, away_ref)


def out_half(width):
    return pl.BlockSpec((width, width // 2), lambda *_: (0, 3))


def middle_part(core, slot_row, x, attended, mine_w, other_w, bias, gain, shift, after=()):
    rows, width = x.shape
    block = pl.BlockSpec((BLOCK, width), lambda i, c: (i, 0))
    return launch(
        middle_kernel,
        "middle",
        (rows // BLOCK,),
        (slot_row, x, attended, mine_w, other_w, bias, gain, shift),
        [
            pl.BlockSpec((1, BLOCK), lambda i, c: (0, i)),
            block,
            block,
            out_half(width),
            out_half(width),
            whole(1, width),
            whole(1, width),
            whole(1, width),
        ],
        (block, whole(CAPACITY, width), whole(CAPACITY, width)),
        (shape_of((rows, width), f32),) + (shape_of((CAPACITY, width), bf16),) * 2,
        [pltpu.VMEM((2 * CAPACITY, width), f32)],
        scalars=(core,),
        after=after,
        work=(4 * CAPACITY * rows * width + 2 * rows * width * width, 10 * rows * width + 4 * CAPACITY * width),
    )


def from_slots(slot, keep_ref, away_ref):
    chosen = lax.broadcasted_iota(jnp.int32, (BLOCK, 2 * CAPACITY), 1) == slot[...]
    chosen = chosen.astype(bf16)
    return dot(chosen[:, :CAPACITY], keep_ref[...]) + dot(chosen[:, CAPACITY:], away_ref[...])


def middle_grad_kernel(
    core, slot, keep_ref, away_ref, mid_ref, g_ref, mine_w, other_w, gain,
    dmid_ref, mine_ref, other_ref, do_ref, gain_ref, shift_ref, bias_ref, dproj_ref,
):
    half = mid_ref.shape[1] // 2
    grad = from_slots(slot, keep_ref, away_ref)
    normed, inverse = norm_parts(mid_ref[...])
    dmid = g_ref[...].astype(f32) + norm_grad(normed, inverse, gain[...], grad)
    dproj_ref[...] = dmid.astype(bf16)
    dmid_ref[...] = dmid
    back = 0.0
    for (w, side), part in zip(sides(core, mine_w, other_w), (mine_ref, other_ref)):
        part[...] = dproj_ref[:, pl.ds(pl.multiple_of(half * side, half), half)]
        back = back + dot(part[...], w[...], NT)
    do_ref[...] = back.astype(bf16)
    add_rows(gain_ref, jnp.sum(grad * normed, 0, keepdims=True))
    add_rows(shift_ref, jnp.sum(grad, 0, keepdims=True))
    add_rows(bias_ref, jnp.sum(dproj_ref[...].astype(f32), 0, keepdims=True))


def middle_grad(core, slot_col, keep, away, middle, g, mine_w, other_w, gain, after=()):
    rows, width = middle.shape
    block = pl.BlockSpec((BLOCK, width), lambda i, c: (i, 0))
    part = pl.BlockSpec((BLOCK, width // 2), lambda i, c: (i, 0))
    slots = whole(CAPACITY, width)
    row = whole(1, width)
    return launch(
        middle_grad_kernel,
        "middle_grad",
        (rows // BLOCK,),
        (slot_col, keep, away, middle, g, mine_w, other_w, gain),
        [pl.BlockSpec((BLOCK, 1), lambda i, c: (i, 0)), slots, slots, block, block]
        + [out_half(width), out_half(width), row],
        (block, part, part, block, row, row, row),
        (shape_of((rows, width), f32),)
        + (shape_of((rows, width // 2), bf16),) * 2
        + (shape_of((rows, width), bf16),)
        + (shape_of((1, width), f32),) * 3,
        [pltpu.VMEM((BLOCK, width), bf16)],
        scalars=(core,),
        after=after,
        work=(4 * CAPACITY * rows * width + 2 * rows * width * width, 16 * rows * width + 4 * CAPACITY * width),
    )


def output_kernel(slot, route, keep_ref, away_ref, mid_ref, bias, out_ref):
    token_bias = jnp.where(route[...] == 0, bias[0:1, :], bias[1:2, :])
    out_ref[...] = (mid_ref[...] + from_slots(slot, keep_ref, away_ref) + token_bias).astype(bf16)


def output(slot_col, route_col, keep, away, middle, bias, after=()):
    rows, width = middle.shape
    block = pl.BlockSpec((BLOCK, width), lambda i: (i, 0))
    column = pl.BlockSpec((BLOCK, 1), lambda i: (i, 0))
    return launch(
        output_kernel,
        "output",
        (rows // BLOCK,),
        (slot_col, route_col, keep, away, middle, bias),
        [column, column, whole(CAPACITY, width), whole(CAPACITY, width), block, whole(2, width)],
        block,
        shape_of((rows, width), bf16),
        after=after,
        work=(4 * CAPACITY * rows * width, 6 * rows * width + 4 * CAPACITY * width),
    )


def input_grad_kernel(
    mine_ref, away_ref, x_ref, dmid_ref, mine_w, other_w, gain, out_ref, gain_ref, shift_ref, bias_ref
):
    half = mine_ref.shape[2]
    grad = 0.0
    for ref, w in ((mine_ref, mine_w), (away_ref, other_w)):
        for j in range(3):
            grad = grad + dot(ref[j], w[:, half * j : half * (j + 1)], NT)
    normed, inverse = norm_parts(x_ref[...].astype(f32))
    out_ref[...] = dmid_ref[...] + norm_grad(normed, inverse, gain[...], grad)
    add_rows(gain_ref, jnp.sum(grad * normed, 0, keepdims=True))
    add_rows(shift_ref, jnp.sum(grad, 0, keepdims=True))
    rows = [jnp.sum(ref[j].astype(f32), 0, keepdims=True) for j in (0, 2) for ref in (mine_ref, away_ref)]
    add_rows(bias_ref, jnp.concatenate(rows, 0))


def input_grads(mine, away, x, dmid, mine_w, other_w, gain, after=()):
    rows, width = x.shape
    half = width // 2
    block = pl.BlockSpec((BLOCK, width), lambda i: (i, 0))
    part = pl.BlockSpec((3, BLOCK, half), lambda i: (0, i, 0))
    row, weight = whole(1, width), whole(width, 3 * half)
    return launch(
        input_grad_kernel,
        "input_grad",
        (rows // BLOCK,),
        (mine, away, x, dmid, mine_w, other_w, gain),
        [part, part, block, block, weight, weight, row],
        (block, row, row, whole(4, half)),
        (
            shape_of((rows, width), f32),
            shape_of((1, width), f32),
            shape_of((1, width), f32),
            shape_of((4, half), f32),
        ),
        after=after,
        work=(6 * rows * width * width, 16 * rows * width + 6 * width * width),
    )


def two_sum_kernel(at, n_dp, me, a1, b1, a2, b2, out_ref, far_x, far_y, t1, t2):
    step = pl.program_id(0)

    @pl.when(step == 0)
    def _():
        t1[...] = a1[...].T
        t2[...] = a2[...].T

    out_ref[...] = (dot(t1[...], b1[0]) + dot(t2[...], b2[0])).astype(bf16)
    rows = out_ref.shape[0] // n_dp
    far = pl.ds(pl.multiple_of((me[0] ^ (n_dp - 1)) * rows, rows), rows)

    @pl.when(step + at < 2)
    def _():
        far_x[...] = out_ref[far, :]

    @pl.when(step + at >= 2)
    def _():
        far_y[...] = out_ref[far, :]


def two_sum(me, n_dp, a1, b1, a2, b2, at, into=(), after=()):
    rows, width = a1.shape
    parts, _, columns = b1.shape
    left, right = whole(rows, width), pl.BlockSpec((1, rows, columns), lambda j, m: (j, 0, 0))
    count = 5 + len(into)

    def body(*refs):
        two_sum_kernel(at, n_dp, *refs[:5], *refs[count + len(after) :])

    far = (width // n_dp, columns)
    return pl.pallas_call(
        body,
        grid_spec=pltpu.PrefetchScalarGridSpec(
            num_scalar_prefetch=1,
            grid=(parts,),
            in_specs=[left, right, left, right] + [pl.BlockSpec(memory_space=pl.ANY)] * (len(into) + len(after)),
            out_specs=(
                pl.BlockSpec((width, columns), lambda j, m: (0, at + j)),
                pl.BlockSpec(far, lambda j, m: (0, jnp.minimum(at + j, 1))),
                pl.BlockSpec(far, lambda j, m: (0, jnp.maximum(at + j - 2, 0))),
            ),
            scratch_shapes=[pltpu.VMEM((width, rows), bf16)] * 2,
        ),
        out_shape=(
            shape_of((width, 4 * columns), bf16),
            shape_of((width // n_dp, 2 * columns), bf16),
            shape_of((width // n_dp, 2 * columns), bf16),
        ),
        input_output_aliases={5 + i: i for i in range(len(into))},
        **params(4 * rows * width * columns * parts, 4 * rows * (width + parts * columns)),
        name="two_sum",
    )(me, a1, b1, a2, b2, *into, *after)


def up_kernel(me, xk, xr, bias, w0, w1, w2, w3a, w3b, act_ref, slope_ref):
    step = pl.program_id(0)
    depth = w0.shape[0]
    far = jnp.where(step < pl.num_programs(0) // 2, w3a[...], w3b[...])
    root = 0.7978845608028654
    for part, x in enumerate((xk, xr)):
        inner = bias[...]
        for r, w in enumerate((w0[...], w1[...], w2[...], far)):
            at = pl.multiple_of((me[0] ^ r) * depth, depth)
            inner = inner + dot(x[:, pl.ds(at, depth)], w)
        square = inner * inner
        bent = jnp.tanh(inner * (root + (root * 0.044715) * square))
        rise = 0.5 + 0.5 * bent
        act = (inner * rise).astype(bf16)
        slope = rise + inner * rise * (1.0 - bent) * (root + (root * 3 * 0.044715) * square)
        rows = slice(part * x.shape[0], (part + 1) * x.shape[0])
        act_ref[rows, :] = act
        slope_ref[rows, :] = slope.astype(bf16)


def up(me, xk, xr, bias, pieces, after=()):
    slots, width = xk.shape
    depth, hidden = pieces[0].shape
    steps = hidden // FBLOCK
    last = steps // 2 - 1
    tokens = whole(slots, width)
    weight = pl.BlockSpec((depth, FBLOCK), lambda i, m: (0, i))
    return launch(
        up_kernel,
        "experts_up",
        (steps,),
        (xk, xr, bias, *pieces),
        [tokens] * 2
        + [pl.BlockSpec((1, FBLOCK), lambda i, m: (0, i))]
        + [weight] * 3
        + [
            pl.BlockSpec((depth, FBLOCK), lambda i, m: (0, jnp.minimum(i, last))),
            pl.BlockSpec((depth, FBLOCK), lambda i, m: (0, jnp.maximum(i - last - 1, 0))),
        ],
        (
            pl.BlockSpec((2 * slots, FBLOCK), lambda i, m: (0, i)),
            pl.BlockSpec((2 * slots, FBLOCK), lambda i, m: (0, i)),
        ),
        (shape_of((2 * slots, hidden), bf16), shape_of((2 * slots, hidden), bf16)),
        scalars=(me,),
        after=after,
        work=(4 * slots * width * hidden, 2 * width * hidden + 8 * slots * hidden),
    )


def outer_kernel(act_ref, gk, gr, out_ref, bias_ref, g):
    @pl.when(pl.program_id(0) == 0)
    def _():
        half = gk.shape[0]
        g[:half, :] = gk[...]
        g[half:, :] = gr[...]
        bias_ref[...] = jnp.sum(g[...].astype(f32), 0, keepdims=True)

    out_ref[...] = dot(act_ref[...], g[...], TN).astype(bf16)


def outer(act, gk, gr, after=()):
    slots, width = gk.shape
    hidden = act.shape[1]
    return launch(
        outer_kernel,
        "experts_outer",
        (hidden // FBLOCK,),
        (act, gk, gr),
        [pl.BlockSpec((2 * slots, FBLOCK), lambda i: (0, i)), whole(slots, width), whole(slots, width)],
        (pl.BlockSpec((FBLOCK, width), lambda i: (i, 0)), whole(1, width)),
        (shape_of((hidden, width), bf16), shape_of((1, width), f32)),
        [pltpu.VMEM((2 * slots, width), bf16)],
        after=after,
        work=(4 * slots * width * hidden, 2 * width * hidden + 4 * slots * hidden),
    )


def hold_block(held, per, pieces):
    w0, w1, w2, w3a, w3b = pieces
    which = pl.program_id(0) // per
    half = w3a.shape[1]
    for r, w in enumerate((w0, w1, w2)):

        @pl.when(which == r)
        def _(w=w):
            held[...] = w[...]

    @pl.when(which == 3)
    def _():
        held[:, :half] = w3a[...]
        held[:, half:] = w3b[...]


def down_grad_kernel(
    me, per, gk, gr, xk, xr, slope_ref, u0, u1, u2, u3a, u3b, w0, w1, w2, w3a, w3b,
    dk_ref, dr_ref, up_ref, far_x, far_y, bias_ref, held, acc, g, t,
):
    step = pl.program_id(0)
    slots = gk.shape[0]
    hold_block(held, per, (w0, w1, w2, w3a, w3b))

    @pl.when(step == 0)
    def _():
        g[:slots, :] = gk[...]
        g[slots:, :] = gr[...]
        t[:, :slots] = xk[...].T
        t[:, slots:] = xr[...].T
        acc[...] = jnp.zeros_like(acc)

    depth = u0.shape[0]
    early = (me[0] ^ (step // per)) * per + step % per < pl.num_programs(0) // 2
    u3 = jnp.where(early, u3a[...], u3b[...])
    inner = (dot(g[...], held[...], NT) * slope_ref[...].astype(f32)).astype(bf16)
    bias_ref[...] = jnp.sum(inner.astype(f32), 0, keepdims=True)
    up_ref[...] = dot(t[...], inner).astype(bf16)
    far = up_ref[pl.ds(pl.multiple_of((me[0] ^ 3) * depth, depth), depth), :]

    @pl.when(early)
    def _():
        far_x[...] = far

    @pl.when(jnp.logical_not(early))
    def _():
        far_y[...] = far

    for r, u in enumerate((u0[...], u1[...], u2[...], u3)):
        at = pl.multiple_of((me[0] ^ r) * depth, depth)
        acc[:, pl.ds(at, depth)] += dot(inner, u, NT)

    @pl.when(step == pl.num_programs(0) - 1)
    def _():
        dk_ref[...] = acc[:slots, :].astype(bf16)
        dr_ref[...] = acc[slots:, :].astype(bf16)


def piece_specs(width, per, which):
    def spec(r, columns):
        return pl.BlockSpec((FBLOCK, columns), lambda i, m: (jnp.clip(i - r * per, 0, per - 1), 0))

    return [spec(r, width // 2 if r == 3 else width) for r in which for _ in range(2 if r == 3 else 1)]


def down_grad(me, gk, gr, xk, xr, slope, up_pieces, down_pieces, after=()):
    slots, width = xk.shape
    depth, hidden = up_pieces[0].shape
    per = down_pieces[0].shape[0] // FBLOCK
    steps = hidden // FBLOCK
    half = steps // 2
    at = lambda i, m: (m[0] ^ (i // per)) * per + i % per

    def far(first):
        def block(i, m):
            low = jnp.where((m[0] < 2) == first, 0, half)
            return 0, at(jnp.clip(i, low, low + half - 1), m) - (0 if first else half)

        return pl.BlockSpec((depth, FBLOCK), block)

    tokens = whole(slots, width)
    weight = pl.BlockSpec((depth, FBLOCK), lambda i, m: (0, at(i, m)))
    return launch(
        lambda me, *refs: down_grad_kernel(me, per, *refs),
        "experts_grad",
        (steps,),
        (gk, gr, xk, xr, slope, *up_pieces, *down_pieces),
        [tokens] * 4
        + [pl.BlockSpec((2 * slots, FBLOCK), lambda i, m: (0, at(i, m)))]
        + [weight] * 3
        + [
            pl.BlockSpec((depth, FBLOCK), lambda i, m: (0, jnp.minimum(at(i, m), half - 1))),
            pl.BlockSpec((depth, FBLOCK), lambda i, m: (0, jnp.maximum(at(i, m) - half, 0))),
        ]
        + piece_specs(width, per, range(4)),
        (
            tokens,
            tokens,
            pl.BlockSpec((width, FBLOCK), lambda i, m: (0, at(i, m))),
            far(True),
            far(False),
            pl.BlockSpec((1, FBLOCK), lambda i, m: (0, at(i, m))),
        ),
        (
            shape_of((slots, width), bf16),
            shape_of((slots, width), bf16),
            shape_of((width, hidden), bf16),
            shape_of((depth, hidden // 2), bf16),
            shape_of((depth, hidden // 2), bf16),
            shape_of((1, hidden), f32),
        ),
        [
            pltpu.VMEM((FBLOCK, width), bf16),
            pltpu.VMEM((2 * slots, width), f32),
            pltpu.VMEM((2 * slots, width), bf16),
            pltpu.VMEM((width, 2 * slots), bf16),
        ],
        scalars=(me,),
        after=after,
        work=(12 * slots * width * hidden, 6 * width * hidden + 4 * slots * hidden),
    )


def down_near_kernel(me, act_ref, w0, w1, w2, out_ref, acc):
    step = pl.program_id(0)
    which = step // (pl.num_programs(0) // 3)
    w = jnp.where(which == 0, w0[...], jnp.where(which == 1, w1[...], w2[...]))
    part = dot(act_ref[...], w)

    @pl.when(step == 0)
    def _():
        acc[...] = part

    @pl.when(step > 0)
    def _():
        acc[...] += part

    @pl.when(step == pl.num_programs(0) - 1)
    def _():
        out_ref[...] = acc[...].astype(bf16)


def down_near(me, act, pieces, after=()):
    slots = act.shape[0]
    rows, width = pieces[0].shape
    per = rows // FBLOCK
    return launch(
        down_near_kernel,
        "down_near",
        (3 * per,),
        (act, *pieces),
        [pl.BlockSpec((slots, FBLOCK), lambda i, m: (0, (m[0] ^ (i // per)) * per + i % per))]
        + piece_specs(width, per, range(3)),
        whole(slots, width),
        shape_of((slots, width), bf16),
        [pltpu.VMEM((slots, width), f32)],
        scalars=(me,),
        after=after,
        work=(2 * slots * width * rows * 3, 2 * width * rows * 3 + 2 * slots * rows * 3),
    )


def down_far_kernel(me, act_ref, wa, wb, near_ref, keep_ref, away_ref, acc):
    half = wa.shape[1]

    @pl.when(pl.program_id(0) == 0)
    def _():
        acc[...] = near_ref[...].astype(f32)

    acc[:, :half] += dot(act_ref[...], wa[...])
    acc[:, half:] += dot(act_ref[...], wb[...])

    @pl.when(pl.program_id(0) == pl.num_programs(0) - 1)
    def _():
        slots = keep_ref.shape[0]
        keep_ref[...] = acc[:slots, :].astype(bf16)
        away_ref[...] = acc[slots:, :].astype(bf16)


def down_far(me, act, wa, wb, near, after=()):
    slots, width = near.shape
    per = wa.shape[0] // FBLOCK
    half = pl.BlockSpec((FBLOCK, width // 2), lambda i, m: (i, 0))
    return launch(
        down_far_kernel,
        "down_far",
        (per,),
        (act, wa, wb, near),
        [pl.BlockSpec((slots, FBLOCK), lambda i, m: (0, (m[0] ^ 3) * per + i)), half, half, whole(slots, width)],
        (whole(slots // 2, width),) * 2,
        (shape_of((slots // 2, width), bf16),) * 2,
        [pltpu.VMEM((slots, width), f32)],
        scalars=(me,),
        after=after,
        work=(2 * slots * width * wa.shape[0], 6 * slots * width),
    )


def place_kernel(at, *refs):
    out_ref = refs[-1]
    for r, piece in enumerate(refs[: 4 if len(refs) == 6 else -1]):

        @pl.when(pl.program_id(0) == r)
        def _(r=r, piece=piece):
            columns = piece.shape[1]
            out_ref[0, :, :columns] = piece[...]
            if columns < out_ref.shape[2]:
                out_ref[0, :, columns:] = refs[r + 1][...]


def place(at, pieces, after=()):
    rows, columns = pieces[0].shape
    count = sum(p.shape[1] for p in pieces) // columns
    return launch(
        place_kernel,
        "place",
        (count,),
        pieces,
        [whole(*p.shape) for p in pieces],
        pl.BlockSpec((1, rows, columns), lambda r, at: (at[0] ^ r, 0, 0)),
        shape_of((count, rows, columns), bf16),
        scalars=(at,),
        after=after,
        work=(0, 4 * count * rows * columns),
    ).reshape(count * rows, columns)


def pick(array, index, axis=0):
    return lax.dynamic_index_in_dim(array, index, axis, keepdims=False)


def swap(value, axis, size, mask):
    return lax.ppermute(value, axis, [(i, i ^ mask) for i in range(size)])


def swap_core(value):
    return swap(value, "c", 2, 1)


def by_core(core, mine, other, axis=0):
    return jnp.where(core == 0, jnp.stack([mine, other], axis), jnp.stack([other, mine], axis))


def add_kernel(me, part_x, part_y, by_x, by_y, next_x, next_y):
    first = pl.program_id(0) == 0
    more_x = jnp.where(first, 0.0, by_y[...].astype(f32))
    more_y = jnp.where(first, by_x[...].astype(f32), 0.0)
    next_x[...] = (part_x[0].astype(f32) + more_x).astype(bf16)
    next_y[...] = (part_y[0].astype(f32) + more_y).astype(bf16)


def scatter_next(me, partial, by_x, by_y, after=()):
    _, rows, columns = partial.shape
    half = columns // 2
    step = rows // 2
    block = lambda mask: pl.BlockSpec((1, step, half), lambda h, i, m: (m[0] ^ mask, i, h))
    next_x, next_y = launch(
        add_kernel,
        "far_add",
        (2, 2),
        (partial, partial, by_x, by_y),
        [
            block(1),
            block(2),
            pl.BlockSpec((step, half), lambda h, i, m: (jnp.where(h == 0, i, 1), 0)),
            pl.BlockSpec((step, half), lambda h, i, m: (jnp.where(h == 0, 0, i), 0)),
        ],
        (pl.BlockSpec((step, half), lambda h, i, m: (i, h)),) * 2,
        (shape_of((rows, columns), bf16),) * 2,
        scalars=(me,),
        after=after,
    )
    return next_x, next_y


def swap_near(x, y):
    return swap(x, "dp", 4, 1), swap(y, "dp", 4, 2)


def near_kernel(me, part, got_x, got_y, out_ref):
    out_ref[...] = (part[0].astype(f32) + got_x[...].astype(f32) + got_y[...].astype(f32)).astype(bf16)


def scatter_near(me, partial, got_x, got_y, after=()):
    _, rows, columns = partial.shape
    step = rows // 4
    block = pl.BlockSpec((step, columns), lambda i, m: (i, 0))
    return launch(
        near_kernel,
        "near_add",
        (4,),
        (partial, got_x, got_y),
        [pl.BlockSpec((1, step, columns), lambda i, m: (m[0], i, 0)), block, block],
        block,
        shape_of((rows, columns), bf16),
        scalars=(me,),
        after=after,
    )


def to_core(total):
    core = lax.axis_index("c")
    halves = total.reshape(2, total.shape[0] // 2, total.shape[1])
    return pick(halves, core), swap_core(pick(halves, 1 - core))


def gather_z(shard):
    return lax.all_gather(shard, "z", axis=0, tiled=True)


def scatter_z(block):
    return lax.psum_scatter(block, "z", scatter_dimension=0, tiled=True)


def later(value, after):
    def body(*refs):
        pass

    return pl.pallas_call(
        body,
        in_specs=[pl.BlockSpec(memory_space=pl.ANY)] * (1 + len(after)),
        out_specs=pl.BlockSpec(memory_space=pl.ANY),
        out_shape=shape_of(value.shape, value.dtype),
        input_output_aliases={0: 0},
        **params(0, 0),
        name="later",
    )(value, *after)


def halves_kernel(x_ref, y_ref, out_x, out_y):
    half = out_x.shape[1]
    out_x[...] = x_ref[:, :half]
    out_y[...] = y_ref[:, half:]


def cut_halves(by_x, by_y, after=()):
    rows, columns = by_x.shape
    step = rows // 2
    block = pl.BlockSpec((step, columns), lambda i: (i, 0))
    half = pl.BlockSpec((step, columns // 2), lambda i: (i, 0))
    return launch(
        halves_kernel,
        "cut_halves",
        (2,),
        (by_x, by_y),
        [block, block],
        (half, half),
        (shape_of((rows, columns // 2), bf16),) * 2,
        after=after,
    )


def gather_far(cut):
    return swap(cut[0], "dp", 4, 2), swap(cut[1], "dp", 4, 1)


def gather_pieces(own):
    full = lax.all_gather(own, "dp", axis=0, tiled=True)
    rows, columns = full.shape
    blocks = full.reshape(4, rows // 4, columns)
    return blocks[0], blocks[1], blocks[2], blocks[3, :, : columns // 2], blocks[3, :, columns // 2 :]


def shards(
    n_dp,
    n_z,
    tokens,
    segment_ids,
    expert_ids,
    ln1_gain,
    ln1_bias,
    qkv_weight,
    query_bias,
    value_bias,
    out_weight,
    out_bias,
    ln2_gain,
    ln2_bias,
    up_weight,
    up_bias,
    down_weight,
    down_bias,
    cotangent,
):
    rows, width = tokens.shape
    devices = n_dp * n_z * 2
    share = qkv_weight.shape[0]
    up_share = up_bias.shape[1]
    core = lax.axis_index("c")
    scalar = lambda v: jnp.reshape(v, (1,)).astype(jnp.int32)
    square = n_dp == 4
    me = scalar(lax.axis_index("dp") if square else 0)

    half = width // 2
    both_w = jnp.concatenate([qkv_weight, out_weight], 1).reshape(share, 4, 2, half)
    mine_w, other_w = (pick(both_w, side, 2).reshape(share, 4 * half) for side in (core, 1 - core))
    attn_shard = place(scalar(core), [mine_w, swap_core(other_w)])
    small = jnp.concatenate(
        [ln1_gain, ln1_bias, query_bias, value_bias, out_bias, ln2_gain, ln2_bias, up_bias.reshape(-1), down_bias.reshape(-1)]
    )
    small = jnp.broadcast_to(small, (devices, small.shape[0]))
    small = lax.all_to_all(small, ALL, 0, 0, tiled=True).astype(f32)
    gain_one, shift_one, bias_query, bias_value, bias_out, gain_two, shift_two = (
        small[:, i * share : (i + 1) * share].reshape(1, width) for i in range(7)
    )
    bias_up = small[:, 7 * share : 7 * share + 2 * up_share].reshape(devices, 2, up_share)
    bias_up = pick(bias_up, core, 1).reshape(1, -1)
    bias_down = small[:, 7 * share + 2 * up_share :].reshape(devices, 2, share)
    bias_down = jnp.swapaxes(bias_down, 0, 1).reshape(2, width)

    def expert_shard(weight, after):
        mine, other = pick(weight, core, 1), swap_core(pick(weight, 1 - core, 1))
        return place(scalar(core), [mine, other], after)

    route = expert_ids[:, 0]
    at = lax.iota(jnp.int32, rows)
    before = (route[:, None] == route[None, :]) & (at[None, :] < at[:, None])
    slot = jnp.sum(before.astype(jnp.int32), 1) + jnp.where(route == core, 0, CAPACITY)
    slot_row, slot_col = slot.reshape(1, rows), slot.reshape(rows, 1)

    grad_keep, grad_away = dispatch(slot_row, cotangent, (attn_shard,))
    grad_got = swap_core(grad_away)
    up_shard = expert_shard(up_weight, (grad_keep,))
    up_own = gather_z(up_shard)
    down_shard = expert_shard(down_weight, (up_shard,))
    attn_own = later(gather_z(attn_shard), (down_shard,))
    if square:
        attn_near = swap_near(attn_own, attn_own)
        attn_far = gather_far(cut_halves(*attn_near))
        mine_w = place(me, [attn_own, *attn_near, *attn_far], (up_own, down_shard, grad_got, bias_down))
        up_near = swap_near(up_own, up_own)
    else:
        mine_w = lax.all_gather(attn_own, "dp", axis=0, tiled=True)
    other_w = swap_core(mine_w)

    side = scalar(core)
    qkv_bias = jnp.concatenate([bias_query, jnp.zeros_like(bias_query), bias_value], 1)
    normed_one, qkv = project(side, tokens, gain_one, shift_one, qkv_bias, mine_w, other_w, (up_own,))
    other_normed_one = swap_core(normed_one)
    seg_row, seg_col = segment_ids, segment_ids.reshape(rows, 1)
    attended, lse = attention(qkv, seg_col, seg_row)
    other_attended = swap_core(attended)
    if square:
        up_cut = cut_halves(*up_near, (attended,))
        w_up = (up_own, *up_near, *gather_far(up_cut))
    else:
        up_cut, w_up = (), gather_pieces(up_own)
    middle, in_keep, in_away = middle_part(
        side, slot_row, tokens, attended, mine_w, other_w, bias_out, gain_two, shift_two, after=(*up_cut, other_normed_one)
    )
    down_own = later(gather_z(down_shard), (middle,))
    in_got = swap_core(later(in_away, (*w_up[3:], down_own)))

    if square:
        down_near_got = swap_near(down_own, down_own)
    act, slope = up(me, in_keep, in_got, bias_up, w_up)
    down_partial, down_bias_grad = outer(act, grad_keep, grad_got)
    if square:
        down_cut = cut_halves(*down_near_got, (down_partial,))
        w_down = (down_own, *down_near_got, *gather_far(down_cut))
    else:
        down_cut, w_down = (), gather_pieces(down_own)
    y_near = down_near(me, act, w_down[:3], down_cut)
    down_half = lax.psum_scatter(later(down_partial, (*w_down[3:], y_near)), "dp", scatter_dimension=0, tiled=True)
    back_keep, back_away, up_partial, up_out_x, up_out_y, up_bias_grad = down_grad(
        me, grad_keep, grad_got, in_keep, in_got, slope, w_up, w_down, after=(y_near,)
    )
    back_got = swap_core(back_away)
    if square:
        up_partial = up_partial.reshape(4, width // 4, -1)
        up_far = swap_near(up_out_x, up_out_y)

    middle_grads, mine_projected, other_projected, attended_grad, gain_two_grad, shift_two_grad, out_bias_grad = (
        middle_grad(side, slot_col, back_keep, back_got, middle, cotangent, mine_w, other_w, gain_two)
    )
    other_projected = swap_core(other_projected)
    qkv_away = attention_grad(qkv, attended_grad, lse, seg_col, seg_row, 1 - core)
    qkv_got = swap_core(qkv_away)
    up_next = scatter_next(me, up_partial, *up_far, after=(qkv_away,)) if square else ()
    partial = two_sum(
        me, 4, attended, mine_projected[None], other_attended, other_projected[None], 0, after=up_next
    )
    down_total = scatter_z(later(down_half, up_next))
    qkv_kept = attention_grad(qkv, attended_grad, lse, seg_col, seg_row, core, after=partial[:1])
    partial, out_x, out_y = two_sum(
        me, 4, normed_one, qkv_kept, other_normed_one, qkv_got, 1, into=partial, after=()
    )
    if square:
        partial = partial.reshape(4, width // 4, -1)
        far = swap_near(out_x, out_y)
        up_block = scatter_near(me, up_partial, *swap_near(*up_next), after=(out_x, down_total))
    else:
        up_block = lax.psum_scatter(up_partial, "dp", scatter_dimension=0, tiled=True)
    up_total = scatter_z(up_block)
    y_keep, y_away = down_far(me, act, *w_down[3:], y_near, after=(up_block,))
    y_got = swap_core(y_away)
    near = scatter_next(me, partial, *far, after=(y_keep,)) if square else ()
    input_grad, gain_one_grad, shift_one_grad, bias_sums = input_grads(
        qkv_kept, qkv_away, tokens, middle_grads, mine_w, other_w, gain_one, after=near
    )
    query_bias_grad = by_core(core, bias_sums[0], bias_sums[1])
    value_bias_grad = by_core(core, bias_sums[2], bias_sums[3])
    if square:
        last = scatter_near(me, partial, *swap_near(*near), after=(input_grad,))
    else:
        last = lax.psum_scatter(partial, "dp", scatter_dimension=0, tiled=True)

    vectors = [
        gain_one_grad,
        shift_one_grad,
        query_bias_grad,
        value_bias_grad,
        out_bias_grad,
        gain_two_grad,
        shift_two_grad,
        up_bias_grad,
        down_bias_grad,
    ]
    sent = later(jnp.concatenate([v.reshape(devices, -1) for v in vectors], 1), (last,))
    got = lax.all_to_all(sent, ALL, 0, 0, tiled=True).reshape(devices // 2, 2, -1)
    both = jnp.sum(got, 0)
    total = both[0] + both[1]
    sums = [total[i * share : (i + 1) * share] for i in range(7)]
    at = 7 * share
    up_bias_sum = both[:, at : at + up_share]
    down_bias_sum = both[:, at + up_share :]

    block_out = output(slot_col, expert_ids, y_keep, y_got, middle, bias_down, after=(sent,))
    down_weight_grad = by_core(core, *to_core(down_total.astype(f32)), 1)
    up_weight_grad = by_core(core, *to_core(up_total.astype(f32)), 1)
    last = later(scatter_z(last), (block_out, down_weight_grad, up_weight_grad))
    last = to_core(last.astype(f32))
    out_weight_grad = by_core(core, *(v[:, :half] for v in last), 1).reshape(share, width)
    qkv_weight_grad = by_core(core, *(v[:, half:].reshape(share, 3, half) for v in last), 2).reshape(share, 3 * width)
    return (
        block_out,
        input_grad,
        sums[0],
        sums[1],
        qkv_weight_grad,
        sums[2],
        sums[3],
        out_weight_grad,
        sums[4],
        sums[5],
        sums[6],
        up_weight_grad,
        up_bias_sum,
        down_weight_grad,
        down_bias_sum,
    )


def solution(mesh):
    n_dp, n_z = mesh.shape["dp"], mesh.shape["fsdp"] // 2
    split = Mesh(mesh.devices.reshape(n_dp, n_z, 2), ALL)
    row, flat, wide, cube = P(ALL, None), P(ALL), P(None, ALL), P(ALL, None, None)
    in_specs = (row, row, row, flat, flat, row, flat, flat, row, flat, flat, flat, cube, wide, cube, wide, row)
    out_specs = (row, row, flat, flat, row, flat, flat, row, flat, flat, flat, cube, wide, cube, wide)
    return jax.shard_map(
        functools.partial(shards, n_dp, n_z), mesh=split, in_specs=in_specs, out_specs=out_specs, check_vma=False
    )
```

```python
import functools

import jax
import jax.numpy as jnp
from jax import lax
from jax.experimental import pallas as pl
from jax.experimental.pallas import tpu as pltpu
from jax.sharding import Mesh, PartitionSpec as P

HEAD_DIM = 64
CAPACITY = 640
LONGEST = 512
PAIR = 2 * HEAD_DIM
TILE_Q = 256
MASKED = -1e30
epsilon = 1e-05
bf16 = jnp.bfloat16
f32 = jnp.float32
ALL = ("dp", "z", "c")
BLOCK = 256
FBLOCK = 512
NN = (((1,), (0,)), ((), ()))
NT = (((1,), (1,)), ((), ()))
TN = (((0,), (0,)), ((), ()))


def dot(a, b, dims=NN):
    return lax.dot_general(a, b, dims, preferred_element_type=f32)


def params(flops, moved, special=0):
    return dict(
        compiler_params=pltpu.CompilerParams(vmem_limit_bytes=58 << 20),
        cost_estimate=pl.CostEstimate(flops=2 * int(flops), bytes_accessed=int(moved), transcendentals=int(special)),
    )


def launch(kernel, name, grid, args, in_specs, out_specs, out_shape, scratch=(), scalars=(), after=(), work=(0, 0)):
    first, last = len(scalars) + len(args), len(scalars) + len(args) + len(after)

    def body(*refs):
        kernel(*refs[:first], *refs[last:])

    return pl.pallas_call(
        body,
        grid_spec=pltpu.PrefetchScalarGridSpec(
            num_scalar_prefetch=len(scalars),
            grid=grid,
            in_specs=[*in_specs, *[pl.BlockSpec(memory_space=pl.ANY)] * len(after)],
            out_specs=out_specs,
            scratch_shapes=list(scratch),
        ),
        out_shape=out_shape,
        **params(*work),
        name=name,
    )(*scalars, *args, *after)


def whole(*shape):
    return pl.BlockSpec(shape, lambda *_: (0,) * len(shape))


def shape_of(shape, dtype):
    return jax.ShapeDtypeStruct(shape, dtype)


def spans(rows):
    out = []
    for start in range(0, rows, TILE_Q):
        low = max(0, (start - LONGEST + 1) // TILE_Q * TILE_Q)
        out.append((start, low, start + TILE_Q))
    return out


def fill_bias(bias_refs, seg_col, seg_row, blocks):
    for bias, (start, low, high) in zip(bias_refs, blocks):
        shape = (high - low, TILE_Q)
        key = low + lax.broadcasted_iota(jnp.int32, shape, 0)
        query = start + lax.broadcasted_iota(jnp.int32, shape, 1)
        same = seg_col[low:high, :] == seg_row[:, start : start + TILE_Q]
        bias[...] = jnp.where((key <= query) & same, 0.0, MASKED)


def forward_kernel(blocks, seg_col, seg_row, q_ref, k_ref, v_ref, o_ref, lse_ref, *bias):
    @pl.when(pl.program_id(0) == 0)
    def _():
        fill_bias(bias, seg_col, seg_row, blocks)

    lane = lax.broadcasted_iota(jnp.int32, (TILE_Q, PAIR), 1)
    work = [(block, head) for block in range(len(blocks)) for head in range(2)]

    def raw_scores(block, head):
        start, low, high = blocks[block]
        q = q_ref[start : start + TILE_Q, :] * jnp.asarray(HEAD_DIM**-0.5, bf16)
        mine = (lane < HEAD_DIM) == (head == 0)
        return dot(k_ref[low:high, :], jnp.where(mine, q, jnp.zeros_like(q)), NT)

    coming, heads = raw_scores(*work[0]), []
    for number, (block, head) in enumerate(work):
        start, low, high = blocks[block]
        rows = slice(start, start + TILE_Q)
        raw = coming
        if number + 1 < len(work):
            coming = raw_scores(*work[number + 1])
        scores = raw + bias[block][...]
        top = jnp.max(scores, 0, keepdims=True)
        probs = jnp.exp(scores - top)
        total = jnp.sum(probs, 0, keepdims=True)
        out = dot(v_ref[low:high, :], probs.astype(bf16), TN)
        heads.append(out[head * HEAD_DIM : (head + 1) * HEAD_DIM] * (1.0 / total))
        lse_ref[0, head : head + 1, rows] = top + jnp.log(total)
        if head == 1:
            o_ref[rows, :] = jnp.concatenate(heads, 0).T.astype(bf16)
            heads = []


def attention(qkv, seg_col, seg_row, after=()):
    rows, width = qkv.shape[0], qkv.shape[1] // 3
    pairs = width // PAIR
    blocks = spans(rows)
    return launch(
        functools.partial(forward_kernel, blocks),
        "attention_forward",
        (pairs,),
        (seg_col, seg_row, qkv, qkv, qkv),
        [
            whole(rows, 1),
            whole(1, rows),
            pl.BlockSpec((rows, PAIR), lambda p: (0, p)),
            pl.BlockSpec((rows, PAIR), lambda p: (0, pairs + p)),
            pl.BlockSpec((rows, PAIR), lambda p: (0, 2 * pairs + p)),
        ],
        (pl.BlockSpec((rows, PAIR), lambda p: (0, p)), pl.BlockSpec((1, 2, rows), lambda p: (p, 0, 0))),
        (shape_of((rows, width), bf16), shape_of((pairs, 2, rows), f32)),
        [pltpu.VMEM((high - low, TILE_Q), f32) for _, low, high in blocks],
        after=after,
        work=(16 * rows * rows * width, 8 * rows * width),
    )


def backward_kernel(
    blocks, first, seg_col, seg_row, q_ref, k_ref, v_ref, do_ref, lse_ref, d_ref, dk_sum, dv_sum, *bias
):
    @pl.when(pl.program_id(0) == 0)
    def _():
        fill_bias(bias, seg_col, seg_row, blocks)

    dk_sum[...] = jnp.zeros_like(dk_sum)
    dv_sum[...] = jnp.zeros_like(dv_sum)
    lane = lax.broadcasted_iota(jnp.int32, (TILE_Q, PAIR), 1)
    scale = HEAD_DIM**-0.5
    work = [(block, head) for block in range(len(blocks)) for head in range(2)]

    def products(block, head):
        start, low, high = blocks[block]
        rows = slice(start, start + TILE_Q)
        mine = (lane < HEAD_DIM) == (head == 0)
        zero = jnp.zeros((TILE_Q, PAIR), bf16)
        q = jnp.where(mine, q_ref[rows, :] * jnp.asarray(scale, bf16), zero)
        do = jnp.where(mine, do_ref[rows, :], zero)
        return q, do, dot(k_ref[low:high, :], q, NT), dot(v_ref[low:high, :], do, NT)

    coming, dq = products(*work[0]), []
    for number, (block, head) in enumerate(work):
        start, low, high = blocks[block]
        rows = slice(start, start + TILE_Q)
        q, do, raw, grad = coming
        if number + 1 < len(work):
            coming = products(*work[number + 1])
        probs = jnp.exp(raw + bias[block][...] - lse_ref[0, head : head + 1, rows])
        weighted = probs * grad
        total = jnp.sum(weighted, 0, keepdims=True)
        ds = (weighted - probs * total).astype(bf16)
        dv_sum[low:high, :] += dot(probs.astype(bf16), do)
        dk_sum[low:high, :] += dot(ds, q)
        dq.append(dot(k_ref[low:high, :], ds, TN)[head * HEAD_DIM : (head + 1) * HEAD_DIM] * scale)
        if head == 1:
            d_ref[0, rows, :] = jnp.concatenate(dq, 0).T.astype(bf16)
            dq = []
    d_ref[1, ...] = dk_sum[...].astype(bf16)
    d_ref[2, ...] = dv_sum[...].astype(bf16)


def attention_grad(qkv, do, lse, seg_col, seg_row, half, after=()):
    rows, width = qkv.shape[0], qkv.shape[1] // 3
    pairs = width // PAIR
    count = pairs // 2
    blocks = spans(rows)
    first = jnp.reshape(half * count, (1,)).astype(jnp.int32)
    return launch(
        functools.partial(backward_kernel, blocks),
        "attention_backward",
        (count,),
        (seg_col, seg_row, qkv, qkv, qkv, do, lse),
        [
            whole(rows, 1),
            whole(1, rows),
            pl.BlockSpec((rows, PAIR), lambda p, b: (0, b[0] + p)),
            pl.BlockSpec((rows, PAIR), lambda p, b: (0, pairs + b[0] + p)),
            pl.BlockSpec((rows, PAIR), lambda p, b: (0, 2 * pairs + b[0] + p)),
            pl.BlockSpec((rows, PAIR), lambda p, b: (0, b[0] + p)),
            pl.BlockSpec((1, 2, rows), lambda p, b: (b[0] + p, 0, 0)),
        ],
        pl.BlockSpec((3, rows, PAIR), lambda p, b: (0, 0, p)),
        shape_of((3, rows, count * PAIR), bf16),
        [pltpu.VMEM((rows, PAIR), f32)] * 2 + [pltpu.VMEM((high - low, TILE_Q), f32) for _, low, high in blocks],
        scalars=(first,),
        after=after,
        work=(12 * rows * rows * width, 8 * rows * width),
    )


def norm_parts(values):
    centre = values - jnp.mean(values, -1, keepdims=True)
    inverse = lax.rsqrt(jnp.mean(centre * centre, -1, keepdims=True) + epsilon)
    return centre * inverse, inverse


def norm_grad(normed, inverse, gain, grad):
    scaled = grad * gain
    return inverse * (
        scaled - jnp.mean(scaled, -1, keepdims=True) - normed * jnp.mean(scaled * normed, -1, keepdims=True)
    )


def add_rows(ref, value):
    @pl.when(pl.program_id(0) == 0)
    def _():
        ref[...] = value

    @pl.when(pl.program_id(0) > 0)
    def _():
        ref[...] += value


def sides(core, mine, other):
    return (mine, core[0]), (other, 1 - core[0])


def project_kernel(core, me, x_ref, gain, shift, bias, *refs):
    pieces, (a_ref, qkv_ref) = refs[:10], refs[10:]
    half = x_ref.shape[1] // 2
    normed, _ = norm_parts(x_ref[...].astype(f32))
    a_ref[...] = (normed * gain[...] + shift[...]).astype(bf16)
    depth = pieces[0].shape[0]
    for ws, side in sides(core, pieces[:5], pieces[5:]):
        first, second = 0.0, 0.0
        for r in range(4):
            a = a_ref[:, pl.ds(pl.multiple_of((me[0] ^ r) * depth, depth), depth)]
            first = first + dot(a, ws[r][:, : 2 * half])
            second = second + dot(a, ws[4][...] if r == 3 else ws[r][:, 2 * half :])
        for j, out in enumerate((first[:, :half], first[:, half:], second)):
            at = pl.ds(pl.multiple_of(2 * half * j + half * side, half), half)
            qkv_ref[:, at] = (out + bias[:, at]).astype(bf16)


def project(core, me, x, gain, shift, bias, mine_w, other_w, after=()):
    rows, width = x.shape
    depth = mine_w[0].shape[0]
    weight = [whole(depth, 3 * width // 2)] * 3 + [whole(depth, width), whole(depth, width // 2)]
    return launch(
        project_kernel,
        "project",
        (rows // BLOCK,),
        (x, gain, shift, bias, *mine_w, *other_w),
        [
            pl.BlockSpec((BLOCK, width), lambda i, c, m: (i, 0)),
            whole(1, width),
            whole(1, width),
            whole(1, 3 * width),
            *weight,
            *weight,
        ],
        (
            pl.BlockSpec((BLOCK, width), lambda i, c, m: (i, 0)),
            pl.BlockSpec((BLOCK, 3 * width), lambda i, c, m: (i, 0)),
        ),
        (shape_of((rows, width), bf16), shape_of((rows, 3 * width), bf16)),
        scalars=(core, me),
        after=after,
        work=(6 * rows * width * width, 6 * width * width + 10 * rows * width),
    )


def send_slots(acc, slot, values, keep_ref, away_ref):
    step = pl.program_id(0)
    chosen = lax.broadcasted_iota(jnp.int32, (2 * CAPACITY, BLOCK), 0) == slot[...]
    part = dot(chosen.astype(bf16), values)

    @pl.when(step == 0)
    def _():
        acc[...] = part

    @pl.when(step > 0)
    def _():
        acc[...] += part

    @pl.when(step == pl.num_programs(0) - 1)
    def _():
        keep_ref[...] = acc[:CAPACITY, :].astype(bf16)
        away_ref[...] = acc[CAPACITY:, :].astype(bf16)


def dispatch_kernel(slot, g_ref, keep_ref, away_ref, acc):
    send_slots(acc, slot, g_ref[...], keep_ref, away_ref)


def dispatch(slot_row, values, after=()):
    rows, width = values.shape
    return launch(
        dispatch_kernel,
        "dispatch",
        (rows // BLOCK,),
        (slot_row, values),
        [pl.BlockSpec((1, BLOCK), lambda i: (0, i)), pl.BlockSpec((BLOCK, width), lambda i: (i, 0))],
        (whole(CAPACITY, width),) * 2,
        (shape_of((CAPACITY, width), bf16),) * 2,
        [pltpu.VMEM((2 * CAPACITY, width), f32)],
        after=after,
        work=(4 * CAPACITY * rows * width, 2 * rows * width + 4 * CAPACITY * width),
    )


def middle_kernel(core, me, slot, x_ref, o_ref, *refs):
    pieces, (bias, gain, shift, mid_ref, keep_ref, away_ref, acc) = refs[:8], refs[8:]
    half = x_ref.shape[1] // 2
    depth = pieces[0].shape[0]
    for ws, side in sides(core, pieces[:4], pieces[4:]):
        at = pl.ds(pl.multiple_of(half * side, half), half)
        out = x_ref[:, at].astype(f32) + bias[:, at]
        for r, w in enumerate(ws):
            out = out + dot(o_ref[:, pl.ds(pl.multiple_of((me[0] ^ r) * depth, depth), depth)], w[...])
        mid_ref[:, at] = out
    normed, _ = norm_parts(mid_ref[...])
    send_slots(acc, slot, (normed * gain[...] + shift[...]).astype(bf16), keep_ref, away_ref)


def out_half(width):
    return pl.BlockSpec((width, width // 2), lambda *_: (0, 3))


def middle_part(core, me, slot_row, x, attended, mine_w, other_w, bias, gain, shift, after=()):
    rows, width = x.shape
    block = pl.BlockSpec((BLOCK, width), lambda i, c, m: (i, 0))
    half, depth = width // 2, mine_w[0].shape[0]
    out_columns = [pl.BlockSpec((depth, half), lambda *_: (0, 3))] * 3 + [pl.BlockSpec((depth, half), lambda *_: (0, 1))]
    of = lambda w: (w[0], w[1], w[2], w[4])
    return launch(
        middle_kernel,
        "middle",
        (rows // BLOCK,),
        (slot_row, x, attended, *of(mine_w), *of(other_w), bias, gain, shift),
        [
            pl.BlockSpec((1, BLOCK), lambda i, c, m: (0, i)),
            block,
            block,
            *out_columns,
            *out_columns,
            whole(1, width),
            whole(1, width),
            whole(1, width),
        ],
        (block, whole(CAPACITY, width), whole(CAPACITY, width)),
        (shape_of((rows, width), f32),) + (shape_of((CAPACITY, width), bf16),) * 2,
        [pltpu.VMEM((2 * CAPACITY, width), f32)],
        scalars=(core, me),
        after=after,
        work=(4 * CAPACITY * rows * width + 2 * rows * width * width, 10 * rows * width + 4 * CAPACITY * width),
    )


def from_slots(slot, keep_ref, away_ref):
    chosen = lax.broadcasted_iota(jnp.int32, (BLOCK, 2 * CAPACITY), 1) == slot[...]
    chosen = chosen.astype(bf16)
    return dot(chosen[:, :CAPACITY], keep_ref[...]) + dot(chosen[:, CAPACITY:], away_ref[...])


def middle_grad_kernel(
    core, slot, keep_ref, away_ref, mid_ref, g_ref, mine_w, other_w, gain,
    dmid_ref, mine_ref, other_ref, do_ref, gain_ref, shift_ref, bias_ref, dproj_ref,
):
    half = mid_ref.shape[1] // 2
    grad = from_slots(slot, keep_ref, away_ref)
    normed, inverse = norm_parts(mid_ref[...])
    dmid = g_ref[...].astype(f32) + norm_grad(normed, inverse, gain[...], grad)
    dproj_ref[...] = dmid.astype(bf16)
    dmid_ref[...] = dmid
    back = 0.0
    for (w, side), part in zip(sides(core, mine_w, other_w), (mine_ref, other_ref)):
        part[...] = dproj_ref[:, pl.ds(pl.multiple_of(half * side, half), half)]
        back = back + dot(part[...], w[...], NT)
    do_ref[...] = back.astype(bf16)
    add_rows(gain_ref, jnp.sum(grad * normed, 0, keepdims=True))
    add_rows(shift_ref, jnp.sum(grad, 0, keepdims=True))
    add_rows(bias_ref, jnp.sum(dproj_ref[...].astype(f32), 0, keepdims=True))


def middle_grad(core, slot_col, keep, away, middle, g, mine_w, other_w, gain, after=()):
    rows, width = middle.shape
    block = pl.BlockSpec((BLOCK, width), lambda i, c: (i, 0))
    part = pl.BlockSpec((BLOCK, width // 2), lambda i, c: (i, 0))
    slots = whole(CAPACITY, width)
    row = whole(1, width)
    return launch(
        middle_grad_kernel,
        "middle_grad",
        (rows // BLOCK,),
        (slot_col, keep, away, middle, g, mine_w, other_w, gain),
        [pl.BlockSpec((BLOCK, 1), lambda i, c: (i, 0)), slots, slots, block, block]
        + [out_half(width), out_half(width), row],
        (block, part, part, block, row, row, row),
        (shape_of((rows, width), f32),)
        + (shape_of((rows, width // 2), bf16),) * 2
        + (shape_of((rows, width), bf16),)
        + (shape_of((1, width), f32),) * 3,
        [pltpu.VMEM((BLOCK, width), bf16)],
        scalars=(core,),
        after=after,
        work=(4 * CAPACITY * rows * width + 2 * rows * width * width, 16 * rows * width + 4 * CAPACITY * width),
    )


def output_kernel(slot, route, keep_ref, away_ref, mid_ref, bias, out_ref):
    token_bias = jnp.where(route[...] == 0, bias[0:1, :], bias[1:2, :])
    out_ref[...] = (mid_ref[...] + from_slots(slot, keep_ref, away_ref) + token_bias).astype(bf16)


def output(slot_col, route_col, keep, away, middle, bias, after=()):
    rows, width = middle.shape
    block = pl.BlockSpec((BLOCK, width), lambda i: (i, 0))
    column = pl.BlockSpec((BLOCK, 1), lambda i: (i, 0))
    return launch(
        output_kernel,
        "output",
        (rows // BLOCK,),
        (slot_col, route_col, keep, away, middle, bias),
        [column, column, whole(CAPACITY, width), whole(CAPACITY, width), block, whole(2, width)],
        block,
        shape_of((rows, width), bf16),
        after=after,
        work=(4 * CAPACITY * rows * width, 6 * rows * width + 4 * CAPACITY * width),
    )


def input_grad_kernel(
    mine_ref, away_ref, x_ref, dmid_ref, mine_w, other_w, gain, out_ref, gain_ref, shift_ref, bias_ref
):
    half = mine_ref.shape[2]
    grad = 0.0
    for ref, w in ((mine_ref, mine_w), (away_ref, other_w)):
        for j in range(3):
            grad = grad + dot(ref[j], w[:, half * j : half * (j + 1)], NT)
    normed, inverse = norm_parts(x_ref[...].astype(f32))
    out_ref[...] = dmid_ref[...] + norm_grad(normed, inverse, gain[...], grad)
    add_rows(gain_ref, jnp.sum(grad * normed, 0, keepdims=True))
    add_rows(shift_ref, jnp.sum(grad, 0, keepdims=True))
    rows = [jnp.sum(ref[j].astype(f32), 0, keepdims=True) for j in (0, 2) for ref in (mine_ref, away_ref)]
    add_rows(bias_ref, jnp.concatenate(rows, 0))


def input_grads(mine, away, x, dmid, mine_w, other_w, gain, after=()):
    rows, width = x.shape
    half = width // 2
    block = pl.BlockSpec((BLOCK, width), lambda i: (i, 0))
    part = pl.BlockSpec((3, BLOCK, half), lambda i: (0, i, 0))
    row, weight = whole(1, width), whole(width, 3 * half)
    return launch(
        input_grad_kernel,
        "input_grad",
        (rows // BLOCK,),
        (mine, away, x, dmid, mine_w, other_w, gain),
        [part, part, block, block, weight, weight, row],
        (block, row, row, whole(4, half)),
        (
            shape_of((rows, width), f32),
            shape_of((1, width), f32),
            shape_of((1, width), f32),
            shape_of((4, half), f32),
        ),
        after=after,
        work=(6 * rows * width * width, 16 * rows * width + 6 * width * width),
    )


def two_sum_kernel(at, n_dp, me, a1, b1, a2, b2, out_ref, far_x, far_y, t1, t2):
    step = pl.program_id(0)

    @pl.when(step == 0)
    def _():
        t1[...] = a1[...].T
        t2[...] = a2[...].T

    out_ref[...] = (dot(t1[...], b1[0]) + dot(t2[...], b2[0])).astype(bf16)
    rows = out_ref.shape[0] // n_dp
    far = pl.ds(pl.multiple_of((me[0] ^ (n_dp - 1)) * rows, rows), rows)

    @pl.when(step + at < 2)
    def _():
        far_x[...] = out_ref[far, :]

    @pl.when(step + at >= 2)
    def _():
        far_y[...] = out_ref[far, :]


def two_sum(me, n_dp, a1, b1, a2, b2, at, into=(), after=()):
    rows, width = a1.shape
    parts, _, columns = b1.shape
    left, right = whole(rows, width), pl.BlockSpec((1, rows, columns), lambda j, m: (j, 0, 0))
    count = 5 + len(into)

    def body(*refs):
        two_sum_kernel(at, n_dp, *refs[:5], *refs[count + len(after) :])

    far = (width // n_dp, columns)
    return pl.pallas_call(
        body,
        grid_spec=pltpu.PrefetchScalarGridSpec(
            num_scalar_prefetch=1,
            grid=(parts,),
            in_specs=[left, right, left, right] + [pl.BlockSpec(memory_space=pl.ANY)] * (len(into) + len(after)),
            out_specs=(
                pl.BlockSpec((width, columns), lambda j, m: (0, at + j)),
                pl.BlockSpec(far, lambda j, m: (0, jnp.minimum(at + j, 1))),
                pl.BlockSpec(far, lambda j, m: (0, jnp.maximum(at + j - 2, 0))),
            ),
            scratch_shapes=[pltpu.VMEM((width, rows), bf16)] * 2,
        ),
        out_shape=(
            shape_of((width, 4 * columns), bf16),
            shape_of((width // n_dp, 2 * columns), bf16),
            shape_of((width // n_dp, 2 * columns), bf16),
        ),
        input_output_aliases={5 + i: i for i in range(len(into))},
        **params(4 * rows * width * columns * parts, 4 * rows * (width + parts * columns)),
        name="two_sum",
    )(me, a1, b1, a2, b2, *into, *after)


def up_kernel(me, xk, xr, bias, w0, w1, w2, w3a, w3b, act_ref, slope_ref):
    step = pl.program_id(0)
    depth = w0.shape[0]
    far = jnp.where(step < pl.num_programs(0) // 2, w3a[...], w3b[...])
    root = 0.7978845608028654
    for part, x in enumerate((xk, xr)):
        inner = bias[...]
        for r, w in enumerate((w0[...], w1[...], w2[...], far)):
            at = pl.multiple_of((me[0] ^ r) * depth, depth)
            inner = inner + dot(x[:, pl.ds(at, depth)], w)
        square = inner * inner
        bent = jnp.tanh(inner * (root + (root * 0.044715) * square))
        rise = 0.5 + 0.5 * bent
        act = (inner * rise).astype(bf16)
        slope = rise + inner * rise * (1.0 - bent) * (root + (root * 3 * 0.044715) * square)
        rows = slice(part * x.shape[0], (part + 1) * x.shape[0])
        act_ref[rows, :] = act
        slope_ref[rows, :] = slope.astype(bf16)


def up(me, xk, xr, bias, pieces, after=()):
    slots, width = xk.shape
    depth, hidden = pieces[0].shape
    steps = hidden // FBLOCK
    last = steps // 2 - 1
    tokens = whole(slots, width)
    weight = pl.BlockSpec((depth, FBLOCK), lambda i, m: (0, i))
    return launch(
        up_kernel,
        "experts_up",
        (steps,),
        (xk, xr, bias, *pieces),
        [tokens] * 2
        + [pl.BlockSpec((1, FBLOCK), lambda i, m: (0, i))]
        + [weight] * 3
        + [
            pl.BlockSpec((depth, FBLOCK), lambda i, m: (0, jnp.minimum(i, last))),
            pl.BlockSpec((depth, FBLOCK), lambda i, m: (0, jnp.maximum(i - last - 1, 0))),
        ],
        (
            pl.BlockSpec((2 * slots, FBLOCK), lambda i, m: (0, i)),
            pl.BlockSpec((2 * slots, FBLOCK), lambda i, m: (0, i)),
        ),
        (shape_of((2 * slots, hidden), bf16), shape_of((2 * slots, hidden), bf16)),
        scalars=(me,),
        after=after,
        work=(4 * slots * width * hidden, 2 * width * hidden + 8 * slots * hidden),
    )


def outer_kernel(act_ref, gk, gr, out_ref, bias_ref, g):
    @pl.when(pl.program_id(0) == 0)
    def _():
        half = gk.shape[0]
        g[:half, :] = gk[...]
        g[half:, :] = gr[...]
        bias_ref[...] = jnp.sum(g[...].astype(f32), 0, keepdims=True)

    out_ref[...] = dot(act_ref[...], g[...], TN).astype(bf16)


def outer(act, gk, gr, after=()):
    slots, width = gk.shape
    hidden = act.shape[1]
    return launch(
        outer_kernel,
        "experts_outer",
        (hidden // FBLOCK,),
        (act, gk, gr),
        [pl.BlockSpec((2 * slots, FBLOCK), lambda i: (0, i)), whole(slots, width), whole(slots, width)],
        (pl.BlockSpec((FBLOCK, width), lambda i: (i, 0)), whole(1, width)),
        (shape_of((hidden, width), bf16), shape_of((1, width), f32)),
        [pltpu.VMEM((2 * slots, width), bf16)],
        after=after,
        work=(4 * slots * width * hidden, 2 * width * hidden + 4 * slots * hidden),
    )


def hold_block(held, per, pieces, right):
    w0, w1, w2, w3a, w3b = pieces
    which = pl.program_id(0) // per
    half = held.shape[1] // 2
    for r, w in enumerate((w0, w1, w2)):

        @pl.when(which == r)
        def _(w=w):
            held[:, :half] = w[...]

    @pl.when(which == 3)
    def _():
        held[:, : half // 2] = w3a[...]
        held[:, half // 2 : half] = w3b[...]

    held[:, half:] = right[...].reshape(held.shape[0], half)


def down_grad_kernel(
    me, per, gk, gr, xk, xr, slope_ref, u0, u1, u2, u3a, u3b, w0, w1, w2, w3a, w3b, right,
    dk_ref, dr_ref, up_ref, far_x, far_y, bias_ref, held, acc, g, t,
):
    step = pl.program_id(0)
    slots = gk.shape[0]
    hold_block(held, per, (w0, w1, w2, w3a, w3b), right)

    @pl.when(step == 0)
    def _():
        g[:slots, :] = gk[...]
        g[slots:, :] = gr[...]
        t[:, :slots] = xk[...].T
        t[:, slots:] = xr[...].T
        acc[...] = jnp.zeros_like(acc)

    depth = u0.shape[0]
    early = (me[0] ^ (step // per)) * per + step % per < pl.num_programs(0) // 2
    u3 = jnp.where(early, u3a[...], u3b[...])
    inner = (dot(g[...], held[...], NT) * slope_ref[...].astype(f32)).astype(bf16)
    bias_ref[...] = jnp.sum(inner.astype(f32), 0, keepdims=True)
    up_ref[...] = dot(t[...], inner).astype(bf16)
    far = up_ref[pl.ds(pl.multiple_of((me[0] ^ 3) * depth, depth), depth), :]

    @pl.when(early)
    def _():
        far_x[...] = far

    @pl.when(jnp.logical_not(early))
    def _():
        far_y[...] = far

    for r, u in enumerate((u0[...], u1[...], u2[...], u3)):
        at = pl.multiple_of((me[0] ^ r) * depth, depth)
        acc[:, pl.ds(at, depth)] += dot(inner, u, NT)

    @pl.when(step == pl.num_programs(0) - 1)
    def _():
        dk_ref[...] = acc[:slots, :].astype(bf16)
        dr_ref[...] = acc[slots:, :].astype(bf16)


def second_specs(pieces, right):
    per = pieces[0].shape[0] // FBLOCK
    _, _, rows, half = right.shape

    def spec(r, columns):
        return pl.BlockSpec((FBLOCK, columns), lambda i, m: (jnp.clip(i - r * per, 0, per - 1), 0))

    return [spec(0, half), spec(1, half), spec(2, half), spec(3, half // 2), spec(3, half // 2)] + [
        pl.BlockSpec((FBLOCK // rows, 1, rows, half), lambda i, m: (i % per, m[0] ^ (i // per), 0, 0))
    ]


def down_grad(me, gk, gr, xk, xr, slope, up_pieces, down_pieces, right, after=()):
    slots, width = xk.shape
    depth, hidden = up_pieces[0].shape
    per = down_pieces[0].shape[0] // FBLOCK
    steps = hidden // FBLOCK
    half = steps // 2
    at = lambda i, m: (m[0] ^ (i // per)) * per + i % per

    def far(first):
        def block(i, m):
            low = jnp.where((m[0] < 2) == first, 0, half)
            return 0, at(jnp.clip(i, low, low + half - 1), m) - (0 if first else half)

        return pl.BlockSpec((depth, FBLOCK), block)

    tokens = whole(slots, width)
    weight = pl.BlockSpec((depth, FBLOCK), lambda i, m: (0, at(i, m)))
    return launch(
        lambda me, *refs: down_grad_kernel(me, per, *refs),
        "experts_grad",
        (steps,),
        (gk, gr, xk, xr, slope, *up_pieces, *down_pieces, right),
        [tokens] * 4
        + [pl.BlockSpec((2 * slots, FBLOCK), lambda i, m: (0, at(i, m)))]
        + [weight] * 3
        + [
            pl.BlockSpec((depth, FBLOCK), lambda i, m: (0, jnp.minimum(at(i, m), half - 1))),
            pl.BlockSpec((depth, FBLOCK), lambda i, m: (0, jnp.maximum(at(i, m) - half, 0))),
        ]
        + second_specs(down_pieces, right),
        (
            tokens,
            tokens,
            pl.BlockSpec((width, FBLOCK), lambda i, m: (0, at(i, m))),
            far(True),
            far(False),
            pl.BlockSpec((1, FBLOCK), lambda i, m: (0, at(i, m))),
        ),
        (
            shape_of((slots, width), bf16),
            shape_of((slots, width), bf16),
            shape_of((width, hidden), bf16),
            shape_of((depth, hidden // 2), bf16),
            shape_of((depth, hidden // 2), bf16),
            shape_of((1, hidden), f32),
        ),
        [
            pltpu.VMEM((FBLOCK, width), bf16),
            pltpu.VMEM((2 * slots, width), f32),
            pltpu.VMEM((2 * slots, width), bf16),
            pltpu.VMEM((width, 2 * slots), bf16),
        ],
        scalars=(me,),
        after=after,
        work=(12 * slots * width * hidden, 6 * width * hidden + 4 * slots * hidden),
    )


def down_kernel(me, per, act_ref, w0, w1, w2, w3a, w3b, right, keep_ref, away_ref, held, acc):
    hold_block(held, per, (w0, w1, w2, w3a, w3b), right)
    part = dot(act_ref[...], held[...])

    @pl.when(pl.program_id(0) == 0)
    def _():
        acc[...] = part

    @pl.when(pl.program_id(0) > 0)
    def _():
        acc[...] += part

    @pl.when(pl.program_id(0) == pl.num_programs(0) - 1)
    def _():
        slots = keep_ref.shape[0]
        keep_ref[...] = acc[:slots, :].astype(bf16)
        away_ref[...] = acc[slots:, :].astype(bf16)


def down(me, act, pieces, right, after=()):
    slots, hidden = act.shape
    width = 2 * right.shape[3]
    per = pieces[0].shape[0] // FBLOCK
    return launch(
        lambda me, *refs: down_kernel(me, per, *refs),
        "experts_down",
        (hidden // FBLOCK,),
        (act, *pieces, right),
        [pl.BlockSpec((slots, FBLOCK), lambda i, m: (0, (m[0] ^ (i // per)) * per + i % per))]
        + second_specs(pieces, right),
        (whole(slots // 2, width),) * 2,
        (shape_of((slots // 2, width), bf16),) * 2,
        [pltpu.VMEM((FBLOCK, width), bf16), pltpu.VMEM((slots, width), f32)],
        scalars=(me,),
        after=after,
        work=(2 * slots * width * hidden, 2 * width * hidden + 2 * slots * hidden),
    )


def place_kernel(at, *refs):
    out_ref = refs[-1]
    for r, piece in enumerate(refs[: 4 if len(refs) == 6 else -1]):

        @pl.when(pl.program_id(0) == r)
        def _(r=r, piece=piece):
            columns = piece.shape[1]
            out_ref[0, :, :columns] = piece[...]
            if columns < out_ref.shape[2]:
                out_ref[0, :, columns:] = refs[r + 1][...]


def place(at, pieces, after=()):
    rows, columns = pieces[0].shape
    count = sum(p.shape[1] for p in pieces) // columns
    return launch(
        place_kernel,
        "place",
        (count,),
        pieces,
        [whole(*p.shape) for p in pieces],
        pl.BlockSpec((1, rows, columns), lambda r, at: (at[0] ^ r, 0, 0)),
        shape_of((count, rows, columns), bf16),
        scalars=(at,),
        after=after,
        work=(0, 4 * count * rows * columns),
    ).reshape(count * rows, columns)


def pick(array, index, axis=0):
    return lax.dynamic_index_in_dim(array, index, axis, keepdims=False)


def swap(value, axis, size, mask):
    return lax.ppermute(value, axis, [(i, i ^ mask) for i in range(size)])


def swap_core(value):
    return swap(value, "c", 2, 1)


def by_core(core, mine, other, axis=0):
    return jnp.where(core == 0, jnp.stack([mine, other], axis), jnp.stack([other, mine], axis))


def add_kernel(me, part_x, part_y, by_x, by_y, next_x, next_y):
    first = pl.program_id(0) == 0
    more_x = jnp.where(first, 0.0, by_y[...].astype(f32))
    more_y = jnp.where(first, by_x[...].astype(f32), 0.0)
    next_x[...] = (part_x[0].astype(f32) + more_x).astype(bf16)
    next_y[...] = (part_y[0].astype(f32) + more_y).astype(bf16)


def scatter_next(me, partial, by_x, by_y, after=()):
    _, rows, columns = partial.shape
    half = columns // 2
    step = rows // 2
    block = lambda mask: pl.BlockSpec((1, step, half), lambda h, i, m: (m[0] ^ mask, i, h))
    next_x, next_y = launch(
        add_kernel,
        "far_add",
        (2, 2),
        (partial, partial, by_x, by_y),
        [
            block(1),
            block(2),
            pl.BlockSpec((step, half), lambda h, i, m: (jnp.where(h == 0, i, 1), 0)),
            pl.BlockSpec((step, half), lambda h, i, m: (jnp.where(h == 0, 0, i), 0)),
        ],
        (pl.BlockSpec((step, half), lambda h, i, m: (i, h)),) * 2,
        (shape_of((rows, columns), bf16),) * 2,
        scalars=(me,),
        after=after,
    )
    return next_x, next_y


def swap_near(x, y):
    return swap(x, "dp", 4, 1), swap(y, "dp", 4, 2)


def near_kernel(me, part, got_x, got_y, out_ref):
    out_ref[...] = (part[0].astype(f32) + got_x[...].astype(f32) + got_y[...].astype(f32)).astype(bf16)


def scatter_near(me, partial, got_x, got_y, after=()):
    _, rows, columns = partial.shape
    step = rows // 4
    block = pl.BlockSpec((step, columns), lambda i, m: (i, 0))
    return launch(
        near_kernel,
        "near_add",
        (4,),
        (partial, got_x, got_y),
        [pl.BlockSpec((1, step, columns), lambda i, m: (m[0], i, 0)), block, block],
        block,
        shape_of((rows, columns), bf16),
        scalars=(me,),
        after=after,
    )


def to_core(total):
    core = lax.axis_index("c")
    halves = total.reshape(2, total.shape[0] // 2, total.shape[1])
    return pick(halves, core), swap_core(pick(halves, 1 - core))


def gather_z(shard):
    return lax.all_gather(shard, "z", axis=0, tiled=True)


def scatter_z(block):
    return lax.psum_scatter(block, "z", scatter_dimension=0, tiled=True)


def later(value, after):
    def body(*refs):
        pass

    return pl.pallas_call(
        body,
        in_specs=[pl.BlockSpec(memory_space=pl.ANY)] * (1 + len(after)),
        out_specs=pl.BlockSpec(memory_space=pl.ANY),
        out_shape=shape_of(value.shape, value.dtype),
        input_output_aliases={0: 0},
        **params(0, 0),
        name="later",
    )(value, *after)


def halves_kernel(x_ref, y_ref, out_x, out_y, held_x, held_y, sems):
    half = out_x.shape[1]
    inward = [
        pltpu.make_async_copy(x_ref.at[:, :half], held_x, sems.at[0]),
        pltpu.make_async_copy(y_ref.at[:, half:], held_y, sems.at[1]),
    ]
    outward = [
        pltpu.make_async_copy(held_x, out_x, sems.at[2]),
        pltpu.make_async_copy(held_y, out_y, sems.at[3]),
    ]
    for copy in inward:
        copy.start()
    for arrived, copy in zip(inward, outward):
        arrived.wait()
        copy.start()
    for copy in outward:
        copy.wait()


def cut_halves(by_x, by_y, after=()):
    rows, columns = by_x.shape
    place = pl.BlockSpec(memory_space=pltpu.HBM)
    return launch(
        halves_kernel,
        "cut_halves",
        (1,),
        (by_x, by_y),
        [place, place],
        (place, place),
        (shape_of((rows, columns // 2), bf16),) * 2,
        [pltpu.VMEM((rows, columns // 2), bf16)] * 2 + [pltpu.SemaphoreType.DMA((4,))],
        after=after,
    )


def gather_far(cut):
    return swap(cut[0], "dp", 4, 2), swap(cut[1], "dp", 4, 1)


def gather_pieces(own):
    full = lax.all_gather(own, "dp", axis=0, tiled=True)
    rows, columns = full.shape
    blocks = full.reshape(4, rows // 4, columns)
    return blocks[0], blocks[1], blocks[2], blocks[3, :, : columns // 2], blocks[3, :, columns // 2 :]


def finish_kernel(core, mine_ref, other_ref, out_ref, qkv_ref):
    half = out_ref.shape[1] // 2
    for value, side in ((mine_ref[0], core[0]), (other_ref[...], 1 - core[0])):
        value = value.astype(f32)
        out_ref[:, pl.ds(pl.multiple_of(half * side, half), half)] = value[:, :half]
        for j in range(3):
            at = pl.ds(pl.multiple_of(2 * half * j + half * side, half), half)
            qkv_ref[:, at] = value[:, half * (j + 1) : half * (j + 2)]


def finish(core, total):
    rows, columns = total.shape[0] // 2, total.shape[1]
    halves = total.reshape(2, rows, columns)
    other = swap_core(pick(halves, 1 - core[0]))
    return launch(
        finish_kernel,
        "finish",
        (1,),
        (halves, other),
        [pl.BlockSpec((1, rows, columns), lambda i, c: (c[0], 0, 0)), whole(rows, columns)],
        (whole(rows, columns // 2), whole(rows, 3 * columns // 2)),
        (shape_of((rows, columns // 2), f32), shape_of((rows, 3 * columns // 2), f32)),
        scalars=(core,),
    )


def shards(
    n_dp,
    n_z,
    tokens,
    segment_ids,
    expert_ids,
    ln1_gain,
    ln1_bias,
    qkv_weight,
    query_bias,
    value_bias,
    out_weight,
    out_bias,
    ln2_gain,
    ln2_bias,
    up_weight,
    up_bias,
    down_weight,
    down_bias,
    cotangent,
):
    rows, width = tokens.shape
    devices = n_dp * n_z * 2
    share = qkv_weight.shape[0]
    up_share = up_bias.shape[1]
    core = lax.axis_index("c")
    scalar = lambda v: jnp.reshape(v, (1,)).astype(jnp.int32)
    square = n_dp == 4 and n_z == 4
    me = scalar(lax.axis_index("dp") if square else 0)

    half = width // 2
    both_w = jnp.concatenate([qkv_weight, out_weight], 1).reshape(share, 4, 2, half)
    mine_w, other_w = (pick(both_w, side, 2).reshape(share, 4 * half) for side in (core, 1 - core))
    attn_shard = place(scalar(core), [mine_w, swap_core(other_w)])
    small = jnp.concatenate(
        [ln1_gain, ln1_bias, query_bias, value_bias, out_bias, ln2_gain, ln2_bias, up_bias.reshape(-1), down_bias.reshape(-1)]
    )
    small = jnp.broadcast_to(small, (devices, small.shape[0]))
    small = lax.all_to_all(small, ALL, 0, 0, tiled=True).astype(f32)
    gain_one, shift_one, bias_query, bias_value, bias_out, gain_two, shift_two = (
        small[:, i * share : (i + 1) * share].reshape(1, width) for i in range(7)
    )
    bias_up = small[:, 7 * share : 7 * share + 2 * up_share].reshape(devices, 2, up_share)
    bias_up = pick(bias_up, core, 1).reshape(1, -1)
    bias_down = small[:, 7 * share + 2 * up_share :].reshape(devices, 2, share)
    bias_down = jnp.swapaxes(bias_down, 0, 1).reshape(2, width)

    qkv_bias = jnp.concatenate([bias_query, jnp.zeros_like(bias_query), bias_value], 1)

    def expert_shard(weight, after):
        mine, other = pick(weight, core, 1), swap_core(pick(weight, 1 - core, 1))
        return place(scalar(core), [mine, other], after)

    route = expert_ids[:, 0]
    at = lax.iota(jnp.int32, rows)
    before = (route[:, None] == route[None, :]) & (at[None, :] < at[:, None])
    slot = jnp.sum(before.astype(jnp.int32), 1) + jnp.where(route == core, 0, CAPACITY)
    slot_row, slot_col = slot.reshape(1, rows), slot.reshape(rows, 1)

    right_shard = expert_shard(down_weight[:, :, half:], (attn_shard,))
    up_shard = expert_shard(up_weight, (right_shard,))
    up_own = gather_z(up_shard)
    if square:
        right_all = place(me, [right_shard] + [swap(right_shard, "dp", 4, mask) for mask in range(1, 4)], (up_shard,))
        attn_own = later(gather_z(attn_shard), (right_all,))
    else:
        attn_own = gather_z(attn_shard)
    grad_keep, grad_away = dispatch(slot_row, cotangent, (attn_own,))
    grad_got = swap_core(grad_away)
    down_shard = expert_shard(down_weight[:, :, :half], (grad_keep,))
    if square:
        right = lax.all_gather(right_all.reshape(4, -1, half), "z", axis=0)
        attn_near = swap_near(attn_own, attn_own)
        mine_p = (attn_own, *attn_near, *gather_far(cut_halves(*attn_near, (down_shard,))))
        up_near = swap_near(up_own, up_own)
    else:
        right = lax.all_gather(gather_z(right_shard), "dp", axis=0, tiled=True)
        right = jnp.swapaxes(right.reshape(4, 4, -1, half), 0, 1)
        mine_p = gather_pieces(attn_own)
    other_p = tuple(swap_core(piece) for piece in mine_p)

    side = scalar(core)
    normed_one, qkv = project(side, me, tokens, gain_one, shift_one, qkv_bias, mine_p, other_p, (up_own, grad_got, bias_out, gain_two, shift_two))
    other_normed_one = swap_core(normed_one)
    seg_row, seg_col = segment_ids, segment_ids.reshape(rows, 1)
    attended, lse = attention(qkv, seg_col, seg_row)
    other_attended = swap_core(attended)
    if square:
        up_cut = cut_halves(*up_near, (attended,))
        w_up = (up_own, *up_near, *gather_far(up_cut))
    else:
        up_cut, w_up = (), gather_pieces(up_own)
    middle, in_keep, in_away = middle_part(
        side, me, slot_row, tokens, attended, mine_p, other_p, bias_out, gain_two, shift_two, after=(*up_cut, other_normed_one)
    )
    mine_w = place(me, mine_p, (middle,))
    other_w = place(me, other_p, (mine_w,))
    down_own = later(gather_z(down_shard), (middle,))
    in_got = swap_core(later(in_away, (*w_up[3:], down_own, other_w)))

    if square:
        down_near_got = swap_near(down_own, down_own)
    act, slope = up(me, in_keep, in_got, bias_up, w_up)
    if square:
        down_cut = cut_halves(*down_near_got, (act,))
        w_down = (down_own, *down_near_got, *gather_far(down_cut))
    else:
        down_cut, w_down = (), gather_pieces(down_own)
    down_partial, down_bias_grad = outer(act, grad_keep, grad_got, (*down_cut, right))
    down_half = lax.psum_scatter(later(down_partial, w_down[3:]), "dp", scatter_dimension=0, tiled=True)
    back_keep, back_away, up_partial, up_out_x, up_out_y, up_bias_grad = down_grad(
        me, grad_keep, grad_got, in_keep, in_got, slope, w_up, w_down, right, after=(other_w,)
    )
    back_got = swap_core(back_away)
    if square:
        up_partial = up_partial.reshape(4, width // 4, -1)
        up_far = swap_near(up_out_x, up_out_y)

    middle_grads, mine_projected, other_projected, attended_grad, gain_two_grad, shift_two_grad, out_bias_grad = (
        middle_grad(side, slot_col, back_keep, back_got, middle, cotangent, mine_w, other_w, gain_two)
    )
    other_projected = swap_core(other_projected)
    qkv_away = attention_grad(qkv, attended_grad, lse, seg_col, seg_row, 1 - core)
    qkv_got = swap_core(qkv_away)
    up_next = scatter_next(me, up_partial, *up_far, after=(qkv_away,)) if square else ()
    partial = two_sum(
        me, 4, attended, mine_projected[None], other_attended, other_projected[None], 0, after=up_next
    )
    down_total = scatter_z(later(down_half, up_next))
    y_keep, y_away = down(me, act, w_down, right, after=partial[:1])
    y_got = swap_core(y_away)
    qkv_kept = attention_grad(qkv, attended_grad, lse, seg_col, seg_row, core, after=(y_keep,))
    if square:
        up_block = scatter_near(me, up_partial, *swap_near(*up_next), after=(qkv_kept, down_total))
    else:
        up_block = lax.psum_scatter(up_partial, "dp", scatter_dimension=0, tiled=True)
    up_total = scatter_z(up_block)
    partial, out_x, out_y = two_sum(
        me, 4, normed_one, qkv_kept, other_normed_one, qkv_got, 1, into=partial, after=(up_block,)
    )
    if square:
        partial = partial.reshape(4, width // 4, -1)
        far = swap_near(out_x, out_y)
    block_out = output(slot_col, expert_ids, y_keep, y_got, middle, bias_down, after=(out_x,))
    near = scatter_next(me, partial, *far, after=(block_out,)) if square else ()
    input_grad, gain_one_grad, shift_one_grad, bias_sums = input_grads(
        qkv_kept, qkv_away, tokens, middle_grads, mine_w, other_w, gain_one, after=near
    )
    query_bias_grad = by_core(core, bias_sums[0], bias_sums[1])
    value_bias_grad = by_core(core, bias_sums[2], bias_sums[3])
    if square:
        last = scatter_near(me, partial, *swap_near(*near), after=(input_grad,))
    else:
        last = lax.psum_scatter(partial, "dp", scatter_dimension=0, tiled=True)

    vectors = [
        gain_one_grad,
        shift_one_grad,
        query_bias_grad,
        value_bias_grad,
        out_bias_grad,
        gain_two_grad,
        shift_two_grad,
        up_bias_grad,
        down_bias_grad,
    ]
    sent = later(jnp.concatenate([v.reshape(devices, -1) for v in vectors], 1), (last,))
    got = lax.all_to_all(sent, ALL, 0, 0, tiled=True).reshape(devices // 2, 2, -1)
    both = jnp.sum(got, 0)
    total = both[0] + both[1]
    sums = [total[i * share : (i + 1) * share] for i in range(7)]
    at = 7 * share
    up_bias_sum = both[:, at : at + up_share]
    down_bias_sum = both[:, at + up_share :]

    down_weight_grad = by_core(core, *to_core(down_total.astype(f32)), 1)
    up_weight_grad = by_core(core, *to_core(up_total.astype(f32)), 1)
    out_weight_grad, qkv_weight_grad = finish(side, later(scatter_z(last), (up_bias_sum, down_weight_grad, up_weight_grad)))
    return (
        block_out,
        input_grad,
        sums[0],
        sums[1],
        qkv_weight_grad,
        sums[2],
        sums[3],
        out_weight_grad,
        sums[4],
        sums[5],
        sums[6],
        up_weight_grad,
        up_bias_sum,
        down_weight_grad,
        down_bias_sum,
    )


def solution(mesh):
    n_dp, n_z = mesh.shape["dp"], mesh.shape["fsdp"] // 2
    split = Mesh(mesh.devices.reshape(n_dp, n_z, 2), ALL)
    row, flat, wide, cube = P(ALL, None), P(ALL), P(None, ALL), P(ALL, None, None)
    in_specs = (row, row, row, flat, flat, row, flat, flat, row, flat, flat, flat, cube, wide, cube, wide, row)
    out_specs = (row, row, flat, flat, row, flat, flat, row, flat, flat, flat, cube, wide, cube, wide)
    return jax.shard_map(
        functools.partial(shards, n_dp, n_z), mesh=split, in_specs=in_specs, out_specs=out_specs, check_vma=False
    )
```

```python
import functools

import jax
import jax.numpy as jnp
from jax import lax
from jax.experimental import pallas as pl
from jax.experimental.pallas import tpu as pltpu
from jax.sharding import Mesh, PartitionSpec as P

HEAD_DIM = 64
CAPACITY = 640
LONGEST = 512
PAIR = 2 * HEAD_DIM
TILE_Q = 256
MASKED = -1e30
epsilon = 1e-05
bf16 = jnp.bfloat16
f32 = jnp.float32
ALL = ("dp", "z", "c")
BLOCK = 256
FBLOCK = 512
NN = (((1,), (0,)), ((), ()))
NT = (((1,), (1,)), ((), ()))
TN = (((0,), (0,)), ((), ()))


def dot(a, b, dims=NN):
    return lax.dot_general(a, b, dims, preferred_element_type=f32)


def params(flops, moved, special=0):
    return dict(
        compiler_params=pltpu.CompilerParams(vmem_limit_bytes=58 << 20),
        cost_estimate=pl.CostEstimate(flops=2 * int(flops), bytes_accessed=int(moved), transcendentals=int(special)),
    )


def launch(kernel, name, grid, args, in_specs, out_specs, out_shape, scratch=(), scalars=(), after=(), work=(0, 0)):
    first, last = len(scalars) + len(args), len(scalars) + len(args) + len(after)

    def body(*refs):
        kernel(*refs[:first], *refs[last:])

    return pl.pallas_call(
        body,
        grid_spec=pltpu.PrefetchScalarGridSpec(
            num_scalar_prefetch=len(scalars),
            grid=grid,
            in_specs=[*in_specs, *[pl.BlockSpec(memory_space=pl.ANY)] * len(after)],
            out_specs=out_specs,
            scratch_shapes=list(scratch),
        ),
        out_shape=out_shape,
        **params(*work),
        name=name,
    )(*scalars, *args, *after)


def whole(*shape):
    return pl.BlockSpec(shape, lambda *_: (0,) * len(shape))


def shape_of(shape, dtype):
    return jax.ShapeDtypeStruct(shape, dtype)


def spans(rows):
    out = []
    for start in range(0, rows, TILE_Q):
        low = max(0, (start - LONGEST + 1) // TILE_Q * TILE_Q)
        out.append((start, low, start + TILE_Q))
    return out


def fill_bias(bias_refs, seg_col, seg_row, blocks):
    for bias, (start, low, high) in zip(bias_refs, blocks):
        shape = (high - low, TILE_Q)
        key = low + lax.broadcasted_iota(jnp.int32, shape, 0)
        query = start + lax.broadcasted_iota(jnp.int32, shape, 1)
        same = seg_col[low:high, :] == seg_row[:, start : start + TILE_Q]
        bias[...] = jnp.where((key <= query) & same, 0.0, MASKED)


def forward_kernel(blocks, seg_col, seg_row, q_ref, k_ref, v_ref, o_ref, lse_ref, *bias):
    @pl.when(pl.program_id(0) == 0)
    def _():
        fill_bias(bias, seg_col, seg_row, blocks)

    lane = lax.broadcasted_iota(jnp.int32, (TILE_Q, PAIR), 1)
    work = [(block, head) for block in range(len(blocks)) for head in range(2)]

    def raw_scores(block, head):
        start, low, high = blocks[block]
        q = q_ref[start : start + TILE_Q, :] * jnp.asarray(HEAD_DIM**-0.5, bf16)
        mine = (lane < HEAD_DIM) == (head == 0)
        return dot(k_ref[low:high, :], jnp.where(mine, q, jnp.zeros_like(q)), NT)

    coming, heads = raw_scores(*work[0]), []
    for number, (block, head) in enumerate(work):
        start, low, high = blocks[block]
        rows = slice(start, start + TILE_Q)
        raw = coming
        if number + 1 < len(work):
            coming = raw_scores(*work[number + 1])
        scores = raw + bias[block][...]
        top = jnp.max(scores, 0, keepdims=True)
        probs = jnp.exp(scores - top)
        total = jnp.sum(probs, 0, keepdims=True)
        out = dot(v_ref[low:high, :], probs.astype(bf16), TN)
        heads.append(out[head * HEAD_DIM : (head + 1) * HEAD_DIM] * (1.0 / total))
        lse_ref[0, head : head + 1, rows] = top + jnp.log(total)
        if head == 1:
            o_ref[rows, :] = jnp.concatenate(heads, 0).T.astype(bf16)
            heads = []


def attention(qkv, seg_col, seg_row, after=()):
    rows, width = qkv.shape[0], qkv.shape[1] // 3
    pairs = width // PAIR
    blocks = spans(rows)
    return launch(
        functools.partial(forward_kernel, blocks),
        "attention_forward",
        (pairs,),
        (seg_col, seg_row, qkv, qkv, qkv),
        [
            whole(rows, 1),
            whole(1, rows),
            pl.BlockSpec((rows, PAIR), lambda p: (0, p)),
            pl.BlockSpec((rows, PAIR), lambda p: (0, pairs + p)),
            pl.BlockSpec((rows, PAIR), lambda p: (0, 2 * pairs + p)),
        ],
        (pl.BlockSpec((rows, PAIR), lambda p: (0, p)), pl.BlockSpec((1, 2, rows), lambda p: (p, 0, 0))),
        (shape_of((rows, width), bf16), shape_of((pairs, 2, rows), f32)),
        [pltpu.VMEM((high - low, TILE_Q), f32) for _, low, high in blocks],
        after=after,
        work=(16 * rows * rows * width, 8 * rows * width),
    )


def backward_kernel(
    blocks, first, seg_col, seg_row, q_ref, k_ref, v_ref, do_ref, lse_ref, d_ref, dk_sum, dv_sum, *bias
):
    @pl.when(pl.program_id(0) == 0)
    def _():
        fill_bias(bias, seg_col, seg_row, blocks)

    dk_sum[...] = jnp.zeros_like(dk_sum)
    dv_sum[...] = jnp.zeros_like(dv_sum)
    lane = lax.broadcasted_iota(jnp.int32, (TILE_Q, PAIR), 1)
    scale = HEAD_DIM**-0.5
    work = [(block, head) for block in range(len(blocks)) for head in range(2)]

    def products(block, head):
        start, low, high = blocks[block]
        rows = slice(start, start + TILE_Q)
        mine = (lane < HEAD_DIM) == (head == 0)
        zero = jnp.zeros((TILE_Q, PAIR), bf16)
        q = jnp.where(mine, q_ref[rows, :] * jnp.asarray(scale, bf16), zero)
        do = jnp.where(mine, do_ref[rows, :], zero)
        return q, do, dot(k_ref[low:high, :], q, NT), dot(v_ref[low:high, :], do, NT)

    coming, dq = products(*work[0]), []
    for number, (block, head) in enumerate(work):
        start, low, high = blocks[block]
        rows = slice(start, start + TILE_Q)
        q, do, raw, grad = coming
        if number + 1 < len(work):
            coming = products(*work[number + 1])
        probs = jnp.exp(raw + bias[block][...] - lse_ref[0, head : head + 1, rows])
        weighted = probs * grad
        total = jnp.sum(weighted, 0, keepdims=True)
        ds = (weighted - probs * total).astype(bf16)
        dv_sum[low:high, :] += dot(probs.astype(bf16), do)
        dk_sum[low:high, :] += dot(ds, q)
        dq.append(dot(k_ref[low:high, :], ds, TN)[head * HEAD_DIM : (head + 1) * HEAD_DIM] * scale)
        if head == 1:
            d_ref[0, rows, :] = jnp.concatenate(dq, 0).T.astype(bf16)
            dq = []
    d_ref[1, ...] = dk_sum[...].astype(bf16)
    d_ref[2, ...] = dv_sum[...].astype(bf16)


def attention_grad(qkv, do, lse, seg_col, seg_row, half, after=()):
    rows, width = qkv.shape[0], qkv.shape[1] // 3
    pairs = width // PAIR
    count = pairs // 2
    blocks = spans(rows)
    first = jnp.reshape(half * count, (1,)).astype(jnp.int32)
    return launch(
        functools.partial(backward_kernel, blocks),
        "attention_backward",
        (count,),
        (seg_col, seg_row, qkv, qkv, qkv, do, lse),
        [
            whole(rows, 1),
            whole(1, rows),
            pl.BlockSpec((rows, PAIR), lambda p, b: (0, b[0] + p)),
            pl.BlockSpec((rows, PAIR), lambda p, b: (0, pairs + b[0] + p)),
            pl.BlockSpec((rows, PAIR), lambda p, b: (0, 2 * pairs + b[0] + p)),
            pl.BlockSpec((rows, PAIR), lambda p, b: (0, b[0] + p)),
            pl.BlockSpec((1, 2, rows), lambda p, b: (b[0] + p, 0, 0)),
        ],
        pl.BlockSpec((3, rows, PAIR), lambda p, b: (0, 0, p)),
        shape_of((3, rows, count * PAIR), bf16),
        [pltpu.VMEM((rows, PAIR), f32)] * 2 + [pltpu.VMEM((high - low, TILE_Q), f32) for _, low, high in blocks],
        scalars=(first,),
        after=after,
        work=(12 * rows * rows * width, 8 * rows * width),
    )


def norm_parts(values):
    centre = values - jnp.mean(values, -1, keepdims=True)
    inverse = lax.rsqrt(jnp.mean(centre * centre, -1, keepdims=True) + epsilon)
    return centre * inverse, inverse


def norm_grad(normed, inverse, gain, grad):
    scaled = grad * gain
    return inverse * (
        scaled - jnp.mean(scaled, -1, keepdims=True) - normed * jnp.mean(scaled * normed, -1, keepdims=True)
    )


def add_rows(ref, value):
    @pl.when(pl.program_id(0) == 0)
    def _():
        ref[...] = value

    @pl.when(pl.program_id(0) > 0)
    def _():
        ref[...] += value


def sides(core, mine, other):
    return (mine, core[0]), (other, 1 - core[0])


def project_kernel(core, me, x_ref, gain, shift, bias, *refs):
    pieces, (a_ref, qkv_ref) = refs[:10], refs[10:]
    half = x_ref.shape[1] // 2
    normed, _ = norm_parts(x_ref[...].astype(f32))
    a_ref[...] = (normed * gain[...] + shift[...]).astype(bf16)
    depth = pieces[0].shape[0]
    for ws, side in sides(core, pieces[:5], pieces[5:]):
        first, second = 0.0, 0.0
        for r in range(4):
            a = a_ref[:, pl.ds(pl.multiple_of((me[0] ^ r) * depth, depth), depth)]
            first = first + dot(a, ws[r][:, : 2 * half])
            second = second + dot(a, ws[4][...] if r == 3 else ws[r][:, 2 * half :])
        for j, out in enumerate((first[:, :half], first[:, half:], second)):
            at = pl.ds(pl.multiple_of(2 * half * j + half * side, half), half)
            qkv_ref[:, at] = (out + bias[:, at]).astype(bf16)


def project(core, me, x, gain, shift, bias, mine_w, other_w, after=()):
    rows, width = x.shape
    depth = mine_w[0].shape[0]
    weight = [whole(depth, 3 * width // 2)] * 3 + [whole(depth, width), whole(depth, width // 2)]
    return launch(
        project_kernel,
        "project",
        (rows // BLOCK,),
        (x, gain, shift, bias, *mine_w, *other_w),
        [
            pl.BlockSpec((BLOCK, width), lambda i, c, m: (i, 0)),
            whole(1, width),
            whole(1, width),
            whole(1, 3 * width),
            *weight,
            *weight,
        ],
        (
            pl.BlockSpec((BLOCK, width), lambda i, c, m: (i, 0)),
            pl.BlockSpec((BLOCK, 3 * width), lambda i, c, m: (i, 0)),
        ),
        (shape_of((rows, width), bf16), shape_of((rows, 3 * width), bf16)),
        scalars=(core, me),
        after=after,
        work=(6 * rows * width * width, 6 * width * width + 10 * rows * width),
    )


def send_slots(acc, slot, values, keep_ref, away_ref):
    step = pl.program_id(0)
    chosen = lax.broadcasted_iota(jnp.int32, (2 * CAPACITY, BLOCK), 0) == slot[...]
    part = dot(chosen.astype(bf16), values)

    @pl.when(step == 0)
    def _():
        acc[...] = part

    @pl.when(step > 0)
    def _():
        acc[...] += part

    @pl.when(step == pl.num_programs(0) - 1)
    def _():
        keep_ref[...] = acc[:CAPACITY, :].astype(bf16)
        away_ref[...] = acc[CAPACITY:, :].astype(bf16)


def dispatch_kernel(slot, g_ref, keep_ref, away_ref, acc):
    send_slots(acc, slot, g_ref[...], keep_ref, away_ref)


def dispatch(slot_row, values, after=()):
    rows, width = values.shape
    return launch(
        dispatch_kernel,
        "dispatch",
        (rows // BLOCK,),
        (slot_row, values),
        [pl.BlockSpec((1, BLOCK), lambda i: (0, i)), pl.BlockSpec((BLOCK, width), lambda i: (i, 0))],
        (whole(CAPACITY, width),) * 2,
        (shape_of((CAPACITY, width), bf16),) * 2,
        [pltpu.VMEM((2 * CAPACITY, width), f32)],
        after=after,
        work=(4 * CAPACITY * rows * width, 2 * rows * width + 4 * CAPACITY * width),
    )


def middle_kernel(core, me, slot, x_ref, o_ref, *refs):
    pieces, (bias, gain, shift, mid_ref, keep_ref, away_ref, acc) = refs[:8], refs[8:]
    half = x_ref.shape[1] // 2
    depth = pieces[0].shape[0]
    for ws, side in sides(core, pieces[:4], pieces[4:]):
        at = pl.ds(pl.multiple_of(half * side, half), half)
        out = x_ref[:, at].astype(f32) + bias[:, at]
        for r, w in enumerate(ws):
            out = out + dot(o_ref[:, pl.ds(pl.multiple_of((me[0] ^ r) * depth, depth), depth)], w[...])
        mid_ref[:, at] = out
    normed, _ = norm_parts(mid_ref[...])
    send_slots(acc, slot, (normed * gain[...] + shift[...]).astype(bf16), keep_ref, away_ref)


def out_half(width):
    return pl.BlockSpec((width, width // 2), lambda *_: (0, 3))


def middle_part(core, me, slot_row, x, attended, mine_w, other_w, bias, gain, shift, after=()):
    rows, width = x.shape
    block = pl.BlockSpec((BLOCK, width), lambda i, c, m: (i, 0))
    half, depth = width // 2, mine_w[0].shape[0]
    out_columns = [pl.BlockSpec((depth, half), lambda *_: (0, 3))] * 3 + [pl.BlockSpec((depth, half), lambda *_: (0, 1))]
    of = lambda w: (w[0], w[1], w[2], w[4])
    return launch(
        middle_kernel,
        "middle",
        (rows // BLOCK,),
        (slot_row, x, attended, *of(mine_w), *of(other_w), bias, gain, shift),
        [
            pl.BlockSpec((1, BLOCK), lambda i, c, m: (0, i)),
            block,
            block,
            *out_columns,
            *out_columns,
            whole(1, width),
            whole(1, width),
            whole(1, width),
        ],
        (block, whole(CAPACITY, width), whole(CAPACITY, width)),
        (shape_of((rows, width), f32),) + (shape_of((CAPACITY, width), bf16),) * 2,
        [pltpu.VMEM((2 * CAPACITY, width), f32)],
        scalars=(core, me),
        after=after,
        work=(4 * CAPACITY * rows * width + 2 * rows * width * width, 10 * rows * width + 4 * CAPACITY * width),
    )


def from_slots(slot, keep_ref, away_ref):
    chosen = lax.broadcasted_iota(jnp.int32, (BLOCK, 2 * CAPACITY), 1) == slot[...]
    chosen = chosen.astype(bf16)
    return dot(chosen[:, :CAPACITY], keep_ref[...]) + dot(chosen[:, CAPACITY:], away_ref[...])


def middle_grad_kernel(
    core, slot, keep_ref, away_ref, mid_ref, g_ref, mine_w, other_w, gain,
    dmid_ref, mine_ref, other_ref, do_ref, gain_ref, shift_ref, bias_ref, dproj_ref,
):
    half = mid_ref.shape[1] // 2
    grad = from_slots(slot, keep_ref, away_ref)
    normed, inverse = norm_parts(mid_ref[...])
    dmid = g_ref[...].astype(f32) + norm_grad(normed, inverse, gain[...], grad)
    dproj_ref[...] = dmid.astype(bf16)
    dmid_ref[...] = dmid
    back = 0.0
    for (w, side), part in zip(sides(core, mine_w, other_w), (mine_ref, other_ref)):
        part[...] = dproj_ref[:, pl.ds(pl.multiple_of(half * side, half), half)]
        back = back + dot(part[...], w[...], NT)
    do_ref[...] = back.astype(bf16)
    add_rows(gain_ref, jnp.sum(grad * normed, 0, keepdims=True))
    add_rows(shift_ref, jnp.sum(grad, 0, keepdims=True))
    add_rows(bias_ref, jnp.sum(dproj_ref[...].astype(f32), 0, keepdims=True))


def middle_grad(core, slot_col, keep, away, middle, g, mine_w, other_w, gain, after=()):
    rows, width = middle.shape
    block = pl.BlockSpec((BLOCK, width), lambda i, c: (i, 0))
    part = pl.BlockSpec((BLOCK, width // 2), lambda i, c: (i, 0))
    slots = whole(CAPACITY, width)
    row = whole(1, width)
    return launch(
        middle_grad_kernel,
        "middle_grad",
        (rows // BLOCK,),
        (slot_col, keep, away, middle, g, mine_w, other_w, gain),
        [pl.BlockSpec((BLOCK, 1), lambda i, c: (i, 0)), slots, slots, block, block]
        + [out_half(width), out_half(width), row],
        (block, part, part, block, row, row, row),
        (shape_of((rows, width), f32),)
        + (shape_of((rows, width // 2), bf16),) * 2
        + (shape_of((rows, width), bf16),)
        + (shape_of((1, width), f32),) * 3,
        [pltpu.VMEM((BLOCK, width), bf16)],
        scalars=(core,),
        after=after,
        work=(4 * CAPACITY * rows * width + 2 * rows * width * width, 16 * rows * width + 4 * CAPACITY * width),
    )


def output_kernel(slot, route, keep_ref, away_ref, mid_ref, bias, out_ref):
    token_bias = jnp.where(route[...] == 0, bias[0:1, :], bias[1:2, :])
    out_ref[...] = (mid_ref[...] + from_slots(slot, keep_ref, away_ref) + token_bias).astype(bf16)


def output(slot_col, route_col, keep, away, middle, bias, after=()):
    rows, width = middle.shape
    block = pl.BlockSpec((BLOCK, width), lambda i: (i, 0))
    column = pl.BlockSpec((BLOCK, 1), lambda i: (i, 0))
    return launch(
        output_kernel,
        "output",
        (rows // BLOCK,),
        (slot_col, route_col, keep, away, middle, bias),
        [column, column, whole(CAPACITY, width), whole(CAPACITY, width), block, whole(2, width)],
        block,
        shape_of((rows, width), bf16),
        after=after,
        work=(0, 2 * rows * width),
    )


def input_grad_kernel(
    mine_ref, away_ref, x_ref, dmid_ref, mine_w, other_w, gain, out_ref, gain_ref, shift_ref, bias_ref
):
    half = mine_ref.shape[2]
    grad = 0.0
    for ref, w in ((mine_ref, mine_w), (away_ref, other_w)):
        for j in range(3):
            grad = grad + dot(ref[j], w[:, half * j : half * (j + 1)], NT)
    normed, inverse = norm_parts(x_ref[...].astype(f32))
    out_ref[...] = dmid_ref[...] + norm_grad(normed, inverse, gain[...], grad)
    add_rows(gain_ref, jnp.sum(grad * normed, 0, keepdims=True))
    add_rows(shift_ref, jnp.sum(grad, 0, keepdims=True))
    rows = [jnp.sum(ref[j].astype(f32), 0, keepdims=True) for j in (0, 2) for ref in (mine_ref, away_ref)]
    add_rows(bias_ref, jnp.concatenate(rows, 0))


def input_grads(mine, away, x, dmid, mine_w, other_w, gain, after=()):
    rows, width = x.shape
    half = width // 2
    block = pl.BlockSpec((BLOCK, width), lambda i: (i, 0))
    part = pl.BlockSpec((3, BLOCK, half), lambda i: (0, i, 0))
    row, weight = whole(1, width), whole(width, 3 * half)
    return launch(
        input_grad_kernel,
        "input_grad",
        (rows // BLOCK,),
        (mine, away, x, dmid, mine_w, other_w, gain),
        [part, part, block, block, weight, weight, row],
        (block, row, row, whole(4, half)),
        (
            shape_of((rows, width), f32),
            shape_of((1, width), f32),
            shape_of((1, width), f32),
            shape_of((4, half), f32),
        ),
        after=after,
        work=(0, 2 * rows * width),
    )


def two_sum_kernel(at, n_dp, me, a1, b1, a2, b2, out_ref, far_x, far_y, t1, t2):
    step = pl.program_id(0)

    @pl.when(step == 0)
    def _():
        t1[...] = a1[...].T
        t2[...] = a2[...].T

    out_ref[...] = (dot(t1[...], b1[0]) + dot(t2[...], b2[0])).astype(bf16)
    rows = out_ref.shape[0] // n_dp
    far = pl.ds(pl.multiple_of((me[0] ^ (n_dp - 1)) * rows, rows), rows)

    @pl.when(step + at < 2)
    def _():
        far_x[...] = out_ref[far, :]

    @pl.when(step + at >= 2)
    def _():
        far_y[...] = out_ref[far, :]


def two_sum(me, n_dp, a1, b1, a2, b2, at, into=(), after=()):
    rows, width = a1.shape
    parts, _, columns = b1.shape
    left, right = whole(rows, width), pl.BlockSpec((1, rows, columns), lambda j, m: (j, 0, 0))
    count = 5 + len(into)

    def body(*refs):
        two_sum_kernel(at, n_dp, *refs[:5], *refs[count + len(after) :])

    far = (width // n_dp, columns)
    return pl.pallas_call(
        body,
        grid_spec=pltpu.PrefetchScalarGridSpec(
            num_scalar_prefetch=1,
            grid=(parts,),
            in_specs=[left, right, left, right] + [pl.BlockSpec(memory_space=pl.ANY)] * (len(into) + len(after)),
            out_specs=(
                pl.BlockSpec((width, columns), lambda j, m: (0, at + j)),
                pl.BlockSpec(far, lambda j, m: (0, jnp.minimum(at + j, 1))),
                pl.BlockSpec(far, lambda j, m: (0, jnp.maximum(at + j - 2, 0))),
            ),
            scratch_shapes=[pltpu.VMEM((width, rows), bf16)] * 2,
        ),
        out_shape=(
            shape_of((width, 4 * columns), bf16),
            shape_of((width // n_dp, 2 * columns), bf16),
            shape_of((width // n_dp, 2 * columns), bf16),
        ),
        input_output_aliases={5 + i: i for i in range(len(into))},
        **params(4 * rows * width * columns * parts, 4 * rows * (width + parts * columns)),
        name="two_sum",
    )(me, a1, b1, a2, b2, *into, *after)


def up_kernel(me, xk, xr, bias, w0, w1, w2, w3a, w3b, act_ref, slope_ref):
    step = pl.program_id(0)
    depth = w0.shape[0]
    far = jnp.where(step < pl.num_programs(0) // 2, w3a[...], w3b[...])
    root = 0.7978845608028654
    for part, x in enumerate((xk, xr)):
        inner = bias[...]
        for r, w in enumerate((w0[...], w1[...], w2[...], far)):
            at = pl.multiple_of((me[0] ^ r) * depth, depth)
            inner = inner + dot(x[:, pl.ds(at, depth)], w)
        square = inner * inner
        bent = jnp.tanh(inner * (root + (root * 0.044715) * square))
        rise = 0.5 + 0.5 * bent
        act = (inner * rise).astype(bf16)
        slope = rise + inner * rise * (1.0 - bent) * (root + (root * 3 * 0.044715) * square)
        rows = slice(part * x.shape[0], (part + 1) * x.shape[0])
        act_ref[rows, :] = act
        slope_ref[rows, :] = slope.astype(bf16)


def up(me, xk, xr, bias, pieces, after=()):
    slots, width = xk.shape
    depth, hidden = pieces[0].shape
    steps = hidden // FBLOCK
    last = steps // 2 - 1
    tokens = whole(slots, width)
    weight = pl.BlockSpec((depth, FBLOCK), lambda i, m: (0, i))
    return launch(
        up_kernel,
        "experts_up",
        (steps,),
        (xk, xr, bias, *pieces),
        [tokens] * 2
        + [pl.BlockSpec((1, FBLOCK), lambda i, m: (0, i))]
        + [weight] * 3
        + [
            pl.BlockSpec((depth, FBLOCK), lambda i, m: (0, jnp.minimum(i, last))),
            pl.BlockSpec((depth, FBLOCK), lambda i, m: (0, jnp.maximum(i - last - 1, 0))),
        ],
        (
            pl.BlockSpec((2 * slots, FBLOCK), lambda i, m: (0, i)),
            pl.BlockSpec((2 * slots, FBLOCK), lambda i, m: (0, i)),
        ),
        (shape_of((2 * slots, hidden), bf16), shape_of((2 * slots, hidden), bf16)),
        scalars=(me,),
        after=after,
        work=(4 * slots * width * hidden, 2 * width * hidden + 8 * slots * hidden),
    )


def outer_kernel(act_ref, gk, gr, out_ref, bias_ref, g):
    @pl.when(pl.program_id(0) == 0)
    def _():
        half = gk.shape[0]
        g[:half, :] = gk[...]
        g[half:, :] = gr[...]
        bias_ref[...] = jnp.sum(g[...].astype(f32), 0, keepdims=True)

    out_ref[...] = dot(act_ref[...], g[...], TN).astype(bf16)


def outer(act, gk, gr, after=()):
    slots, width = gk.shape
    hidden = act.shape[1]
    return launch(
        outer_kernel,
        "experts_outer",
        (hidden // FBLOCK,),
        (act, gk, gr),
        [pl.BlockSpec((2 * slots, FBLOCK), lambda i: (0, i)), whole(slots, width), whole(slots, width)],
        (pl.BlockSpec((FBLOCK, width), lambda i: (i, 0)), whole(1, width)),
        (shape_of((hidden, width), bf16), shape_of((1, width), f32)),
        [pltpu.VMEM((2 * slots, width), bf16)],
        after=after,
        work=(4 * slots * width * hidden, 2 * width * hidden + 4 * slots * hidden),
    )


def hold_block(held, per, pieces, right):
    w0, w1, w2, w3a, w3b = pieces
    which = pl.program_id(0) // per
    half = held.shape[1] // 2
    for r, w in enumerate((w0, w1, w2)):

        @pl.when(which == r)
        def _(w=w):
            held[:, :half] = w[...]

    @pl.when(which == 3)
    def _():
        held[:, : half // 2] = w3a[...]
        held[:, half // 2 : half] = w3b[...]

    held[:, half:] = right[...].reshape(held.shape[0], half)


def down_grad_kernel(
    me, per, gk, gr, xk, xr, slope_ref, u0, u1, u2, u3a, u3b, w0, w1, w2, w3a, w3b, right,
    dk_ref, dr_ref, up_ref, far_x, far_y, bias_ref, held, acc, g, t,
):
    step = pl.program_id(0)
    slots = gk.shape[0]
    hold_block(held, per, (w0, w1, w2, w3a, w3b), right)

    @pl.when(step == 0)
    def _():
        g[:slots, :] = gk[...]
        g[slots:, :] = gr[...]
        t[:, :slots] = xk[...].T
        t[:, slots:] = xr[...].T
        acc[...] = jnp.zeros_like(acc)

    depth = u0.shape[0]
    early = (me[0] ^ (step // per)) * per + step % per < pl.num_programs(0) // 2
    u3 = jnp.where(early, u3a[...], u3b[...])
    inner = (dot(g[...], held[...], NT) * slope_ref[...].astype(f32)).astype(bf16)
    bias_ref[...] = jnp.sum(inner.astype(f32), 0, keepdims=True)
    up_ref[...] = dot(t[...], inner).astype(bf16)
    far = up_ref[pl.ds(pl.multiple_of((me[0] ^ 3) * depth, depth), depth), :]

    @pl.when(early)
    def _():
        far_x[...] = far

    @pl.when(jnp.logical_not(early))
    def _():
        far_y[...] = far

    for r, u in enumerate((u0[...], u1[...], u2[...], u3)):
        at = pl.multiple_of((me[0] ^ r) * depth, depth)
        acc[:, pl.ds(at, depth)] += dot(inner, u, NT)

    @pl.when(step == pl.num_programs(0) - 1)
    def _():
        dk_ref[...] = acc[:slots, :].astype(bf16)
        dr_ref[...] = acc[slots:, :].astype(bf16)


def second_specs(pieces, right):
    per = pieces[0].shape[0] // FBLOCK
    _, _, rows, half = right.shape

    def spec(r, columns):
        return pl.BlockSpec((FBLOCK, columns), lambda i, m: (jnp.clip(i - r * per, 0, per - 1), 0))

    return [spec(0, half), spec(1, half), spec(2, half), spec(3, half // 2), spec(3, half // 2)] + [
        pl.BlockSpec((FBLOCK // rows, 1, rows, half), lambda i, m: (i % per, m[0] ^ (i // per), 0, 0))
    ]


def down_grad(me, gk, gr, xk, xr, slope, up_pieces, down_pieces, right, after=()):
    slots, width = xk.shape
    depth, hidden = up_pieces[0].shape
    per = down_pieces[0].shape[0] // FBLOCK
    steps = hidden // FBLOCK
    half = steps // 2
    at = lambda i, m: (m[0] ^ (i // per)) * per + i % per

    def far(first):
        def block(i, m):
            low = jnp.where((m[0] < 2) == first, 0, half)
            return 0, at(jnp.clip(i, low, low + half - 1), m) - (0 if first else half)

        return pl.BlockSpec((depth, FBLOCK), block)

    tokens = whole(slots, width)
    weight = pl.BlockSpec((depth, FBLOCK), lambda i, m: (0, at(i, m)))
    return launch(
        lambda me, *refs: down_grad_kernel(me, per, *refs),
        "experts_grad",
        (steps,),
        (gk, gr, xk, xr, slope, *up_pieces, *down_pieces, right),
        [tokens] * 4
        + [pl.BlockSpec((2 * slots, FBLOCK), lambda i, m: (0, at(i, m)))]
        + [weight] * 3
        + [
            pl.BlockSpec((depth, FBLOCK), lambda i, m: (0, jnp.minimum(at(i, m), half - 1))),
            pl.BlockSpec((depth, FBLOCK), lambda i, m: (0, jnp.maximum(at(i, m) - half, 0))),
        ]
        + second_specs(down_pieces, right),
        (
            tokens,
            tokens,
            pl.BlockSpec((width, FBLOCK), lambda i, m: (0, at(i, m))),
            far(True),
            far(False),
            pl.BlockSpec((1, FBLOCK), lambda i, m: (0, at(i, m))),
        ),
        (
            shape_of((slots, width), bf16),
            shape_of((slots, width), bf16),
            shape_of((width, hidden), bf16),
            shape_of((depth, hidden // 2), bf16),
            shape_of((depth, hidden // 2), bf16),
            shape_of((1, hidden), f32),
        ),
        [
            pltpu.VMEM((FBLOCK, width), bf16),
            pltpu.VMEM((2 * slots, width), f32),
            pltpu.VMEM((2 * slots, width), bf16),
            pltpu.VMEM((width, 2 * slots), bf16),
        ],
        scalars=(me,),
        after=after,
        work=(12 * slots * width * hidden, 6 * width * hidden + 4 * slots * hidden),
    )


def down_kernel(me, per, act_ref, w0, w1, w2, w3a, w3b, right, keep_ref, away_ref, held, acc):
    hold_block(held, per, (w0, w1, w2, w3a, w3b), right)
    part = dot(act_ref[...], held[...])

    @pl.when(pl.program_id(0) == 0)
    def _():
        acc[...] = part

    @pl.when(pl.program_id(0) > 0)
    def _():
        acc[...] += part

    @pl.when(pl.program_id(0) == pl.num_programs(0) - 1)
    def _():
        slots = keep_ref.shape[0]
        keep_ref[...] = acc[:slots, :].astype(bf16)
        away_ref[...] = acc[slots:, :].astype(bf16)


def down(me, act, pieces, right, after=()):
    slots, hidden = act.shape
    width = 2 * right.shape[3]
    per = pieces[0].shape[0] // FBLOCK
    return launch(
        lambda me, *refs: down_kernel(me, per, *refs),
        "experts_down",
        (hidden // FBLOCK,),
        (act, *pieces, right),
        [pl.BlockSpec((slots, FBLOCK), lambda i, m: (0, (m[0] ^ (i // per)) * per + i % per))]
        + second_specs(pieces, right),
        (whole(slots // 2, width),) * 2,
        (shape_of((slots // 2, width), bf16),) * 2,
        [pltpu.VMEM((FBLOCK, width), bf16), pltpu.VMEM((slots, width), f32)],
        scalars=(me,),
        after=after,
        work=(2 * slots * width * hidden, 2 * width * hidden + 2 * slots * hidden),
    )


def place_kernel(at, *refs):
    out_ref = refs[-1]
    for r, piece in enumerate(refs[: 4 if len(refs) == 6 else -1]):

        @pl.when(pl.program_id(0) == r)
        def _(r=r, piece=piece):
            columns = piece.shape[1]
            out_ref[0, :, :columns] = piece[...]
            if columns < out_ref.shape[2]:
                out_ref[0, :, columns:] = refs[r + 1][...]


def place(at, pieces, after=()):
    rows, columns = pieces[0].shape
    count = sum(p.shape[1] for p in pieces) // columns
    return launch(
        place_kernel,
        "place",
        (count,),
        pieces,
        [whole(*p.shape) for p in pieces],
        pl.BlockSpec((1, rows, columns), lambda r, at: (at[0] ^ r, 0, 0)),
        shape_of((count, rows, columns), bf16),
        scalars=(at,),
        after=after,
        work=(0, 4 * count * rows * columns),
    ).reshape(count * rows, columns)


def pick(array, index, axis=0):
    return lax.dynamic_index_in_dim(array, index, axis, keepdims=False)


def swap(value, axis, size, mask):
    return lax.ppermute(value, axis, [(i, i ^ mask) for i in range(size)])


def swap_core(value):
    return swap(value, "c", 2, 1)


def by_core(core, mine, other, axis=0):
    return jnp.where(core == 0, jnp.stack([mine, other], axis), jnp.stack([other, mine], axis))


def add_kernel(me, part_x, part_y, by_x, by_y, next_x, next_y):
    first = pl.program_id(0) == 0
    more_x = jnp.where(first, 0.0, by_y[...].astype(f32))
    more_y = jnp.where(first, by_x[...].astype(f32), 0.0)
    next_x[...] = (part_x[0].astype(f32) + more_x).astype(bf16)
    next_y[...] = (part_y[0].astype(f32) + more_y).astype(bf16)


def scatter_next(me, partial, by_x, by_y, after=()):
    _, rows, columns = partial.shape
    half = columns // 2
    step = rows // 2
    block = lambda mask: pl.BlockSpec((1, step, half), lambda h, i, m: (m[0] ^ mask, i, h))
    next_x, next_y = launch(
        add_kernel,
        "far_add",
        (2, 2),
        (partial, partial, by_x, by_y),
        [
            block(1),
            block(2),
            pl.BlockSpec((step, half), lambda h, i, m: (jnp.where(h == 0, i, 1), 0)),
            pl.BlockSpec((step, half), lambda h, i, m: (jnp.where(h == 0, 0, i), 0)),
        ],
        (pl.BlockSpec((step, half), lambda h, i, m: (i, h)),) * 2,
        (shape_of((rows, columns), bf16),) * 2,
        scalars=(me,),
        after=after,
    )
    return next_x, next_y


def swap_near(x, y):
    return swap(x, "dp", 4, 1), swap(y, "dp", 4, 2)


def near_kernel(me, part, got_x, got_y, out_ref):
    out_ref[...] = (part[0].astype(f32) + got_x[...].astype(f32) + got_y[...].astype(f32)).astype(bf16)


def scatter_near(me, partial, got_x, got_y, after=()):
    _, rows, columns = partial.shape
    step = rows // 4
    block = pl.BlockSpec((step, columns), lambda i, m: (i, 0))
    return launch(
        near_kernel,
        "near_add",
        (4,),
        (partial, got_x, got_y),
        [pl.BlockSpec((1, step, columns), lambda i, m: (m[0], i, 0)), block, block],
        block,
        shape_of((rows, columns), bf16),
        scalars=(me,),
        after=after,
    )


def pair_kernel(core, mine_ref, other_ref, out_ref):
    mine, other = mine_ref[0].astype(f32), other_ref[...].astype(f32)
    out_ref[:, 0, :] = jnp.where(core[0] == 0, mine, other)
    out_ref[:, 1, :] = jnp.where(core[0] == 0, other, mine)


def pair(core, total):
    rows, columns = total.shape[0] // 2, total.shape[1]
    halves = total.reshape(2, rows, columns)
    other = swap_core(pick(halves, 1 - core[0]))
    return launch(
        pair_kernel,
        "pair",
        (1,),
        (halves, other),
        [pl.BlockSpec((1, rows, columns), lambda i, c: (c[0], 0, 0)), whole(rows, columns)],
        whole(rows, 2, columns),
        shape_of((rows, 2, columns), f32),
        scalars=(core,),
        work=(0, 2 * rows * columns),
    )


def gather_z(shard):
    return lax.all_gather(shard, "z", axis=0, tiled=True)


def scatter_z(block):
    return lax.psum_scatter(block, "z", scatter_dimension=0, tiled=True)


def later(value, after):
    def body(*refs):
        pass

    return pl.pallas_call(
        body,
        in_specs=[pl.BlockSpec(memory_space=pl.ANY)] * (1 + len(after)),
        out_specs=pl.BlockSpec(memory_space=pl.ANY),
        out_shape=shape_of(value.shape, value.dtype),
        input_output_aliases={0: 0},
        **params(0, 0),
        name="later",
    )(value, *after)


def halves_kernel(x_ref, y_ref, out_x, out_y, held_x, held_y, sems):
    half = out_x.shape[1]
    inward = [
        pltpu.make_async_copy(x_ref.at[:, :half], held_x, sems.at[0]),
        pltpu.make_async_copy(y_ref.at[:, half:], held_y, sems.at[1]),
    ]
    outward = [
        pltpu.make_async_copy(held_x, out_x, sems.at[2]),
        pltpu.make_async_copy(held_y, out_y, sems.at[3]),
    ]
    for copy in inward:
        copy.start()
    for arrived, copy in zip(inward, outward):
        arrived.wait()
        copy.start()
    for copy in outward:
        copy.wait()


def cut_halves(by_x, by_y, after=()):
    rows, columns = by_x.shape
    place = pl.BlockSpec(memory_space=pltpu.HBM)
    return launch(
        halves_kernel,
        "cut_halves",
        (1,),
        (by_x, by_y),
        [place, place],
        (place, place),
        (shape_of((rows, columns // 2), bf16),) * 2,
        [pltpu.VMEM((rows, columns // 2), bf16)] * 2 + [pltpu.SemaphoreType.DMA((4,))],
        after=after,
    )


def gather_far(cut):
    return swap(cut[0], "dp", 4, 2), swap(cut[1], "dp", 4, 1)


def gather_pieces(own):
    full = lax.all_gather(own, "dp", axis=0, tiled=True)
    rows, columns = full.shape
    blocks = full.reshape(4, rows // 4, columns)
    return blocks[0], blocks[1], blocks[2], blocks[3, :, : columns // 2], blocks[3, :, columns // 2 :]


def finish_kernel(core, mine_ref, other_ref, out_ref, qkv_ref):
    half = out_ref.shape[1] // 2
    for value, side in ((mine_ref[0], core[0]), (other_ref[...], 1 - core[0])):
        value = value.astype(f32)
        out_ref[:, pl.ds(pl.multiple_of(half * side, half), half)] = value[:, :half]
        for j in range(3):
            at = pl.ds(pl.multiple_of(2 * half * j + half * side, half), half)
            qkv_ref[:, at] = value[:, half * (j + 1) : half * (j + 2)]


def finish(core, total):
    rows, columns = total.shape[0] // 2, total.shape[1]
    halves = total.reshape(2, rows, columns)
    other = swap_core(pick(halves, 1 - core[0]))
    return launch(
        finish_kernel,
        "finish",
        (1,),
        (halves, other),
        [pl.BlockSpec((1, rows, columns), lambda i, c: (c[0], 0, 0)), whole(rows, columns)],
        (whole(rows, columns // 2), whole(rows, 3 * columns // 2)),
        (shape_of((rows, columns // 2), f32), shape_of((rows, 3 * columns // 2), f32)),
        scalars=(core,),
    )


def shards(
    n_dp,
    n_z,
    tokens,
    segment_ids,
    expert_ids,
    ln1_gain,
    ln1_bias,
    qkv_weight,
    query_bias,
    value_bias,
    out_weight,
    out_bias,
    ln2_gain,
    ln2_bias,
    up_weight,
    up_bias,
    down_weight,
    down_bias,
    cotangent,
):
    rows, width = tokens.shape
    devices = n_dp * n_z * 2
    share = qkv_weight.shape[0]
    up_share = up_bias.shape[1]
    core = lax.axis_index("c")
    scalar = lambda v: jnp.reshape(v, (1,)).astype(jnp.int32)
    square = n_dp == 4 and n_z == 4
    me = scalar(lax.axis_index("dp") if square else 0)

    half = width // 2
    both_w = jnp.concatenate([qkv_weight, out_weight], 1).reshape(share, 4, 2, half)
    mine_w, other_w = (pick(both_w, side, 2).reshape(share, 4 * half) for side in (core, 1 - core))
    attn_shard = place(scalar(core), [mine_w, swap_core(other_w)])
    small = jnp.concatenate(
        [ln1_gain, ln1_bias, query_bias, value_bias, out_bias, ln2_gain, ln2_bias, up_bias.reshape(-1), down_bias.reshape(-1)]
    )
    small = jnp.broadcast_to(small, (devices, small.shape[0]))
    small = lax.all_to_all(small, ALL, 0, 0, tiled=True).astype(f32)
    gain_one, shift_one, bias_query, bias_value, bias_out, gain_two, shift_two = (
        small[:, i * share : (i + 1) * share].reshape(1, width) for i in range(7)
    )
    bias_up = small[:, 7 * share : 7 * share + 2 * up_share].reshape(devices, 2, up_share)
    bias_up = pick(bias_up, core, 1).reshape(1, -1)
    bias_down = small[:, 7 * share + 2 * up_share :].reshape(devices, 2, share)
    bias_down = jnp.swapaxes(bias_down, 0, 1).reshape(2, width)

    qkv_bias = jnp.concatenate([bias_query, jnp.zeros_like(bias_query), bias_value], 1)

    def expert_shard(weight, after):
        mine, other = pick(weight, core, 1), swap_core(pick(weight, 1 - core, 1))
        return place(scalar(core), [mine, other], after)

    route = expert_ids[:, 0]
    at = lax.iota(jnp.int32, rows)
    before = (route[:, None] == route[None, :]) & (at[None, :] < at[:, None])
    slot = jnp.sum(before.astype(jnp.int32), 1) + jnp.where(route == core, 0, CAPACITY)
    slot_row, slot_col = slot.reshape(1, rows), slot.reshape(rows, 1)

    right_shard = expert_shard(down_weight[:, :, half:], (attn_shard,))
    up_shard = expert_shard(up_weight, (right_shard,))
    up_own = gather_z(up_shard)
    if square:
        right_all = place(me, [right_shard] + [swap(right_shard, "dp", 4, mask) for mask in range(1, 4)], (up_shard,))
        attn_own = later(gather_z(attn_shard), (right_all,))
    else:
        attn_own = gather_z(attn_shard)
    grad_keep, grad_away = dispatch(slot_row, cotangent, (attn_own,))
    grad_got = swap_core(grad_away)
    down_shard = expert_shard(down_weight[:, :, :half], (grad_keep,))
    if square:
        right = lax.all_gather(right_all.reshape(4, -1, half), "z", axis=0)
        attn_near = swap_near(attn_own, attn_own)
        mine_p = (attn_own, *attn_near, *gather_far(cut_halves(*attn_near, (down_shard,))))
        up_near = swap_near(up_own, up_own)
    else:
        right = lax.all_gather(gather_z(right_shard), "dp", axis=0, tiled=True)
        right = jnp.swapaxes(right.reshape(4, 4, -1, half), 0, 1)
        mine_p = gather_pieces(attn_own)
    other_p = tuple(swap_core(piece) for piece in mine_p)

    side = scalar(core)
    normed_one, qkv = project(side, me, tokens, gain_one, shift_one, qkv_bias, mine_p, other_p, (up_own, grad_got, bias_out, gain_two, shift_two))
    other_normed_one = swap_core(normed_one)
    seg_row, seg_col = segment_ids, segment_ids.reshape(rows, 1)
    attended, lse = attention(qkv, seg_col, seg_row)
    other_attended = swap_core(attended)
    if square:
        up_cut = cut_halves(*up_near, (attended,))
        w_up = (up_own, *up_near, *gather_far(up_cut))
    else:
        up_cut, w_up = (), gather_pieces(up_own)
    middle, in_keep, in_away = middle_part(
        side, me, slot_row, tokens, attended, mine_p, other_p, bias_out, gain_two, shift_two, after=(*up_cut, other_normed_one)
    )
    mine_w = place(me, mine_p, (middle,))
    other_w = place(me, other_p, (mine_w,))
    down_own = later(gather_z(down_shard), (middle,))
    in_got = swap_core(later(in_away, (*w_up[3:], down_own, other_w)))

    if square:
        down_near_got = swap_near(down_own, down_own)
    act, slope = up(me, in_keep, in_got, bias_up, w_up)
    if square:
        down_cut = cut_halves(*down_near_got, (act,))
        w_down = (down_own, *down_near_got, *gather_far(down_cut))
    else:
        down_cut, w_down = (), gather_pieces(down_own)
    down_partial, down_bias_grad = outer(act, grad_keep, grad_got, (*down_cut, right))
    down_half = lax.psum_scatter(later(down_partial, w_down[3:]), "dp", scatter_dimension=0, tiled=True)
    back_keep, back_away, up_partial, up_out_x, up_out_y, up_bias_grad = down_grad(
        me, grad_keep, grad_got, in_keep, in_got, slope, w_up, w_down, right, after=(other_w,)
    )
    back_got = swap_core(back_away)
    if square:
        up_partial = up_partial.reshape(4, width // 4, -1)
        up_far = swap_near(up_out_x, up_out_y)

    middle_grads, mine_projected, other_projected, attended_grad, gain_two_grad, shift_two_grad, out_bias_grad = (
        middle_grad(side, slot_col, back_keep, back_got, middle, cotangent, mine_w, other_w, gain_two)
    )
    other_projected = swap_core(other_projected)
    qkv_away = attention_grad(qkv, attended_grad, lse, seg_col, seg_row, 1 - core)
    qkv_got = swap_core(qkv_away)
    partial = two_sum(
        me, 4, attended, mine_projected[None], other_attended, other_projected[None], 0, after=(qkv_away,)
    )
    up_next = scatter_next(me, up_partial, *up_far, after=partial[:1]) if square else partial[:1]
    down_total = scatter_z(later(down_half, up_next))
    qkv_kept = attention_grad(qkv, attended_grad, lse, seg_col, seg_row, core, after=up_next)
    partial, out_x, out_y = two_sum(me, 4, normed_one, qkv_kept, other_normed_one, qkv_got, 1, into=partial)
    input_grad, gain_one_grad, shift_one_grad, bias_sums = input_grads(
        qkv_kept, qkv_away, tokens, middle_grads, mine_w, other_w, gain_one, after=(out_x,)
    )
    if square:
        partial = partial.reshape(4, width // 4, -1)
        far = swap_near(out_x, out_y)
        up_block = scatter_near(me, up_partial, *swap_near(*up_next), after=(input_grad, down_total))
        up_block = later(up_block, far)
        near = scatter_next(me, partial, *far, after=(up_block,))
        near_got = swap_near(*near)
    else:
        near = ()
        up_block = lax.psum_scatter(up_partial, "dp", scatter_dimension=0, tiled=True)
    up_total = scatter_z(up_block)
    down_weight_grad = pair(side, down_total)
    y_keep, y_away = down(me, act, w_down, right, after=(*near, down_weight_grad))
    y_got = swap_core(y_away)
    if square:
        last = scatter_near(me, partial, *near_got, after=(y_keep,))
    else:
        last = lax.psum_scatter(partial, "dp", scatter_dimension=0, tiled=True)
    block_out = output(slot_col, expert_ids, y_keep, y_got, middle, bias_down, after=(last,))
    query_bias_grad = by_core(core, bias_sums[0], bias_sums[1])
    value_bias_grad = by_core(core, bias_sums[2], bias_sums[3])

    vectors = [
        gain_one_grad,
        shift_one_grad,
        query_bias_grad.reshape(1, width),
        value_bias_grad.reshape(1, width),
        out_bias_grad,
        gain_two_grad,
        shift_two_grad,
        down_bias_grad,
    ]
    vectors = jnp.concatenate([v.reshape(1, width) for v in vectors], 0).reshape(8, devices, share)
    vectors = jnp.swapaxes(vectors, 0, 1).reshape(devices, 8 * share)
    sent = later(jnp.concatenate([vectors, up_bias_grad.reshape(devices, up_share)], 1), (last,))
    got = lax.all_to_all(sent, ALL, 0, 0, tiled=True).reshape(devices // 2, 2, -1)
    both = jnp.sum(got, 0)
    total = both[0] + both[1]
    sums = [total[i * share : (i + 1) * share] for i in range(7)]
    down_bias_sum = both[:, 7 * share : 8 * share]
    up_bias_sum = both[:, 8 * share :]

    up_weight_grad = pair(side, up_total)
    out_weight_grad, qkv_weight_grad = finish(side, later(scatter_z(last), (up_bias_sum, down_weight_grad, up_weight_grad, block_out)))
    return (
        block_out,
        input_grad,
        sums[0],
        sums[1],
        qkv_weight_grad,
        sums[2],
        sums[3],
        out_weight_grad,
        sums[4],
        sums[5],
        sums[6],
        up_weight_grad,
        up_bias_sum,
        down_weight_grad,
        down_bias_sum,
    )


def solution(mesh):
    n_dp, n_z = mesh.shape["dp"], mesh.shape["fsdp"] // 2
    split = Mesh(mesh.devices.reshape(n_dp, n_z, 2), ALL)
    row, flat, wide, cube = P(ALL, None), P(ALL), P(None, ALL), P(ALL, None, None)
    in_specs = (row, row, row, flat, flat, row, flat, flat, row, flat, flat, flat, cube, wide, cube, wide, row)
    out_specs = (row, row, flat, flat, row, flat, flat, row, flat, flat, flat, cube, wide, cube, wide)
    return jax.shard_map(
        functools.partial(shards, n_dp, n_z), mesh=split, in_specs=in_specs, out_specs=out_specs, check_vma=False
    )
```

```python
import functools

import jax
import jax.numpy as jnp
from jax import lax
from jax.experimental import pallas as pl
from jax.experimental.pallas import tpu as pltpu
from jax.sharding import Mesh, PartitionSpec as P

HEAD_DIM = 64
CAPACITY = 640
LONGEST = 512
PAIR = 2 * HEAD_DIM
TILE_Q = 256
MASKED = -1e30
epsilon = 1e-05
bf16 = jnp.bfloat16
f32 = jnp.float32
ALL = ("dp", "z", "c")
BLOCK = 256
WIDE = 512
FBLOCK = 512
NN = (((1,), (0,)), ((), ()))
NT = (((1,), (1,)), ((), ()))
TN = (((0,), (0,)), ((), ()))


def dot(a, b, dims=NN):
    return lax.dot_general(a, b, dims, preferred_element_type=f32)


def params(flops, moved, special=0):
    return dict(
        compiler_params=pltpu.CompilerParams(vmem_limit_bytes=58 << 20),
        cost_estimate=pl.CostEstimate(flops=2 * int(flops), bytes_accessed=int(moved), transcendentals=int(special)),
    )


def launch(kernel, name, grid, args, in_specs, out_specs, out_shape, scratch=(), scalars=(), after=(), work=(0, 0)):
    first, last = len(scalars) + len(args), len(scalars) + len(args) + len(after)

    def body(*refs):
        kernel(*refs[:first], *refs[last:])

    return pl.pallas_call(
        body,
        grid_spec=pltpu.PrefetchScalarGridSpec(
            num_scalar_prefetch=len(scalars),
            grid=grid,
            in_specs=[*in_specs, *[pl.BlockSpec(memory_space=pl.ANY)] * len(after)],
            out_specs=out_specs,
            scratch_shapes=list(scratch),
        ),
        out_shape=out_shape,
        **params(*work),
        name=name,
    )(*scalars, *args, *after)


def whole(*shape):
    return pl.BlockSpec(shape, lambda *_: (0,) * len(shape))


def shape_of(shape, dtype):
    return jax.ShapeDtypeStruct(shape, dtype)


def spans(rows):
    out = []
    for start in range(0, rows, TILE_Q):
        low = max(0, (start - LONGEST + 1) // TILE_Q * TILE_Q)
        out.append((start, low, start + TILE_Q))
    return out


def fill_bias(bias_refs, seg_col, seg_row, blocks):
    for bias, (start, low, high) in zip(bias_refs, blocks):
        shape = (high - low, TILE_Q)
        key = low + lax.broadcasted_iota(jnp.int32, shape, 0)
        query = start + lax.broadcasted_iota(jnp.int32, shape, 1)
        same = seg_col[low:high, :] == seg_row[:, start : start + TILE_Q]
        bias[...] = jnp.where((key <= query) & same, 0.0, MASKED)


def forward_kernel(blocks, seg_col, seg_row, q_ref, k_ref, v_ref, o_ref, lse_ref, *bias):
    @pl.when(pl.program_id(0) == 0)
    def _():
        fill_bias(bias, seg_col, seg_row, blocks)

    lane = lax.broadcasted_iota(jnp.int32, (TILE_Q, PAIR), 1)
    work = [(block, head) for block in range(len(blocks)) for head in range(2)]

    def raw_scores(block, head):
        start, low, high = blocks[block]
        q = q_ref[start : start + TILE_Q, :] * jnp.asarray(HEAD_DIM**-0.5, bf16)
        mine = (lane < HEAD_DIM) == (head == 0)
        return dot(k_ref[low:high, :], jnp.where(mine, q, jnp.zeros_like(q)), NT)

    coming, heads = raw_scores(*work[0]), []
    for number, (block, head) in enumerate(work):
        start, low, high = blocks[block]
        rows = slice(start, start + TILE_Q)
        raw = coming
        if number + 1 < len(work):
            coming = raw_scores(*work[number + 1])
        scores = raw + bias[block][...]
        top = jnp.max(scores, 0, keepdims=True)
        probs = jnp.exp(scores - top)
        total = jnp.sum(probs, 0, keepdims=True)
        out = dot(v_ref[low:high, :], probs.astype(bf16), TN)
        heads.append(out[head * HEAD_DIM : (head + 1) * HEAD_DIM] * (1.0 / total))
        lse_ref[0, head : head + 1, rows] = top + jnp.log(total)
        if head == 1:
            o_ref[rows, :] = jnp.concatenate(heads, 0).T.astype(bf16)
            heads = []


def attention(qkv, seg_col, seg_row, after=()):
    rows, width = qkv.shape[0], qkv.shape[1] // 3
    pairs = width // PAIR
    blocks = spans(rows)
    return launch(
        functools.partial(forward_kernel, blocks),
        "attention_forward",
        (pairs,),
        (seg_col, seg_row, qkv, qkv, qkv),
        [
            whole(rows, 1),
            whole(1, rows),
            pl.BlockSpec((rows, PAIR), lambda p: (0, p)),
            pl.BlockSpec((rows, PAIR), lambda p: (0, pairs + p)),
            pl.BlockSpec((rows, PAIR), lambda p: (0, 2 * pairs + p)),
        ],
        (pl.BlockSpec((rows, PAIR), lambda p: (0, p)), pl.BlockSpec((1, 2, rows), lambda p: (p, 0, 0))),
        (shape_of((rows, width), bf16), shape_of((pairs, 2, rows), f32)),
        [pltpu.VMEM((high - low, TILE_Q), f32) for _, low, high in blocks],
        after=after,
        work=(16 * rows * rows * width, 8 * rows * width),
    )


def backward_kernel(
    blocks, first, seg_col, seg_row, q_ref, k_ref, v_ref, do_ref, lse_ref, d_ref, dk_sum, dv_sum, *bias
):
    @pl.when(pl.program_id(0) == 0)
    def _():
        fill_bias(bias, seg_col, seg_row, blocks)

    dk_sum[...] = jnp.zeros_like(dk_sum)
    dv_sum[...] = jnp.zeros_like(dv_sum)
    lane = lax.broadcasted_iota(jnp.int32, (TILE_Q, PAIR), 1)
    scale = HEAD_DIM**-0.5
    work = [(block, head) for block in range(len(blocks)) for head in range(2)]

    def products(block, head):
        start, low, high = blocks[block]
        rows = slice(start, start + TILE_Q)
        mine = (lane < HEAD_DIM) == (head == 0)
        zero = jnp.zeros((TILE_Q, PAIR), bf16)
        q = jnp.where(mine, q_ref[rows, :] * jnp.asarray(scale, bf16), zero)
        do = jnp.where(mine, do_ref[rows, :], zero)
        return q, do, dot(k_ref[low:high, :], q, NT), dot(v_ref[low:high, :], do, NT)

    coming, dq = products(*work[0]), []
    for number, (block, head) in enumerate(work):
        start, low, high = blocks[block]
        rows = slice(start, start + TILE_Q)
        q, do, raw, grad = coming
        if number + 1 < len(work):
            coming = products(*work[number + 1])
        probs = jnp.exp(raw + bias[block][...] - lse_ref[0, head : head + 1, rows])
        weighted = probs * grad
        total = jnp.sum(weighted, 0, keepdims=True)
        ds = (weighted - probs * total).astype(bf16)
        dv_sum[low:high, :] += dot(probs.astype(bf16), do)
        dk_sum[low:high, :] += dot(ds, q)
        dq.append(dot(k_ref[low:high, :], ds, TN)[head * HEAD_DIM : (head + 1) * HEAD_DIM] * scale)
        if head == 1:
            d_ref[0, rows, :] = jnp.concatenate(dq, 0).T.astype(bf16)
            dq = []
    d_ref[1, ...] = dk_sum[...].astype(bf16)
    d_ref[2, ...] = dv_sum[...].astype(bf16)


def attention_grad(qkv, do, lse, seg_col, seg_row, half, after=()):
    rows, width = qkv.shape[0], qkv.shape[1] // 3
    pairs = width // PAIR
    count = pairs // 2
    blocks = spans(rows)
    first = jnp.reshape(half * count, (1,)).astype(jnp.int32)
    return launch(
        functools.partial(backward_kernel, blocks),
        "attention_backward",
        (count,),
        (seg_col, seg_row, qkv, qkv, qkv, do, lse),
        [
            whole(rows, 1),
            whole(1, rows),
            pl.BlockSpec((rows, PAIR), lambda p, b: (0, b[0] + p)),
            pl.BlockSpec((rows, PAIR), lambda p, b: (0, pairs + b[0] + p)),
            pl.BlockSpec((rows, PAIR), lambda p, b: (0, 2 * pairs + b[0] + p)),
            pl.BlockSpec((rows, PAIR), lambda p, b: (0, b[0] + p)),
            pl.BlockSpec((1, 2, rows), lambda p, b: (b[0] + p, 0, 0)),
        ],
        pl.BlockSpec((3, rows, PAIR), lambda p, b: (0, 0, p)),
        shape_of((3, rows, count * PAIR), bf16),
        [pltpu.VMEM((rows, PAIR), f32)] * 2 + [pltpu.VMEM((high - low, TILE_Q), f32) for _, low, high in blocks],
        scalars=(first,),
        after=after,
        work=(12 * rows * rows * width, 8 * rows * width),
    )


def norm_parts(values):
    centre = values - jnp.mean(values, -1, keepdims=True)
    inverse = lax.rsqrt(jnp.mean(centre * centre, -1, keepdims=True) + epsilon)
    return centre * inverse, inverse


def norm_grad(normed, inverse, gain, grad):
    scaled = grad * gain
    return inverse * (
        scaled - jnp.mean(scaled, -1, keepdims=True) - normed * jnp.mean(scaled * normed, -1, keepdims=True)
    )


def add_rows(ref, value):
    @pl.when(pl.program_id(0) == 0)
    def _():
        ref[...] = value

    @pl.when(pl.program_id(0) > 0)
    def _():
        ref[...] += value


def sides(core, mine, other):
    return (mine, core[0]), (other, 1 - core[0])


def project_kernel(core, me, x_ref, gain, shift, bias, *refs):
    pieces, (a_ref, qkv_ref) = refs[:10], refs[10:]
    half = x_ref.shape[1] // 2
    normed, _ = norm_parts(x_ref[...].astype(f32))
    a_ref[...] = (normed * gain[...] + shift[...]).astype(bf16)
    depth = pieces[0].shape[0]
    for ws, side in sides(core, pieces[:5], pieces[5:]):
        first, second = 0.0, 0.0
        for r in range(4):
            a = a_ref[:, pl.ds(pl.multiple_of((me[0] ^ r) * depth, depth), depth)]
            first = first + dot(a, ws[r][:, : 2 * half])
            second = second + dot(a, ws[4][...] if r == 3 else ws[r][:, 2 * half :])
        for j, out in enumerate((first[:, :half], first[:, half:], second)):
            at = pl.ds(pl.multiple_of(2 * half * j + half * side, half), half)
            qkv_ref[:, at] = (out + bias[:, at]).astype(bf16)


def project(core, me, x, gain, shift, bias, mine_w, other_w, after=()):
    rows, width = x.shape
    depth = mine_w[0].shape[0]
    weight = [whole(depth, 3 * width // 2)] * 3 + [whole(depth, width), whole(depth, width // 2)]
    return launch(
        project_kernel,
        "project",
        (rows // BLOCK,),
        (x, gain, shift, bias, *mine_w, *other_w),
        [
            pl.BlockSpec((BLOCK, width), lambda i, c, m: (i, 0)),
            whole(1, width),
            whole(1, width),
            whole(1, 3 * width),
            *weight,
            *weight,
        ],
        (
            pl.BlockSpec((BLOCK, width), lambda i, c, m: (i, 0)),
            pl.BlockSpec((BLOCK, 3 * width), lambda i, c, m: (i, 0)),
        ),
        (shape_of((rows, width), bf16), shape_of((rows, 3 * width), bf16)),
        scalars=(core, me),
        after=after,
        work=(6 * rows * width * width, 6 * width * width + 10 * rows * width),
    )


def send_slots(acc, slot, values, keep_ref, away_ref):
    step = pl.program_id(0)
    chosen = lax.broadcasted_iota(jnp.int32, (2 * CAPACITY, values.shape[0]), 0) == slot[...]
    part = dot(chosen.astype(bf16), values)

    @pl.when(step == 0)
    def _():
        acc[...] = part

    @pl.when(step > 0)
    def _():
        acc[...] += part

    @pl.when(step == pl.num_programs(0) - 1)
    def _():
        keep_ref[...] = acc[:CAPACITY, :].astype(bf16)
        away_ref[...] = acc[CAPACITY:, :].astype(bf16)


def dispatch_kernel(slot, g_ref, keep_ref, away_ref, acc):
    send_slots(acc, slot, g_ref[...], keep_ref, away_ref)


def dispatch(slot_row, values, after=()):
    rows, width = values.shape
    return launch(
        dispatch_kernel,
        "dispatch",
        (rows // WIDE,),
        (slot_row, values),
        [pl.BlockSpec((1, WIDE), lambda i: (0, i)), pl.BlockSpec((WIDE, width), lambda i: (i, 0))],
        (whole(CAPACITY, width),) * 2,
        (shape_of((CAPACITY, width), bf16),) * 2,
        [pltpu.VMEM((2 * CAPACITY, width), f32)],
        after=after,
        work=(4 * CAPACITY * rows * width, 2 * rows * width + 4 * CAPACITY * width),
    )


def middle_kernel(core, me, slot, x_ref, o_ref, *refs):
    pieces, (bias, gain, shift, mid_ref, keep_ref, away_ref, acc) = refs[:8], refs[8:]
    half = x_ref.shape[1] // 2
    depth = pieces[0].shape[0]
    for ws, side in sides(core, pieces[:4], pieces[4:]):
        at = pl.ds(pl.multiple_of(half * side, half), half)
        out = x_ref[:, at].astype(f32) + bias[:, at]
        for r, w in enumerate(ws):
            out = out + dot(o_ref[:, pl.ds(pl.multiple_of((me[0] ^ r) * depth, depth), depth)], w[...])
        mid_ref[:, at] = out
    normed, _ = norm_parts(mid_ref[...])
    send_slots(acc, slot, (normed * gain[...] + shift[...]).astype(bf16), keep_ref, away_ref)


def out_half(width):
    return pl.BlockSpec((width, width // 2), lambda *_: (0, 3))


def middle_part(core, me, slot_row, x, attended, mine_w, other_w, bias, gain, shift, after=()):
    rows, width = x.shape
    block = pl.BlockSpec((WIDE, width), lambda i, c, m: (i, 0))
    half, depth = width // 2, mine_w[0].shape[0]
    out_columns = [pl.BlockSpec((depth, half), lambda *_: (0, 3))] * 3 + [pl.BlockSpec((depth, half), lambda *_: (0, 1))]
    of = lambda w: (w[0], w[1], w[2], w[4])
    return launch(
        middle_kernel,
        "middle",
        (rows // WIDE,),
        (slot_row, x, attended, *of(mine_w), *of(other_w), bias, gain, shift),
        [
            pl.BlockSpec((1, WIDE), lambda i, c, m: (0, i)),
            block,
            block,
            *out_columns,
            *out_columns,
            whole(1, width),
            whole(1, width),
            whole(1, width),
        ],
        (block, whole(CAPACITY, width), whole(CAPACITY, width)),
        (shape_of((rows, width), f32),) + (shape_of((CAPACITY, width), bf16),) * 2,
        [pltpu.VMEM((2 * CAPACITY, width), f32)],
        scalars=(core, me),
        after=after,
        work=(4 * CAPACITY * rows * width + 2 * rows * width * width, 10 * rows * width + 4 * CAPACITY * width),
    )


def from_slots(slot, keep_ref, away_ref):
    chosen = lax.broadcasted_iota(jnp.int32, (slot.shape[0], 2 * CAPACITY), 1) == slot[...]
    chosen = chosen.astype(bf16)
    return dot(chosen[:, :CAPACITY], keep_ref[...]) + dot(chosen[:, CAPACITY:], away_ref[...])


def middle_grad_kernel(
    core, slot, keep_ref, away_ref, mid_ref, g_ref, mine_w, other_w, gain,
    dmid_ref, mine_ref, other_ref, do_ref, gain_ref, shift_ref, bias_ref, dproj_ref,
):
    half = mid_ref.shape[1] // 2
    grad = from_slots(slot, keep_ref, away_ref)
    normed, inverse = norm_parts(mid_ref[...])
    dmid = g_ref[...].astype(f32) + norm_grad(normed, inverse, gain[...], grad)
    dproj_ref[...] = dmid.astype(bf16)
    dmid_ref[...] = dmid
    back = 0.0
    for (w, side), part in zip(sides(core, mine_w, other_w), (mine_ref, other_ref)):
        part[...] = dproj_ref[:, pl.ds(pl.multiple_of(half * side, half), half)]
        back = back + dot(part[...], w[...], NT)
    do_ref[...] = back.astype(bf16)
    add_rows(gain_ref, jnp.sum(grad * normed, 0, keepdims=True))
    add_rows(shift_ref, jnp.sum(grad, 0, keepdims=True))
    add_rows(bias_ref, jnp.sum(dproj_ref[...].astype(f32), 0, keepdims=True))


def middle_grad(core, slot_col, keep, away, middle, g, mine_w, other_w, gain, after=()):
    rows, width = middle.shape
    block = pl.BlockSpec((BLOCK, width), lambda i, c: (i, 0))
    part = pl.BlockSpec((BLOCK, width // 2), lambda i, c: (i, 0))
    slots = whole(CAPACITY, width)
    row = whole(1, width)
    return launch(
        middle_grad_kernel,
        "middle_grad",
        (rows // BLOCK,),
        (slot_col, keep, away, middle, g, mine_w, other_w, gain),
        [pl.BlockSpec((BLOCK, 1), lambda i, c: (i, 0)), slots, slots, block, block]
        + [out_half(width), out_half(width), row],
        (block, part, part, block, row, row, row),
        (shape_of((rows, width), f32),)
        + (shape_of((rows, width // 2), bf16),) * 2
        + (shape_of((rows, width), bf16),)
        + (shape_of((1, width), f32),) * 3,
        [pltpu.VMEM((BLOCK, width), bf16)],
        scalars=(core,),
        after=after,
        work=(4 * CAPACITY * rows * width + 2 * rows * width * width, 16 * rows * width + 4 * CAPACITY * width),
    )


def output_kernel(slot, route, keep_ref, away_ref, mid_ref, bias, out_ref):
    token_bias = jnp.where(route[...] == 0, bias[0:1, :], bias[1:2, :])
    out_ref[...] = (mid_ref[...] + from_slots(slot, keep_ref, away_ref) + token_bias).astype(bf16)


def output(slot_col, route_col, keep, away, middle, bias, after=()):
    rows, width = middle.shape
    block = pl.BlockSpec((WIDE, width), lambda i: (i, 0))
    column = pl.BlockSpec((WIDE, 1), lambda i: (i, 0))
    return launch(
        output_kernel,
        "output",
        (rows // WIDE,),
        (slot_col, route_col, keep, away, middle, bias),
        [column, column, whole(CAPACITY, width), whole(CAPACITY, width), block, whole(2, width)],
        block,
        shape_of((rows, width), bf16),
        after=after,
        work=(0, 2 * rows * width),
    )


def input_grad_kernel(
    mine_ref, away_ref, x_ref, dmid_ref, mine_w, other_w, gain, out_ref, gain_ref, shift_ref, bias_ref
):
    half = mine_ref.shape[2]
    grad = 0.0
    for ref, w in ((mine_ref, mine_w), (away_ref, other_w)):
        for j in range(3):
            grad = grad + dot(ref[j], w[:, half * j : half * (j + 1)], NT)
    normed, inverse = norm_parts(x_ref[...].astype(f32))
    out_ref[...] = dmid_ref[...] + norm_grad(normed, inverse, gain[...], grad)
    add_rows(gain_ref, jnp.sum(grad * normed, 0, keepdims=True))
    add_rows(shift_ref, jnp.sum(grad, 0, keepdims=True))
    rows = [jnp.sum(ref[j].astype(f32), 0, keepdims=True) for j in (0, 2) for ref in (mine_ref, away_ref)]
    add_rows(bias_ref, jnp.concatenate(rows, 0))


def input_grads(mine, away, x, dmid, mine_w, other_w, gain, after=()):
    rows, width = x.shape
    half = width // 2
    block = pl.BlockSpec((BLOCK, width), lambda i: (i, 0))
    part = pl.BlockSpec((3, BLOCK, half), lambda i: (0, i, 0))
    row, weight = whole(1, width), whole(width, 3 * half)
    return launch(
        input_grad_kernel,
        "input_grad",
        (rows // BLOCK,),
        (mine, away, x, dmid, mine_w, other_w, gain),
        [part, part, block, block, weight, weight, row],
        (block, row, row, whole(4, half)),
        (
            shape_of((rows, width), f32),
            shape_of((1, width), f32),
            shape_of((1, width), f32),
            shape_of((4, half), f32),
        ),
        after=after,
        work=(0, 2 * rows * width),
    )


def two_sum_kernel(at, n_dp, me, a1, b1, a2, b2, out_ref, far_x, far_y, t1, t2):
    step = pl.program_id(0)

    @pl.when(step == 0)
    def _():
        t1[...] = a1[...].T
        t2[...] = a2[...].T

    out_ref[...] = (dot(t1[...], b1[0]) + dot(t2[...], b2[0])).astype(bf16)
    rows = out_ref.shape[0] // n_dp
    far = pl.ds(pl.multiple_of((me[0] ^ (n_dp - 1)) * rows, rows), rows)

    @pl.when(step + at < 2)
    def _():
        far_x[...] = out_ref[far, :]

    @pl.when(step + at >= 2)
    def _():
        far_y[...] = out_ref[far, :]


def two_sum(me, n_dp, a1, b1, a2, b2, at, into=(), after=()):
    rows, width = a1.shape
    parts, _, columns = b1.shape
    left, right = whole(rows, width), pl.BlockSpec((1, rows, columns), lambda j, m: (j, 0, 0))
    count = 5 + len(into)

    def body(*refs):
        two_sum_kernel(at, n_dp, *refs[:5], *refs[count + len(after) :])

    far = (width // n_dp, columns)
    return pl.pallas_call(
        body,
        grid_spec=pltpu.PrefetchScalarGridSpec(
            num_scalar_prefetch=1,
            grid=(parts,),
            in_specs=[left, right, left, right] + [pl.BlockSpec(memory_space=pl.ANY)] * (len(into) + len(after)),
            out_specs=(
                pl.BlockSpec((width, columns), lambda j, m: (0, at + j)),
                pl.BlockSpec(far, lambda j, m: (0, jnp.minimum(at + j, 1))),
                pl.BlockSpec(far, lambda j, m: (0, jnp.maximum(at + j - 2, 0))),
            ),
            scratch_shapes=[pltpu.VMEM((width, rows), bf16)] * 2,
        ),
        out_shape=(
            shape_of((width, 4 * columns), bf16),
            shape_of((width // n_dp, 2 * columns), bf16),
            shape_of((width // n_dp, 2 * columns), bf16),
        ),
        input_output_aliases={5 + i: i for i in range(len(into))},
        **params(4 * rows * width * columns * parts, 4 * rows * (width + parts * columns)),
        name="two_sum",
    )(me, a1, b1, a2, b2, *into, *after)


def up_kernel(me, xk, xr, bias, w0, w1, w2, w3a, w3b, act_ref, slope_ref):
    step = pl.program_id(0)
    depth = w0.shape[0]
    far = jnp.where(step < pl.num_programs(0) // 2, w3a[...], w3b[...])
    root = 0.7978845608028654
    for part, x in enumerate((xk, xr)):
        inner = bias[...]
        for r, w in enumerate((w0[...], w1[...], w2[...], far)):
            at = pl.multiple_of((me[0] ^ r) * depth, depth)
            inner = inner + dot(x[:, pl.ds(at, depth)], w)
        square = inner * inner
        bent = jnp.tanh(inner * (root + (root * 0.044715) * square))
        rise = 0.5 + 0.5 * bent
        act = (inner * rise).astype(bf16)
        slope = rise + inner * rise * (1.0 - bent) * (root + (root * 3 * 0.044715) * square)
        rows = slice(part * x.shape[0], (part + 1) * x.shape[0])
        act_ref[rows, :] = act
        slope_ref[rows, :] = slope.astype(bf16)


def up(me, xk, xr, bias, pieces, after=()):
    slots, width = xk.shape
    depth, hidden = pieces[0].shape
    steps = hidden // FBLOCK
    last = steps // 2 - 1
    tokens = whole(slots, width)
    weight = pl.BlockSpec((depth, FBLOCK), lambda i, m: (0, i))
    return launch(
        up_kernel,
        "experts_up",
        (steps,),
        (xk, xr, bias, *pieces),
        [tokens] * 2
        + [pl.BlockSpec((1, FBLOCK), lambda i, m: (0, i))]
        + [weight] * 3
        + [
            pl.BlockSpec((depth, FBLOCK), lambda i, m: (0, jnp.minimum(i, last))),
            pl.BlockSpec((depth, FBLOCK), lambda i, m: (0, jnp.maximum(i - last - 1, 0))),
        ],
        (
            pl.BlockSpec((2 * slots, FBLOCK), lambda i, m: (0, i)),
            pl.BlockSpec((2 * slots, FBLOCK), lambda i, m: (0, i)),
        ),
        (shape_of((2 * slots, hidden), bf16), shape_of((2 * slots, hidden), bf16)),
        scalars=(me,),
        after=after,
        work=(4 * slots * width * hidden, 2 * width * hidden + 8 * slots * hidden),
    )


def outer_kernel(act_ref, gk, gr, out_ref, bias_ref, g):
    @pl.when(pl.program_id(0) == 0)
    def _():
        half = gk.shape[0]
        g[:half, :] = gk[...]
        g[half:, :] = gr[...]
        bias_ref[...] = jnp.sum(g[...].astype(f32), 0, keepdims=True)

    out_ref[...] = dot(act_ref[...], g[...], TN).astype(bf16)


def outer(act, gk, gr, after=()):
    slots, width = gk.shape
    hidden = act.shape[1]
    return launch(
        outer_kernel,
        "experts_outer",
        (hidden // FBLOCK,),
        (act, gk, gr),
        [pl.BlockSpec((2 * slots, FBLOCK), lambda i: (0, i)), whole(slots, width), whole(slots, width)],
        (pl.BlockSpec((FBLOCK, width), lambda i: (i, 0)), whole(1, width)),
        (shape_of((hidden, width), bf16), shape_of((1, width), f32)),
        [pltpu.VMEM((2 * slots, width), bf16)],
        after=after,
        work=(4 * slots * width * hidden, 2 * width * hidden + 4 * slots * hidden),
    )


def hold_block(held, per, pieces, right):
    w0, w1, w2, w3a, w3b = pieces
    which = pl.program_id(0) // per
    half = held.shape[1] // 2
    for r, w in enumerate((w0, w1, w2)):

        @pl.when(which == r)
        def _(w=w):
            held[:, :half] = w[...]

    @pl.when(which == 3)
    def _():
        held[:, : half // 2] = w3a[...]
        held[:, half // 2 : half] = w3b[...]

    held[:, half:] = right[...].reshape(held.shape[0], half)


def down_grad_kernel(
    me, per, gk, gr, xk, xr, slope_ref, u0, u1, u2, u3a, u3b, w0, w1, w2, w3a, w3b, right,
    dk_ref, dr_ref, up_ref, far_x, far_y, bias_ref, held, acc, g, t,
):
    step = pl.program_id(0)
    slots = gk.shape[0]
    hold_block(held, per, (w0, w1, w2, w3a, w3b), right)

    @pl.when(step == 0)
    def _():
        g[:slots, :] = gk[...]
        g[slots:, :] = gr[...]
        t[:, :slots] = xk[...].T
        t[:, slots:] = xr[...].T
        acc[...] = jnp.zeros_like(acc)

    depth = u0.shape[0]
    early = (me[0] ^ (step // per)) * per + step % per < pl.num_programs(0) // 2
    u3 = jnp.where(early, u3a[...], u3b[...])
    inner = (dot(g[...], held[...], NT) * slope_ref[...].astype(f32)).astype(bf16)
    bias_ref[...] = jnp.sum(inner.astype(f32), 0, keepdims=True)
    up_ref[...] = dot(t[...], inner).astype(bf16)
    far = up_ref[pl.ds(pl.multiple_of((me[0] ^ 3) * depth, depth), depth), :]

    @pl.when(early)
    def _():
        far_x[...] = far

    @pl.when(jnp.logical_not(early))
    def _():
        far_y[...] = far

    for r, u in enumerate((u0[...], u1[...], u2[...], u3)):
        at = pl.multiple_of((me[0] ^ r) * depth, depth)
        acc[:, pl.ds(at, depth)] += dot(inner, u, NT)

    @pl.when(step == pl.num_programs(0) - 1)
    def _():
        dk_ref[...] = acc[:slots, :].astype(bf16)
        dr_ref[...] = acc[slots:, :].astype(bf16)


def second_specs(pieces, right):
    per = pieces[0].shape[0] // FBLOCK
    _, _, rows, half = right.shape

    def spec(r, columns):
        return pl.BlockSpec((FBLOCK, columns), lambda i, m: (jnp.clip(i - r * per, 0, per - 1), 0))

    return [spec(0, half), spec(1, half), spec(2, half), spec(3, half // 2), spec(3, half // 2)] + [
        pl.BlockSpec((FBLOCK // rows, 1, rows, half), lambda i, m: (i % per, m[0] ^ (i // per), 0, 0))
    ]


def down_grad(me, gk, gr, xk, xr, slope, up_pieces, down_pieces, right, after=()):
    slots, width = xk.shape
    depth, hidden = up_pieces[0].shape
    per = down_pieces[0].shape[0] // FBLOCK
    steps = hidden // FBLOCK
    half = steps // 2
    at = lambda i, m: (m[0] ^ (i // per)) * per + i % per

    def far(first):
        def block(i, m):
            low = jnp.where((m[0] < 2) == first, 0, half)
            return 0, at(jnp.clip(i, low, low + half - 1), m) - (0 if first else half)

        return pl.BlockSpec((depth, FBLOCK), block)

    tokens = whole(slots, width)
    weight = pl.BlockSpec((depth, FBLOCK), lambda i, m: (0, at(i, m)))
    return launch(
        lambda me, *refs: down_grad_kernel(me, per, *refs),
        "experts_grad",
        (steps,),
        (gk, gr, xk, xr, slope, *up_pieces, *down_pieces, right),
        [tokens] * 4
        + [pl.BlockSpec((2 * slots, FBLOCK), lambda i, m: (0, at(i, m)))]
        + [weight] * 3
        + [
            pl.BlockSpec((depth, FBLOCK), lambda i, m: (0, jnp.minimum(at(i, m), half - 1))),
            pl.BlockSpec((depth, FBLOCK), lambda i, m: (0, jnp.maximum(at(i, m) - half, 0))),
        ]
        + second_specs(down_pieces, right),
        (
            tokens,
            tokens,
            pl.BlockSpec((width, FBLOCK), lambda i, m: (0, at(i, m))),
            far(True),
            far(False),
            pl.BlockSpec((1, FBLOCK), lambda i, m: (0, at(i, m))),
        ),
        (
            shape_of((slots, width), bf16),
            shape_of((slots, width), bf16),
            shape_of((width, hidden), bf16),
            shape_of((depth, hidden // 2), bf16),
            shape_of((depth, hidden // 2), bf16),
            shape_of((1, hidden), f32),
        ),
        [
            pltpu.VMEM((FBLOCK, width), bf16),
            pltpu.VMEM((2 * slots, width), f32),
            pltpu.VMEM((2 * slots, width), bf16),
            pltpu.VMEM((width, 2 * slots), bf16),
        ],
        scalars=(me,),
        after=after,
        work=(12 * slots * width * hidden, 6 * width * hidden + 4 * slots * hidden),
    )


def down_kernel(me, per, act_ref, w0, w1, w2, w3a, w3b, right, keep_ref, away_ref, held, acc):
    hold_block(held, per, (w0, w1, w2, w3a, w3b), right)
    part = dot(act_ref[...], held[...])

    @pl.when(pl.program_id(0) == 0)
    def _():
        acc[...] = part

    @pl.when(pl.program_id(0) > 0)
    def _():
        acc[...] += part

    @pl.when(pl.program_id(0) == pl.num_programs(0) - 1)
    def _():
        slots = keep_ref.shape[0]
        keep_ref[...] = acc[:slots, :].astype(bf16)
        away_ref[...] = acc[slots:, :].astype(bf16)


def down(me, act, pieces, right, after=()):
    slots, hidden = act.shape
    width = 2 * right.shape[3]
    per = pieces[0].shape[0] // FBLOCK
    return launch(
        lambda me, *refs: down_kernel(me, per, *refs),
        "experts_down",
        (hidden // FBLOCK,),
        (act, *pieces, right),
        [pl.BlockSpec((slots, FBLOCK), lambda i, m: (0, (m[0] ^ (i // per)) * per + i % per))]
        + second_specs(pieces, right),
        (whole(slots // 2, width),) * 2,
        (shape_of((slots // 2, width), bf16),) * 2,
        [pltpu.VMEM((FBLOCK, width), bf16), pltpu.VMEM((slots, width), f32)],
        scalars=(me,),
        after=after,
        work=(2 * slots * width * hidden, 2 * width * hidden + 2 * slots * hidden),
    )


def place_kernel(at, *refs):
    out_ref = refs[-1]
    for r, piece in enumerate(refs[: 4 if len(refs) == 6 else -1]):

        @pl.when(pl.program_id(0) == r)
        def _(r=r, piece=piece):
            columns = piece.shape[1]
            out_ref[0, :, :columns] = piece[...]
            if columns < out_ref.shape[2]:
                out_ref[0, :, columns:] = refs[r + 1][...]


def place(at, pieces, after=()):
    rows, columns = pieces[0].shape
    count = sum(p.shape[1] for p in pieces) // columns
    return launch(
        place_kernel,
        "place",
        (count,),
        pieces,
        [whole(*p.shape) for p in pieces],
        pl.BlockSpec((1, rows, columns), lambda r, at: (at[0] ^ r, 0, 0)),
        shape_of((count, rows, columns), bf16),
        scalars=(at,),
        after=after,
        work=(0, 4 * count * rows * columns),
    ).reshape(count * rows, columns)


def pick(array, index, axis=0):
    return lax.dynamic_index_in_dim(array, index, axis, keepdims=False)


def swap(value, axis, size, mask):
    return lax.ppermute(value, axis, [(i, i ^ mask) for i in range(size)])


def swap_core(value):
    return swap(value, "c", 2, 1)


def by_core(core, mine, other, axis=0):
    return jnp.where(core == 0, jnp.stack([mine, other], axis), jnp.stack([other, mine], axis))


def add_kernel(me, part_x, part_y, by_x, by_y, next_x, next_y):
    first = pl.program_id(0) == 0
    more_x = jnp.where(first, 0.0, by_y[...].astype(f32))
    more_y = jnp.where(first, by_x[...].astype(f32), 0.0)
    next_x[...] = (part_x[0].astype(f32) + more_x).astype(bf16)
    next_y[...] = (part_y[0].astype(f32) + more_y).astype(bf16)


def scatter_next(me, partial, by_x, by_y, after=()):
    _, rows, columns = partial.shape
    half = columns // 2
    step = rows // 2
    block = lambda mask: pl.BlockSpec((1, step, half), lambda h, i, m: (m[0] ^ mask, i, h))
    next_x, next_y = launch(
        add_kernel,
        "far_add",
        (2, 2),
        (partial, partial, by_x, by_y),
        [
            block(1),
            block(2),
            pl.BlockSpec((step, half), lambda h, i, m: (jnp.where(h == 0, i, 1), 0)),
            pl.BlockSpec((step, half), lambda h, i, m: (jnp.where(h == 0, 0, i), 0)),
        ],
        (pl.BlockSpec((step, half), lambda h, i, m: (i, h)),) * 2,
        (shape_of((rows, columns), bf16),) * 2,
        scalars=(me,),
        after=after,
    )
    return next_x, next_y


def swap_near(x, y):
    return swap(x, "dp", 4, 1), swap(y, "dp", 4, 2)


def near_kernel(me, part, got_x, got_y, out_ref):
    out_ref[...] = (part[0].astype(f32) + got_x[...].astype(f32) + got_y[...].astype(f32)).astype(bf16)


def scatter_near(me, partial, got_x, got_y, after=()):
    _, rows, columns = partial.shape
    step = rows // 4
    block = pl.BlockSpec((step, columns), lambda i, m: (i, 0))
    return launch(
        near_kernel,
        "near_add",
        (4,),
        (partial, got_x, got_y),
        [pl.BlockSpec((1, step, columns), lambda i, m: (m[0], i, 0)), block, block],
        block,
        shape_of((rows, columns), bf16),
        scalars=(me,),
        after=after,
    )


def pair_kernel(core, mine_ref, other_ref, out_ref):
    mine, other = mine_ref[0].astype(f32), other_ref[...].astype(f32)
    out_ref[:, 0, :] = jnp.where(core[0] == 0, mine, other)
    out_ref[:, 1, :] = jnp.where(core[0] == 0, other, mine)


def pair(core, total):
    rows, columns = total.shape[0] // 2, total.shape[1]
    halves = total.reshape(2, rows, columns)
    other = swap_core(pick(halves, 1 - core[0]))
    return launch(
        pair_kernel,
        "pair",
        (1,),
        (halves, other),
        [pl.BlockSpec((1, rows, columns), lambda i, c: (c[0], 0, 0)), whole(rows, columns)],
        whole(rows, 2, columns),
        shape_of((rows, 2, columns), f32),
        scalars=(core,),
        work=(0, 2 * rows * columns),
    )


def gather_z(shard):
    return lax.all_gather(shard, "z", axis=0, tiled=True)


def scatter_z(block):
    return lax.psum_scatter(block, "z", scatter_dimension=0, tiled=True)


def later(value, after):
    def body(*refs):
        pass

    return pl.pallas_call(
        body,
        in_specs=[pl.BlockSpec(memory_space=pl.ANY)] * (1 + len(after)),
        out_specs=pl.BlockSpec(memory_space=pl.ANY),
        out_shape=shape_of(value.shape, value.dtype),
        input_output_aliases={0: 0},
        **params(0, 0),
        name="later",
    )(value, *after)


def halves_kernel(x_ref, y_ref, out_x, out_y, held_x, held_y, sems):
    half = out_x.shape[1]
    inward = [
        pltpu.make_async_copy(x_ref.at[:, :half], held_x, sems.at[0]),
        pltpu.make_async_copy(y_ref.at[:, half:], held_y, sems.at[1]),
    ]
    outward = [
        pltpu.make_async_copy(held_x, out_x, sems.at[2]),
        pltpu.make_async_copy(held_y, out_y, sems.at[3]),
    ]
    for copy in inward:
        copy.start()
    for arrived, copy in zip(inward, outward):
        arrived.wait()
        copy.start()
    for copy in outward:
        copy.wait()


def cut_halves(by_x, by_y, after=()):
    rows, columns = by_x.shape
    place = pl.BlockSpec(memory_space=pltpu.HBM)
    return launch(
        halves_kernel,
        "cut_halves",
        (1,),
        (by_x, by_y),
        [place, place],
        (place, place),
        (shape_of((rows, columns // 2), bf16),) * 2,
        [pltpu.VMEM((rows, columns // 2), bf16)] * 2 + [pltpu.SemaphoreType.DMA((4,))],
        after=after,
    )


def gather_far(cut):
    return swap(cut[0], "dp", 4, 2), swap(cut[1], "dp", 4, 1)


def gather_pieces(own):
    full = lax.all_gather(own, "dp", axis=0, tiled=True)
    rows, columns = full.shape
    blocks = full.reshape(4, rows // 4, columns)
    return blocks[0], blocks[1], blocks[2], blocks[3, :, : columns // 2], blocks[3, :, columns // 2 :]


def finish_kernel(core, mine_ref, other_ref, out_ref, qkv_ref):
    half = out_ref.shape[1] // 2
    for value, side in ((mine_ref[0], core[0]), (other_ref[...], 1 - core[0])):
        value = value.astype(f32)
        out_ref[:, pl.ds(pl.multiple_of(half * side, half), half)] = value[:, :half]
        for j in range(3):
            at = pl.ds(pl.multiple_of(2 * half * j + half * side, half), half)
            qkv_ref[:, at] = value[:, half * (j + 1) : half * (j + 2)]


def finish(core, total):
    rows, columns = total.shape[0] // 2, total.shape[1]
    halves = total.reshape(2, rows, columns)
    other = swap_core(pick(halves, 1 - core[0]))
    return launch(
        finish_kernel,
        "finish",
        (1,),
        (halves, other),
        [pl.BlockSpec((1, rows, columns), lambda i, c: (c[0], 0, 0)), whole(rows, columns)],
        (whole(rows, columns // 2), whole(rows, 3 * columns // 2)),
        (shape_of((rows, columns // 2), f32), shape_of((rows, 3 * columns // 2), f32)),
        scalars=(core,),
    )


def shards(
    n_dp,
    n_z,
    tokens,
    segment_ids,
    expert_ids,
    ln1_gain,
    ln1_bias,
    qkv_weight,
    query_bias,
    value_bias,
    out_weight,
    out_bias,
    ln2_gain,
    ln2_bias,
    up_weight,
    up_bias,
    down_weight,
    down_bias,
    cotangent,
):
    rows, width = tokens.shape
    devices = n_dp * n_z * 2
    share = qkv_weight.shape[0]
    up_share = up_bias.shape[1]
    core = lax.axis_index("c")
    scalar = lambda v: jnp.reshape(v, (1,)).astype(jnp.int32)
    square = n_dp == 4 and n_z == 4
    me = scalar(lax.axis_index("dp") if square else 0)

    half = width // 2
    both_w = jnp.concatenate([qkv_weight, out_weight], 1).reshape(share, 4, 2, half)
    mine_w, other_w = (pick(both_w, side, 2).reshape(share, 4 * half) for side in (core, 1 - core))
    attn_shard = place(scalar(core), [mine_w, swap_core(other_w)])
    small = jnp.concatenate(
        [ln1_gain, ln1_bias, query_bias, value_bias, out_bias, ln2_gain, ln2_bias, up_bias.reshape(-1), down_bias.reshape(-1)]
    )
    small = jnp.broadcast_to(small, (devices, small.shape[0]))
    small = lax.all_to_all(small, ALL, 0, 0, tiled=True).astype(f32)
    gain_one, shift_one, bias_query, bias_value, bias_out, gain_two, shift_two = (
        small[:, i * share : (i + 1) * share].reshape(1, width) for i in range(7)
    )
    bias_up = small[:, 7 * share : 7 * share + 2 * up_share].reshape(devices, 2, up_share)
    bias_up = pick(bias_up, core, 1).reshape(1, -1)
    bias_down = small[:, 7 * share + 2 * up_share :].reshape(devices, 2, share)
    bias_down = jnp.swapaxes(bias_down, 0, 1).reshape(2, width)

    qkv_bias = jnp.concatenate([bias_query, jnp.zeros_like(bias_query), bias_value], 1)

    def expert_shard(weight, after):
        mine, other = pick(weight, core, 1), swap_core(pick(weight, 1 - core, 1))
        return place(scalar(core), [mine, other], after)

    route = expert_ids[:, 0]
    at = lax.iota(jnp.int32, rows)
    before = (route[:, None] == route[None, :]) & (at[None, :] < at[:, None])
    slot = jnp.sum(before.astype(jnp.int32), 1) + jnp.where(route == core, 0, CAPACITY)
    slot_row, slot_col = slot.reshape(1, rows), slot.reshape(rows, 1)

    right_shard = expert_shard(down_weight[:, :, half:], (attn_shard,))
    up_shard = expert_shard(up_weight, (right_shard,))
    up_own = gather_z(up_shard)
    if square:
        right_all = place(me, [right_shard] + [swap(right_shard, "dp", 4, mask) for mask in range(1, 4)], (up_shard,))
        attn_own = later(gather_z(attn_shard), (right_all,))
    else:
        attn_own = gather_z(attn_shard)
    grad_keep, grad_away = dispatch(slot_row, cotangent, (attn_own,))
    grad_got = swap_core(grad_away)
    down_shard = expert_shard(down_weight[:, :, :half], (grad_keep,))
    if square:
        right = lax.all_gather(right_all.reshape(4, -1, half), "z", axis=0)
        attn_near = swap_near(attn_own, attn_own)
        mine_p = (attn_own, *attn_near, *gather_far(cut_halves(*attn_near, (down_shard,))))
        up_near = swap_near(up_own, up_own)
    else:
        right = lax.all_gather(gather_z(right_shard), "dp", axis=0, tiled=True)
        right = jnp.swapaxes(right.reshape(4, 4, -1, half), 0, 1)
        mine_p = gather_pieces(attn_own)
    other_p = tuple(swap_core(piece) for piece in mine_p)

    side = scalar(core)
    normed_one, qkv = project(side, me, tokens, gain_one, shift_one, qkv_bias, mine_p, other_p, (up_own, grad_got, bias_out, gain_two, shift_two))
    other_normed_one = swap_core(normed_one)
    seg_row, seg_col = segment_ids, segment_ids.reshape(rows, 1)
    attended, lse = attention(qkv, seg_col, seg_row)
    other_attended = swap_core(attended)
    if square:
        up_cut = cut_halves(*up_near, (attended,))
        w_up = (up_own, *up_near, *gather_far(up_cut))
    else:
        up_cut, w_up = (), gather_pieces(up_own)
    middle, in_keep, in_away = middle_part(
        side, me, slot_row, tokens, attended, mine_p, other_p, bias_out, gain_two, shift_two, after=(*up_cut, other_normed_one)
    )
    mine_w = place(me, mine_p, (middle,))
    other_w = place(me, other_p, (mine_w,))
    down_own = later(gather_z(down_shard), (middle,))
    in_got = swap_core(later(in_away, (*w_up[3:], down_own, other_w)))

    if square:
        down_near_got = swap_near(down_own, down_own)
    act, slope = up(me, in_keep, in_got, bias_up, w_up)
    if square:
        down_cut = cut_halves(*down_near_got, (act,))
        w_down = (down_own, *down_near_got, *gather_far(down_cut))
    else:
        down_cut, w_down = (), gather_pieces(down_own)
    down_partial, down_bias_grad = outer(act, grad_keep, grad_got, (*down_cut, right))
    down_half = lax.psum_scatter(later(down_partial, w_down[3:]), "dp", scatter_dimension=0, tiled=True)
    back_keep, back_away, up_partial, up_out_x, up_out_y, up_bias_grad = down_grad(
        me, grad_keep, grad_got, in_keep, in_got, slope, w_up, w_down, right, after=(other_w,)
    )
    back_got = swap_core(back_away)
    if square:
        up_partial = up_partial.reshape(4, width // 4, -1)
        up_far = swap_near(up_out_x, up_out_y)

    middle_grads, mine_projected, other_projected, attended_grad, gain_two_grad, shift_two_grad, out_bias_grad = (
        middle_grad(side, slot_col, back_keep, back_got, middle, cotangent, mine_w, other_w, gain_two)
    )
    other_projected = swap_core(other_projected)
    qkv_away = attention_grad(qkv, attended_grad, lse, seg_col, seg_row, 1 - core)
    qkv_got = swap_core(qkv_away)
    partial = two_sum(
        me, 4, attended, mine_projected[None], other_attended, other_projected[None], 0, after=(qkv_away,)
    )
    up_next = scatter_next(me, up_partial, *up_far, after=partial[:1]) if square else partial[:1]
    down_total = scatter_z(later(down_half, up_next))
    qkv_kept = attention_grad(qkv, attended_grad, lse, seg_col, seg_row, core, after=up_next)
    partial, out_x, out_y = two_sum(me, 4, normed_one, qkv_kept, other_normed_one, qkv_got, 1, into=partial)
    input_grad, gain_one_grad, shift_one_grad, bias_sums = input_grads(
        qkv_kept, qkv_away, tokens, middle_grads, mine_w, other_w, gain_one, after=(out_x,)
    )
    if square:
        partial = partial.reshape(4, width // 4, -1)
        far = swap_near(out_x, out_y)
        up_block = scatter_near(me, up_partial, *swap_near(*up_next), after=(input_grad, down_total))
        up_block = later(up_block, far)
        near = scatter_next(me, partial, *far, after=(up_block,))
        near_got = swap_near(*near)
    else:
        near = ()
        up_block = lax.psum_scatter(up_partial, "dp", scatter_dimension=0, tiled=True)
    up_total = scatter_z(up_block)
    down_weight_grad = pair(side, down_total)
    y_keep, y_away = down(me, act, w_down, right, after=(*near, down_weight_grad))
    y_got = swap_core(y_away)
    if square:
        last = scatter_near(me, partial, *near_got, after=(y_keep,))
    else:
        last = lax.psum_scatter(partial, "dp", scatter_dimension=0, tiled=True)
    block_out = output(slot_col, expert_ids, y_keep, y_got, middle, bias_down, after=(last,))
    query_bias_grad = by_core(core, bias_sums[0], bias_sums[1])
    value_bias_grad = by_core(core, bias_sums[2], bias_sums[3])

    vectors = [
        gain_one_grad,
        shift_one_grad,
        query_bias_grad.reshape(1, width),
        value_bias_grad.reshape(1, width),
        out_bias_grad,
        gain_two_grad,
        shift_two_grad,
        down_bias_grad,
    ]
    vectors = jnp.concatenate([v.reshape(1, width) for v in vectors], 0).reshape(8, devices, share)
    vectors = jnp.swapaxes(vectors, 0, 1).reshape(devices, 8 * share)
    sent = later(jnp.concatenate([vectors, up_bias_grad.reshape(devices, up_share)], 1), (last,))
    got = lax.all_to_all(sent, ALL, 0, 0, tiled=True).reshape(devices // 2, 2, -1)
    both = jnp.sum(got, 0)
    total = both[0] + both[1]
    sums = [total[i * share : (i + 1) * share] for i in range(7)]
    down_bias_sum = both[:, 7 * share : 8 * share]
    up_bias_sum = both[:, 8 * share :]

    up_weight_grad = pair(side, up_total)
    out_weight_grad, qkv_weight_grad = finish(side, later(scatter_z(last), (up_bias_sum, down_weight_grad, up_weight_grad, block_out)))
    return (
        block_out,
        input_grad,
        sums[0],
        sums[1],
        qkv_weight_grad,
        sums[2],
        sums[3],
        out_weight_grad,
        sums[4],
        sums[5],
        sums[6],
        up_weight_grad,
        up_bias_sum,
        down_weight_grad,
        down_bias_sum,
    )


def solution(mesh):
    n_dp, n_z = mesh.shape["dp"], mesh.shape["fsdp"] // 2
    split = Mesh(mesh.devices.reshape(n_dp, n_z, 2), ALL)
    row, flat, wide, cube = P(ALL, None), P(ALL), P(None, ALL), P(ALL, None, None)
    in_specs = (row, row, row, flat, flat, row, flat, flat, row, flat, flat, flat, cube, wide, cube, wide, row)
    out_specs = (row, row, flat, flat, row, flat, flat, row, flat, flat, flat, cube, wide, cube, wide)
    return jax.shard_map(
        functools.partial(shards, n_dp, n_z), mesh=split, in_specs=in_specs, out_specs=out_specs, check_vma=False
    )
```
